32 devices in a mesh: side: 4 (over y, core), batch: 8 (over z, x).
Axes of the slice: x: 2, y: 2, z: 4, core: 2. Of those that a mesh axis runs over, the one named last changes fastest.
Arguments:
- hidden_in: bfloat16 [4, 8, 1024, 512], P('side', 'batch'), may hold values from -6 to 6
- segments: int32 [4, 8, 1024], P('side', 'batch'), may hold values from -1 to 31, as said below
- query_cls: int32 [8, 32], P('batch'), may hold values from 0 to 930, as said below
- passage_cls: int32 [4, 8, 5], P('side', 'batch'), may hold values from 0 to 800, as said below
- pair_passage: int32 [256], P('batch'), may hold values from 0 to 119
- passage_cluster: int32 [120], replicated, may hold values from 0 to 31
- teacher: float32 [256, 120], P('batch'), may hold values from -6 to 6
- query_weight: bfloat16 [512, 512], replicated, may hold values from -0.25 to 0.25
- query_bias: float32 [512], replicated, may hold values from -3 to 3
- key_weight: bfloat16 [512, 512], replicated, may hold values from -0.25 to 0.25
- value_weight: bfloat16 [512, 512], replicated, may hold values from -0.25 to 0.25
- value_bias: float32 [512], replicated, may hold values from -1.75 to 1.75
- out_weight: bfloat16 [512, 512], replicated, may hold values from -1 to 1
- out_bias: float32 [512], replicated, may hold values from -1.75 to 1.75
- first_gain: float32 [512], replicated, may hold values from 0.5 to 1.5
- first_shift: float32 [512], replicated, may hold values from -1.75 to 1.75
- inner_weight: bfloat16 [512, 2048], replicated, may hold values from -0.25 to 0.25
- inner_bias: float32 [2048], replicated, may hold values from -3 to 3
- outer_weight: bfloat16 [2048, 512], replicated, may hold values from -0.125 to 0.125
- outer_bias: float32 [512], replicated, may hold values from -1.75 to 1.75
- second_gain: float32 [512], replicated, may hold values from 0.5 to 1.5
- second_shift: float32 [512], replicated, may hold values from -1.75 to 1.75
Outputs:
- loss: float32 [], replicated
- rows_out: bfloat16 [4, 8, 1024, 512], P('side', 'batch')
- input_grad: bfloat16 [4, 8, 1024, 512], P('side', 'batch')
- grad_query_weight: float32 [512, 512], replicated
- grad_query_bias: float32 [512], replicated
- grad_key_weight: float32 [512, 512], replicated
- grad_value_weight: float32 [512, 512], replicated
- grad_value_bias: float32 [512], replicated
- grad_out_weight: float32 [512, 512], replicated
- grad_out_bias: float32 [512], replicated
- grad_first_gain: float32 [512], replicated
- grad_first_shift: float32 [512], replicated
- grad_inner_weight: float32 [512, 2048], replicated
- grad_inner_bias: float32 [2048], replicated
- grad_outer_weight: float32 [2048, 512], replicated
- grad_outer_bias: float32 [512], replicated
- grad_second_gain: float32 [512], replicated
- grad_second_shift: float32 [512], replicated
The draws below stay inside these ranges and needn't reach their ends.
Inputs may be any that keep to these rules, and one draw needn't show every extreme that they name: `segments`: in every row segment numbers start at 0 and never fall; the tokens after the last segment carry -1. A row of the first group holds 32 queries of 8 to 30 tokens, one of exactly 30; a row of another group holds 5 passages of 50 to 200 tokens, one of exactly 200. `query_cls`: the first token of each segment of the first group's row, in order. `passage_cls`: the first token of each passage of the row, in order; in the first group it holds the first 5 query starts, which nothing uses.
All inputs are finite; a program needn't handle non-finite values.
Results may differ from the reference program's by a relative error of at most 0.02.
Values may be sent and summed in bfloat16 or wider, within the bound.
No kernel may reach another device: no remote copies, remote signals or barrier semaphores. Data moves between devices by JAX's collectives and lax.ppermute only.
A program may use at most 192 MiB of HBM per device.

```python
import math
import jax
import jax.numpy as jnp
import numpy as np
from jax import lax

D = 512
HEADS = 8
HD = 64
FF = 2048
TOK_DEV = 1024
QLEN = 30
QMIN = 8
CLUSTERS = 32
QSEG = 32
PSEG = 5
PMAX = 200
PMIN = 50
GROUPS = 4
ROWS = 8
NQ = 256
NPAS = 120


def layout_lengths(key):
    base = jax.random.fold_in(key, 11)
    key_query, key_qtop, key_pass, key_ptop, key_qfull, key_pfull = jax.random.split(base, 6)
    query_len = jax.random.randint(key_query, (ROWS, QSEG), QMIN, QLEN + 1, dtype=jnp.int32)
    query_top = jax.random.randint(key_qtop, (ROWS, 1), 0, QSEG, dtype=jnp.int32)
    query_len = jnp.where(jnp.arange(QSEG, dtype=jnp.int32)[None, :] == query_top, QLEN, query_len)
    query_full = jax.random.randint(key_qfull, (), 0, ROWS, dtype=jnp.int32)
    query_len = jnp.where(jnp.arange(ROWS, dtype=jnp.int32)[:, None] == query_full, QLEN, query_len)
    pass_len = jax.random.randint(key_pass, (GROUPS - 1, ROWS, PSEG), PMIN, PMAX + 1, dtype=jnp.int32)
    pass_top = jax.random.randint(key_ptop, (GROUPS - 1, ROWS, 1), 0, PSEG, dtype=jnp.int32)
    pass_len = jnp.where(jnp.arange(PSEG, dtype=jnp.int32)[None, None, :] == pass_top, PMAX, pass_len)
    pass_full = jax.random.randint(key_pfull, (), 0, (GROUPS - 1) * ROWS, dtype=jnp.int32)
    row_number = jnp.arange((GROUPS - 1) * ROWS, dtype=jnp.int32).reshape(GROUPS - 1, ROWS, 1)
    pass_len = jnp.where(row_number == pass_full, PMAX, pass_len)
    return (query_len.astype(jnp.int32), pass_len.astype(jnp.int32))


def start_points(lengths):
    return (jnp.cumsum(lengths, axis=-1) - lengths).astype(jnp.int32)


def segment_numbers(lengths):
    starts = start_points(lengths)
    positions = jnp.arange(TOK_DEV, dtype=jnp.int32)
    opened = jnp.sum((starts[..., None, :] <= positions[:, None]).astype(jnp.int32), axis=-1) - 1
    ending = jnp.sum(lengths, axis=-1, keepdims=True)
    return jnp.where(positions < ending, opened, -1).astype(jnp.int32)


def draw_segments(key, part):
    query_len, pass_len = layout_lengths(key)
    query_rows = segment_numbers(query_len)
    pass_rows = segment_numbers(pass_len)
    return jnp.concatenate([query_rows[None], pass_rows], axis=0).astype(jnp.int32)


def draw_query_cls(key, part):
    query_len, pass_len = layout_lengths(key)
    return start_points(query_len)


def draw_passage_cls(key, part):
    query_len, pass_len = layout_lengths(key)
    query_starts = start_points(query_len)[:, :PSEG]
    return jnp.concatenate([query_starts[None], start_points(pass_len)], axis=0).astype(jnp.int32)


def with_ends(array, rng, smallest, largest):
    shape = array.shape
    index_at = [jax.random.randint(jax.random.fold_in(rng, axis), (), 0, shape[axis]) for axis in range(len(shape))]
    array = array.at[tuple(index_at)].set(smallest)
    longest = shape.index(max(shape))
    index_at[longest] = (index_at[longest] + 1) % shape[longest]
    return array.at[tuple(index_at)].set(largest)


def shard_levels(rng, dims, pieces, low, largest):
    level = 1.0
    for axis_at, shards_of in pieces:
        heights = jax.random.uniform(jax.random.fold_in(jax.random.fold_in(rng, 6), axis_at), (shards_of,), jnp.float32, low / len(pieces), largest / len(pieces))
        level = level * jnp.repeat(jnp.exp(heights), dims[axis_at] // shards_of).reshape((-1,) + (1,) * (len(dims) - 1 - axis_at))
    return level


def rank_table(count, lean):
    loads = [(1 << 20) // math.isqrt(grade ** lean) + 1 for grade in range(1, count + 1)]
    spread = 1 + sum(loads) // (1 << 30)
    return np.cumsum(np.array([max(1, weight // spread) for weight in loads]))


def ranked(stream_key, extent, number_of, slope):
    listing = rank_table(number_of, slope)
    pick = jax.random.randint(jax.random.fold_in(stream_key, 1), extent, 0, int(listing[number_of - 1]))
    rank = jnp.searchsorted(jnp.asarray(listing, jnp.int32), pick, side="right")
    return jax.random.permutation(jax.random.fold_in(stream_key, 2), number_of)[rank].astype(jnp.int32)


def centred(stream_key, shape, width, bound, shards=(), kind=jnp.bfloat16):
    array = width * jax.random.normal(stream_key, shape, jnp.float32)
    if shards:
        array = array * shard_levels(stream_key, shape, shards, -0.22, 0.18)
    return jnp.clip(array, -bound, bound).astype(kind)


def setup_inputs(seed: int = 0) -> dict:
    key_list = jax.random.split(jax.random.key(seed), 23)
    hidden_in = centred(key_list[0], (GROUPS, ROWS, TOK_DEV, D), 1.0, 6.0, ((0, 4), (1, 8)))
    segments = draw_segments(jax.random.fold_in(key_list[22], 71), 0)
    query_cls = draw_query_cls(jax.random.fold_in(key_list[22], 71), 0)
    passage_cls = draw_passage_cls(jax.random.fold_in(key_list[22], 71), 0)
    pair_passage = with_ends(jax.random.randint(key_list[4], (NQ,), 0, NPAS), jax.random.fold_in(key_list[4], 1), 0, NPAS - 1).astype(jnp.int32)
    passage_cluster = with_ends(ranked(key_list[5], (NPAS,), CLUSTERS, 2), jax.random.fold_in(key_list[5], 3), 0, CLUSTERS - 1).astype(jnp.int32)
    teacher = centred(key_list[6], (NQ, NPAS), 1.0, 6.0, ((0, 8),), jnp.float32)
    query_weight = centred(key_list[7], (D, D), D ** -0.5, 0.25)
    query_bias = centred(key_list[8], (D,), 0.5, 3.0, (), jnp.float32)
    key_weight = centred(key_list[9], (D, D), D ** -0.5, 0.25)
    value_weight = centred(key_list[10], (D, D), D ** -0.5, 0.25)
    value_bias = centred(key_list[11], (D,), 0.3, 1.75, (), jnp.float32)
    out_weight = centred(key_list[12], (D, D), (D // 16) ** -0.5, 1.0)
    out_bias = centred(key_list[13], (D,), 0.3, 1.75, (), jnp.float32)
    first_gain = jnp.clip(1.0 + 0.1 * jax.random.normal(key_list[14], (D,), jnp.float32), 0.5, 1.5)
    first_shift = centred(key_list[15], (D,), 0.3, 1.75, (), jnp.float32)
    inner_weight = centred(key_list[16], (D, FF), D ** -0.5, 0.25)
    inner_bias = centred(key_list[17], (FF,), 0.5, 3.0, (), jnp.float32)
    outer_weight = centred(key_list[18], (FF, D), FF ** -0.5, 0.125)
    outer_bias = centred(key_list[19], (D,), 0.3, 1.75, (), jnp.float32)
    second_gain = jnp.clip(1.0 + 0.1 * jax.random.normal(key_list[20], (D,), jnp.float32), 0.5, 1.5)
    second_shift = centred(key_list[21], (D,), 0.3, 1.75, (), jnp.float32)
    return {"hidden_in": hidden_in, "segments": segments, "query_cls": query_cls, "passage_cls": passage_cls, "pair_passage": pair_passage, "passage_cluster": passage_cluster, "teacher": teacher, "query_weight": query_weight, "query_bias": query_bias, "key_weight": key_weight, "value_weight": value_weight, "value_bias": value_bias, "out_weight": out_weight, "out_bias": out_bias, "first_gain": first_gain, "first_shift": first_shift, "inner_weight": inner_weight, "inner_bias": inner_bias, "outer_weight": outer_weight, "outer_bias": outer_bias, "second_gain": second_gain, "second_shift": second_shift}


@jax.custom_vjp
def low(v):
    return lax.optimization_barrier(v.astype(jnp.bfloat16)).astype(jnp.float32)

@jax.custom_vjp
def low_back(v):
    return v

def low_keep(v):
    return (low(v), None)

def low_pass(kept, grad):
    return (grad,)

def back_keep(v):
    return (v, None)

def back_low(kept, grad):
    return (low(grad),)
low.defvjp(low_keep, low_pass)
low_back.defvjp(back_keep, back_low)
EPSILON = 1e-05
PRECISE = lax.Precision.HIGHEST

def norm_apply(summed, gain, shift):
    centre = lax.optimization_barrier(jnp.mean(summed, axis=-1, keepdims=True))
    deviation = summed - centre
    variance = lax.optimization_barrier(jnp.mean(deviation * deviation, axis=-1, keepdims=True))
    return deviation * lax.rsqrt(variance + EPSILON) * gain + shift

def reference(hidden_in, segments, query_cls, passage_cls, pair_passage, passage_cluster, teacher, query_weight, query_bias, key_weight, value_weight, value_bias, out_weight, out_bias, first_gain, first_shift, inner_weight, inner_bias, outer_weight, outer_bias, second_gain, second_shift):
    score_scale = HD ** (-0.5)
    cls_scale = D ** (-0.5)
    flat_rows = hidden_in.astype(jnp.float32).reshape(GROUPS * ROWS, TOK_DEV, D)
    flat_segs = segments.reshape(GROUPS * ROWS, TOK_DEV)
    query_index = query_cls.astype(jnp.int32)
    passage_index = passage_cls[1:].reshape((GROUPS - 1) * ROWS, PSEG).astype(jnp.int32)
    params = (query_weight.astype(jnp.float32), query_bias, key_weight.astype(jnp.float32), value_weight.astype(jnp.float32), value_bias, out_weight.astype(jnp.float32), out_bias, first_gain, first_shift, inner_weight.astype(jnp.float32), inner_bias, outer_weight.astype(jnp.float32), outer_bias, second_gain, second_shift)

    def forward(rows_f, w_query, b_query, w_key, w_value, b_value, w_out, b_out, gain_one, shift_one, w_inner, b_inner, w_outer, b_outer, gain_two, shift_two):

        def row_layer(item):
            row_x, row_seg = item
            queries = low(low_back(jnp.dot(row_x, w_query, precision=PRECISE)) + b_query)
            keys_all = low(low_back(jnp.dot(row_x, w_key, precision=PRECISE)))
            values_all = low(low_back(jnp.dot(row_x, w_value, precision=PRECISE)) + b_value)
            queries3 = queries.reshape(TOK_DEV, HEADS, HD)
            keys3 = keys_all.reshape(TOK_DEV, HEADS, HD)
            values3 = values_all.reshape(TOK_DEV, HEADS, HD)
            raw = jnp.einsum('qhd,khd->hqk', queries3, keys3, precision=PRECISE)
            scaled = low_back(raw * score_scale)
            same = row_seg[:, None] == row_seg[None, :]
            masked = jnp.where(same[None], scaled, -1e+30)
            probs = jax.nn.softmax(masked, axis=-1)
            context = jnp.einsum('hqk,khd->qhd', low(probs), values3, precision=PRECISE).reshape(TOK_DEV, D)
            context = low(low_back(context))
            attended = row_x + (low_back(jnp.dot(context, w_out, precision=PRECISE)) + b_out)
            first = norm_apply(attended, gain_one, shift_one)
            pre = low_back(jnp.dot(low(first), w_inner, precision=PRECISE)) + b_inner
            active = low(jax.nn.gelu(pre, approximate=False))
            second = first + (low_back(jnp.dot(active, w_outer, precision=PRECISE)) + b_outer)
            return norm_apply(second, gain_two, shift_two)
        finals = lax.map(jax.checkpoint(row_layer), (rows_f, flat_segs))
        qvec = jnp.take_along_axis(finals[:ROWS], query_index[:, :, None], axis=1).reshape(NQ, D)
        pvec = jnp.take_along_axis(finals[ROWS:], passage_index[:, :, None], axis=1).reshape(NPAS, D)
        qvec = low(qvec)
        pvec = low(pvec)
        score = low_back(jnp.dot(qvec, pvec.T, precision=PRECISE)) * cls_scale
        columns = jnp.arange(NPAS, dtype=jnp.int32)
        is_pair = pair_passage[:, None] == columns[None, :]
        query_cluster = lax.optimization_barrier(jnp.sum(jnp.where(is_pair, passage_cluster[None, :], 0), axis=1))
        counted = (passage_cluster[None, :] == query_cluster[:, None]) & jnp.logical_not(is_pair)
        pair_score = lax.optimization_barrier(jnp.sum(jnp.where(is_pair, score, 0.0), axis=1, keepdims=True))
        resid = jnp.where(counted, pair_score - score - teacher, 0.0)
        squares = jnp.sum(resid * resid)
        return (0.5 * squares, (finals, squares, jnp.sum(counted.astype(jnp.float32))))
    objective, pull, extra = jax.vjp(forward, flat_rows, *params, has_aux=True)
    finals, squares, pair_count = extra
    grads = pull(jnp.ones_like(objective))
    loss = squares / jnp.maximum(pair_count, 1.0)
    rows_out = finals.reshape(GROUPS, ROWS, TOK_DEV, D).astype(jnp.bfloat16)
    input_grad = grads[0].reshape(GROUPS, ROWS, TOK_DEV, D).astype(jnp.bfloat16)
    return (loss, rows_out, input_grad, grads[1], grads[2], grads[3], grads[4], grads[5], grads[6], grads[7], grads[8], grads[9], grads[10], grads[11], grads[12], grads[13], grads[14], grads[15])
```

```python
import jax
import jax.numpy as jnp
from jax import lax
from jax.sharding import PartitionSpec as P

HEADS = 8
HD = 64
EPSILON = 1e-05
NEG_FILL = -1e30
BF = jnp.bfloat16
F32 = jnp.float32
CORE_SWAP = [(0, 1), (1, 0), (2, 3), (3, 2)]
CHIP_SWAP = [(0, 2), (2, 0), (1, 3), (3, 1)]


def dot(left, right):
    return jnp.dot(left, right, preferred_element_type=F32)


def dot_t(left, right):
    return lax.dot_general(left, right, (((1,), (1,)), ((), ())), preferred_element_type=F32)


def t_dot(left, right):
    return lax.dot_general(left, right, (((0,), (0,)), ((), ())), preferred_element_type=F32)


def norm_stats(summed):
    centre = jnp.mean(summed, axis=1, keepdims=True)
    deviation = summed - centre
    inverse = lax.rsqrt(jnp.mean(deviation * deviation, axis=1, keepdims=True) + EPSILON)
    return deviation * inverse, inverse


def norm_back(upstream, normed, inverse, gain):
    scaled = upstream * gain
    inner = jnp.mean(scaled, axis=1, keepdims=True)
    cross = jnp.mean(scaled * normed, axis=1, keepdims=True)
    return inverse * (scaled - inner - normed * cross)


def gelu_parts(pre):
    phi = 0.5 * (1.0 + lax.erf(pre * (0.5**0.5)))
    density = jnp.exp(-0.5 * pre * pre) * 0.3989422804014327
    return pre * phi, phi + pre * density


def head_mask(rows, width):
    row_head = lax.broadcasted_iota(jnp.int32, (HEADS * rows, width), 0) // rows
    col_head = lax.broadcasted_iota(jnp.int32, (HEADS * rows, width), 1) // HD
    return row_head == col_head


def spread_heads(rows):
    tiled = jnp.tile(rows, (HEADS, 1))
    return jnp.where(head_mask(rows.shape[0], rows.shape[1]), tiled, jnp.zeros_like(tiled))


def fold_heads(wide, rows):
    masked = jnp.where(head_mask(rows, wide.shape[1]), wide, 0.0)
    return jnp.sum(masked.reshape(HEADS, rows, wide.shape[1]), axis=0)


def gather_rows(rows, n_query, n_pass, core, chip):
    batch_n = lax.axis_size("batch")
    block = n_query + 3 * n_pass
    block = block + block % 2
    pad = block - n_query - 3 * n_pass
    width = rows.shape[1]
    other = lax.ppermute(rows, "side", CORE_SWAP)
    low = jnp.where(core == 0, rows, other)
    high = jnp.where(core == 0, other, rows)
    n_first = n_query + n_pass
    first_chip = jnp.concatenate([low, high[:n_pass]], axis=0)
    second_chip = jnp.concatenate(
        [low[:n_pass], high[:n_pass], jnp.zeros((n_first - 2 * n_pass, width), rows.dtype)], axis=0
    )
    packed = jnp.where(chip == 0, first_chip, second_chip)
    far = lax.ppermute(packed, "side", CHIP_SWAP)
    head = jnp.where(chip == 0, packed, far)
    tail = jnp.where(chip == 0, far, packed)[: 2 * n_pass]
    full = jnp.concatenate([head, tail, jnp.zeros((pad, width), rows.dtype)], axis=0)
    half = jnp.where(core == 0, full[: block // 2], full[block // 2 :])
    sent = jnp.broadcast_to(half[None], (batch_n,) + half.shape)
    mine = lax.all_to_all(sent, "batch", split_axis=0, concat_axis=0)
    theirs = lax.ppermute(mine, "side", CORE_SWAP)
    left = jnp.where(core == 0, mine, theirs)
    right = jnp.where(core == 0, theirs, mine)
    return jnp.concatenate([left, right], axis=1).reshape(batch_n * block, width)


def sum_over_devices(key_part, value_part, core):
    batch_n = lax.axis_size("batch")
    keep = jnp.where(core == 0, key_part, value_part)
    give = jnp.where(core == 0, value_part, key_part).astype(BF)
    chip_sum = keep + lax.ppermute(give, "side", CORE_SWAP).astype(F32)
    peers = 2 * batch_n
    rows = chip_sum.shape[0] // peers
    groups = [[(y * 2 + c) * batch_n + b for y in range(2) for b in range(batch_n)] for c in range(2)]
    chunks = chip_sum.astype(BF).reshape(peers, rows, -1)
    parts = lax.all_to_all(
        chunks, ("side", "batch"), split_axis=0, concat_axis=0, axis_index_groups=groups
    )
    total = jnp.sum(parts.astype(F32), axis=0).astype(BF)
    sent = jnp.broadcast_to(total[None], (peers,) + total.shape)
    whole = lax.all_to_all(
        sent, ("side", "batch"), split_axis=0, concat_axis=0, axis_index_groups=groups
    ).reshape(chip_sum.shape)
    other = lax.ppermute(whole, "side", CORE_SWAP)
    return jnp.where(core == 0, whole, other).astype(F32), jnp.where(core == 0, other, whole).astype(F32)


def dense_context(queries, keys_low, values_low, seg_ids):
    count_tok = queries.shape[0]
    block_rows = min(512, count_tok)
    queries3 = queries.reshape(count_tok, HEADS, HD)
    keys3 = keys_low.reshape(count_tok, HEADS, HD)
    values3 = values_low.reshape(count_tok, HEADS, HD)
    contexts = []
    for first_row in range(0, count_tok, block_rows):
        raw = (
            jnp.einsum(
                "qhd,khd->hqk",
                queries3[first_row : first_row + block_rows],
                keys3,
                preferred_element_type=F32,
            )
            * HD ** (-0.5)
        )
        same = seg_ids[first_row : first_row + block_rows, None] == seg_ids[None, :]
        scores = jnp.where(same[None], raw, NEG_FILL)
        expo = jnp.exp(scores - jnp.max(scores, axis=2, keepdims=True))
        probs = expo / jnp.sum(expo, axis=2, keepdims=True)
        contexts.append(
            jnp.einsum("hqk,khd->qhd", probs.astype(BF), values3, preferred_element_type=F32)
        )
    return jnp.concatenate(contexts, axis=0).reshape(queries.shape).astype(BF)


def body(
    hidden_in,
    segments,
    query_cls,
    passage_cls,
    pair_passage,
    passage_cluster,
    teacher,
    query_weight,
    query_bias,
    key_weight,
    value_weight,
    value_bias,
    out_weight,
    out_bias,
    first_gain,
    first_shift,
    inner_weight,
    inner_bias,
    outer_weight,
    outer_bias,
    second_gain,
    second_shift,
):
    count_tok = hidden_in.shape[2]
    width = hidden_in.shape[3]
    n_query = query_cls.shape[1]
    n_pass = passage_cls.shape[2]
    batch_n = lax.axis_size("batch")
    side = lax.axis_index("side")
    batch = lax.axis_index("batch")
    core = side % 2
    chip = side // 2
    is_query = side == 0
    pass_count = teacher.shape[1]
    score_scale = HD ** (-0.5)
    cls_scale = width ** (-0.5)
    tokens = hidden_in.reshape(count_tok, width)
    seg_ids = segments.reshape(count_tok)

    keys_low = dot(tokens, key_weight).astype(BF)
    values_low = (dot(tokens, value_weight) + value_bias).astype(BF)
    own_count = jnp.where(is_query, n_query, n_pass)
    slots = jnp.arange(n_query, dtype=jnp.int32)
    cls = jnp.where(
        is_query,
        query_cls.reshape(-1),
        jnp.concatenate([passage_cls.reshape(-1), jnp.zeros((n_query - n_pass,), jnp.int32)]),
    )
    pick = (cls[:, None] == jnp.arange(count_tok, dtype=jnp.int32)[None, :]) & (
        slots[:, None] < own_count
    )
    pick_low = pick.astype(BF)
    cls_tokens = dot(pick_low, tokens).astype(BF)
    cls_seg = jnp.sum(jnp.where(pick, seg_ids[None, :], 0), axis=1)
    cls_query = (dot(cls_tokens, query_weight) + query_bias).astype(BF)
    query_wide = spread_heads(cls_query)
    same = jnp.tile(cls_seg, (HEADS,))[:, None] == seg_ids[None, :]
    scores = jnp.where(same, dot_t(query_wide, keys_low) * score_scale, NEG_FILL)
    expo = jnp.exp(scores - jnp.max(scores, axis=1, keepdims=True))
    probs = expo / jnp.sum(expo, axis=1, keepdims=True)
    probs_low = probs.astype(BF)
    cls_context = fold_heads(dot(probs_low, values_low), n_query).astype(BF)

    both = gather_rows(jnp.concatenate([cls_context, cls_tokens], axis=1), n_query, n_pass, core, chip)
    block = both.shape[0] // batch_n
    all_context = both[:, :width]
    all_tokens = both[:, width:]
    told = jnp.concatenate([teacher, pair_passage[:, None].astype(F32)], axis=1)
    told = lax.all_to_all(
        jnp.broadcast_to(told[None], (batch_n,) + told.shape), "batch", split_axis=0, concat_axis=0
    ).reshape(batch_n * n_query, pass_count + 1)
    teacher_all = told[:, :pass_count]
    pair_all = told[:, pass_count].astype(jnp.int32)

    attended = all_tokens.astype(F32) + (dot(all_context, out_weight) + out_bias)
    first_hat, first_inv = norm_stats(attended)
    first = first_hat * first_gain + first_shift
    first_low = first.astype(BF)
    pre = dot(first_low, inner_weight) + inner_bias
    active, slope = gelu_parts(pre)
    active_low = active.astype(BF)
    second = first + (dot(active_low, outer_weight) + outer_bias)
    second_hat, second_inv = norm_stats(second)
    final_low = (second_hat * second_gain + second_shift).astype(BF)

    blocks = final_low.reshape(batch_n, block, width)
    query_vec = blocks[:, :n_query].reshape(batch_n * n_query, width)
    pass_vec = (
        blocks[:, n_query : n_query + 3 * n_pass]
        .reshape(batch_n, 3, n_pass, width)
        .transpose(1, 0, 2, 3)
        .reshape(pass_count, width)
    )
    scores_cls = dot_t(query_vec, pass_vec) * cls_scale
    columns = jnp.arange(pass_count, dtype=jnp.int32)
    is_pair = pair_all[:, None] == columns[None, :]
    query_cluster = jnp.sum(jnp.where(is_pair, passage_cluster[None, :], 0), axis=1)
    counted = (passage_cluster[None, :] == query_cluster[:, None]) & jnp.logical_not(is_pair)
    pair_score = jnp.sum(jnp.where(is_pair, scores_cls, 0.0), axis=1, keepdims=True)
    resid = jnp.where(counted, pair_score - scores_cls - teacher_all, 0.0)
    loss = jnp.sum(resid * resid) / jnp.maximum(jnp.sum(counted.astype(F32)), 1.0)
    grad_score = jnp.where(is_pair, jnp.sum(resid, axis=1, keepdims=True), 0.0) - resid
    grad_score_low = (grad_score * cls_scale).astype(BF)
    grad_query_vec = dot(grad_score_low, pass_vec).reshape(batch_n, n_query, width)
    grad_pass_vec = (
        t_dot(grad_score_low, query_vec)
        .reshape(3, batch_n, n_pass, width)
        .transpose(1, 0, 2, 3)
        .reshape(batch_n, 3 * n_pass, width)
    )
    grad_final = jnp.concatenate(
        [
            grad_query_vec,
            grad_pass_vec,
            jnp.zeros((batch_n, block - n_query - 3 * n_pass, width), F32),
        ],
        axis=1,
    ).reshape(batch_n * block, width)

    grad_second = norm_back(grad_final, second_hat, second_inv, second_gain)
    second_low = grad_second.astype(BF)
    grad_pre = dot_t(second_low, outer_weight) * slope
    pre_low = grad_pre.astype(BF)
    grad_first = dot_t(pre_low, inner_weight) + grad_second
    grad_attended = norm_back(grad_first, first_hat, first_inv, first_gain)
    attended_low = grad_attended.astype(BF)
    grad_context = dot_t(attended_low, out_weight).astype(BF)

    start = batch * block + jnp.where(is_query, 0, n_query + n_pass * (side - 1))
    live = (slots < own_count)[:, None]

    def own(rows):
        padded = jnp.concatenate([rows, jnp.zeros((n_query, rows.shape[1]), rows.dtype)], axis=0)
        taken = lax.dynamic_slice_in_dim(padded, start, n_query, axis=0)
        return jnp.where(live, taken, jnp.zeros_like(taken))

    context_wide = spread_heads(own(grad_context))
    grad_probs = dot_t(context_wide, values_low)
    row_dot = jnp.sum(probs * grad_probs, axis=1, keepdims=True)
    grad_scores = (probs * (grad_probs - row_dot)).astype(BF)
    query_low = (fold_heads(dot(grad_scores, keys_low), n_query) * score_scale).astype(BF)
    key_low = (t_dot(grad_scores, query_wide) * score_scale).astype(BF)
    value_low = t_dot(probs_low, context_wide).astype(BF)
    grad_key_weight, grad_value_weight = sum_over_devices(
        t_dot(tokens, key_low), t_dot(tokens, value_low), core
    )
    all_query_low = gather_rows(query_low, n_query, n_pass, core, chip)

    grad_query_weight = t_dot(all_tokens, all_query_low)
    grad_query_bias = jnp.sum(all_query_low.astype(F32), axis=0)
    grad_value_bias = jnp.sum(grad_context.astype(F32), axis=0)
    grad_out_weight = t_dot(all_context, attended_low)
    grad_out_bias = jnp.sum(grad_attended, axis=0)
    grad_first_gain = jnp.sum(grad_first * first_hat, axis=0)
    grad_first_shift = jnp.sum(grad_first, axis=0)
    grad_inner_weight = t_dot(first_low, pre_low)
    grad_inner_bias = jnp.sum(grad_pre, axis=0)
    grad_outer_weight = t_dot(active_low, second_low)
    grad_outer_bias = jnp.sum(grad_second, axis=0)
    grad_second_gain = jnp.sum(grad_final * second_hat, axis=0)
    grad_second_shift = jnp.sum(grad_final, axis=0)

    sparse = own(grad_attended) + dot_t(query_low, query_weight)
    sparse_high = sparse.astype(BF)
    sparse_rest = (sparse - sparse_high.astype(F32)).astype(BF)
    input_grad = (
        dot_t(key_low, key_weight)
        + dot_t(value_low, value_weight)
        + t_dot(jnp.concatenate([pick_low, pick_low]), jnp.concatenate([sparse_high, sparse_rest]))
    ).astype(BF)

    queries = (dot(tokens, query_weight) + query_bias).astype(BF)
    context_low = dense_context(queries, keys_low, values_low, seg_ids)
    attended_d = tokens.astype(F32) + (dot(context_low, out_weight) + out_bias)
    first_d = norm_stats(attended_d)[0] * first_gain + first_shift
    pre_d = dot(first_d.astype(BF), inner_weight) + inner_bias
    active_d = (pre_d * 0.5 * (1.0 + lax.erf(pre_d * (0.5**0.5)))).astype(BF)
    second_d = first_d + (dot(active_d, outer_weight) + outer_bias)
    rows_out = (norm_stats(second_d)[0] * second_gain + second_shift).astype(BF)

    return (
        loss,
        rows_out.reshape(1, 1, count_tok, width),
        input_grad.reshape(1, 1, count_tok, width),
        grad_query_weight,
        grad_query_bias,
        grad_key_weight,
        grad_value_weight,
        grad_value_bias,
        grad_out_weight,
        grad_out_bias,
        grad_first_gain,
        grad_first_shift,
        grad_inner_weight,
        grad_inner_bias,
        grad_outer_weight,
        grad_outer_bias,
        grad_second_gain,
        grad_second_shift,
    )


def solution(mesh):
    rows = P("side", "batch", None, None)
    in_specs = (
        rows,
        P("side", "batch", None),
        P("batch", None),
        P("side", "batch", None),
        P("batch"),
        P(),
        P("batch", None),
    ) + (P(),) * 15
    out_specs = (P(), rows, rows) + (P(),) * 15
    return jax.shard_map(body, mesh=mesh, in_specs=in_specs, out_specs=out_specs, check_vma=False)
```

```python
import functools

import jax
import jax.numpy as jnp
import numpy as np
from jax import lax
from jax.experimental import pallas as pl
from jax.experimental.pallas import tpu as pltpu
from jax.sharding import PartitionSpec as P

HEADS = 8
HD = 64
EPSILON = 1e-05
NEG_FILL = -1e30
BF = jnp.bfloat16
F32 = jnp.float32
CORE_SWAP = [(0, 1), (1, 0), (2, 3), (3, 2)]
CHIP_SWAP = [(0, 2), (2, 0), (1, 3), (3, 1)]
MIB = 1 << 20
VM = pl.BlockSpec(memory_space=pltpu.VMEM)


def dot(left, right, precision=None):
    return jnp.dot(left, right, preferred_element_type=F32, precision=precision)


def dot_t(left, right):
    return lax.dot_general(left, right, (((1,), (1,)), ((), ())), preferred_element_type=F32)


def t_dot(left, right):
    return lax.dot_general(left, right, (((0,), (0,)), ((), ())), preferred_element_type=F32)


def iota(shape, axis):
    return lax.broadcasted_iota(jnp.int32, shape, axis)


def one_hot(rows, cols, row_of_col):
    return jnp.where(iota((rows, cols), 0) == row_of_col, 1.0, 0.0).astype(BF)


def norm_stats(summed):
    centre = jnp.mean(summed, axis=1, keepdims=True)
    deviation = summed - centre
    inverse = lax.rsqrt(jnp.mean(deviation * deviation, axis=1, keepdims=True) + EPSILON)
    return deviation * inverse, inverse


def norm_back(upstream, normed, inverse, gain):
    scaled = upstream * gain
    inner = jnp.mean(scaled, axis=1, keepdims=True)
    cross = jnp.mean(scaled * normed, axis=1, keepdims=True)
    return inverse * (scaled - inner - normed * cross)


def gelu(pre):
    return (0.5 * pre) * (1.0 + lax.erf(pre * (0.5**0.5)))


def gelu_parts(pre):
    phi = 0.5 + 0.5 * lax.erf(pre * (0.5**0.5))
    density = jnp.exp(-0.5 * (pre * pre)) * 0.3989422804014327
    return pre * phi, phi + pre * density


def spread_heads(rows):
    head = iota((1, rows.shape[1]), 1) // HD
    return jnp.concatenate(
        [jnp.where(head == h, rows, jnp.zeros_like(rows)) for h in range(HEADS)], axis=0
    )


def fold_heads(wide):
    count = wide.shape[0] // HEADS
    head = iota((1, wide.shape[1]), 1) // HD
    total = jnp.zeros((count, wide.shape[1]), wide.dtype)
    for h in range(HEADS):
        total = jnp.where(head == h, wide[h * count : (h + 1) * count], total)
    return total


class Fetched:
    def __init__(self, source, buffer, semaphores, axis=0, parts=1):
        self.buffer, self.shape = buffer, buffer.shape
        self.axis, self.size = axis, buffer.shape[axis] // parts
        self.waiting = {}
        for i in range(parts):
            at = self.place(i) if parts > 1 else (Ellipsis,)
            copy = pltpu.make_async_copy(source.at[at], buffer.at[at], semaphores.at[i])
            copy.start()
            self.waiting[i] = copy

    def place(self, i):
        return (slice(None),) * self.axis + (pl.ds(i * self.size, self.size),)

    def part(self, i):
        if i in self.waiting:
            self.waiting.pop(i).wait()
        return self.buffer[self.place(i)]

    def ref(self):
        for i in sorted(self.waiting):
            self.waiting.pop(i).wait()
        return self.buffer

    def __getitem__(self, index):
        return self.ref()[index]


class Result:
    def __init__(self, buffer, target, semaphores):
        self.buffer, self.target, self.semaphores = buffer, target, semaphores
        self.shape, self.dtype, self.copies = buffer.shape, buffer.dtype, []

    def __setitem__(self, index, value):
        self.buffer[index] = value

    def __getitem__(self, index):
        return self.buffer[index]

    def flush(self, first=None, size=None):
        source, target = self.buffer, self.target
        if first is not None:
            source, target = source.at[pl.ds(first, size)], target.at[pl.ds(first, size)]
        copy = pltpu.make_async_copy(source, target, self.semaphores.at[len(self.copies)])
        copy.start()
        self.copies.append(copy)


PARTS = 4
TOKEN = ((8, 128), F32, False)


def call(kernel, outs, ins, flops=0, scratch=(), limit=8, far=(), smem=(), split=None, after=(), name=None):
    n_in, n_out, n_after = len(ins), len(outs), len(after)
    split = split or {}
    far_in = list(smem) + [i for i in far if i not in smem]
    far_out = [i for i in range(n_out) if not outs[i][2]]
    shapes = [(pltpu.VMEM if near else pltpu.HBM)(s, d) for s, d, near in list(outs) + [TOKEN]]
    moved = sum(x.size * x.dtype.itemsize for x in ins)
    moved += sum(int(np.prod(s)) * jnp.dtype(d).itemsize for s, d, _ in outs)
    ins = [pltpu.with_memory_space_constraint(x, pltpu.HBM) if i in far_in else x for i, x in enumerate(ins)]
    after = [pltpu.with_memory_space_constraint(x, pltpu.HBM) for x in after]

    def wrapped(*refs):
        refs = list(refs)
        in_refs, refs = refs[:n_in], refs[n_in + n_after :]
        out_refs, refs = refs[:n_out], refs[n_out + 1 :]
        in_bufs, refs = refs[: len(far_in)], refs[len(far_in) :]
        out_bufs, refs = refs[: len(far_out)], refs[len(far_out) :]
        if far_in:
            semaphores, refs = refs[0], refs[1:]
            for k, i in enumerate(far_in):
                in_refs[i] = Fetched(in_refs[i], in_bufs[k], semaphores.at[k], *split.get(i, ()))
        if far_out:
            semaphores, refs = refs[0], refs[1:]
            for k, i in enumerate(far_out):
                out_refs[i] = Result(out_bufs[k], out_refs[i], semaphores.at[k])
        kernel(*in_refs, *out_refs, *refs)
        for i in far_in:
            in_refs[i].ref()
        for i in far_out:
            if not out_refs[i].copies:
                out_refs[i].flush()
        for i in far_out:
            for copy in out_refs[i].copies:
                copy.wait()

    hbm = pl.BlockSpec(memory_space=pltpu.HBM)
    spaces = [hbm if i in far_in else VM for i in range(n_in)] + [hbm] * n_after
    out_spaces = [hbm if i in far_out else VM for i in range(n_out)] + [hbm]
    buffers = [(pltpu.SMEM if i in smem else pltpu.VMEM)(ins[i].shape, ins[i].dtype) for i in far_in]
    buffers += [pltpu.VMEM(outs[i][0], outs[i][1]) for i in far_out]
    if far_in:
        buffers.append(pltpu.SemaphoreType.DMA((len(far_in), PARTS)))
    if far_out:
        buffers.append(pltpu.SemaphoreType.DMA((len(far_out), PARTS)))
    return pl.pallas_call(
        wrapped,
        out_shape=shapes,
        in_specs=spaces,
        out_specs=out_spaces,
        scratch_shapes=buffers + list(scratch),
        compiler_params=pltpu.CompilerParams(vmem_limit_bytes=limit * MIB),
        cost_estimate=pl.CostEstimate(
            flops=int(flops), bytes_accessed=int(moved), transcendentals=0
        ),
        name=name,
    )(*ins, *after)


def behind(value, *tokens):
    tokens = [pltpu.with_memory_space_constraint(x, pltpu.HBM) for x in tokens]
    return pl.pallas_call(
        lambda *refs: None,
        out_shape=pltpu.VMEM(value.shape, value.dtype),
        in_specs=[VM] + [pl.BlockSpec(memory_space=pltpu.HBM)] * len(tokens),
        out_specs=VM,
        input_output_aliases={0: 0},
        name="hand_on",
    )(value, *tokens)


class Rows:
    def __init__(self, batch_n, n_query, n_pass, pass_count):
        block = n_query + 3 * n_pass
        block += -block % 16
        self.batch_n, self.n_query, self.n_pass, self.block = batch_n, n_query, n_pass, block
        self.half = block // 2
        self.columns = pass_count + 1 + -(pass_count + 1) % 128
        self.count = batch_n * block
        self.quarter = block // 4
        self.slot = self.quarter + -self.quarter % 16
        core, batch, rest = np.meshgrid(
            np.arange(2), np.arange(batch_n), np.arange(self.half), indexing="ij"
        )
        place = (core * self.half + rest).reshape(-1)
        batch = batch.reshape(-1)
        self.code = (batch * block + place).astype(np.int32)
        y, peer, spot = np.meshgrid(
            np.arange(2), np.arange(batch_n), np.arange(self.slot), indexing="ij"
        )
        spot = np.where(spot < self.quarter, peer * self.half + y * self.quarter + spot, -1).reshape(-1)
        self.slots = np.concatenate([spot, np.where(spot < 0, -1, spot + batch_n * self.half)])
        self.slots = self.slots.astype(np.int32)
        self.query = np.where(place < n_query, batch * n_query + place, -1).astype(np.int32)
        group, slot = (place - n_query) // n_pass, (place - n_query) % n_pass
        is_pass = (place >= n_query) & (group < 3)
        self.passage = np.where(is_pass, (group * batch_n + batch) * n_pass + slot, -1).astype(np.int32)


def core_chip():
    side = lax.axis_index("side")
    return side % 2, side // 2


def block_source(rows, at):
    core, chip = core_chip()
    n, p = rows.n_query, rows.n_pass
    begin = lambda c, y: jnp.where(y == chip, 0, 2 * n) + jnp.where(c == core, 0, n)
    source = jnp.where(at < n + 3 * p, begin(1, 1) + at - (n + 2 * p), -1)
    source = jnp.where(at < n + 2 * p, begin(0, 1) + at - (n + p), source)
    source = jnp.where(at < n + p, begin(1, 0) + at - n, source)
    return jnp.where(at < n, begin(0, 0) + at, source)


def take_rows(source, parts):
    total = sum(p.shape[0] for p in parts)
    pick = jnp.where(iota((source.shape[0], total), 1) == source, 1.0, 0.0).astype(BF)
    return dot(pick, jnp.concatenate([p[...] for p in parts], axis=0)).astype(BF)


def half_kernel(rows, own_ref, other_ref, far_ref, far_other_ref, *refs):
    core, chip = core_chip()
    n = rows.n_query
    at = iota((rows.half, 1), 0) + core * rows.half
    half = take_rows(block_source(rows, at), (own_ref, other_ref, far_ref, far_other_ref))
    out_ref = refs[-1]
    if len(refs) == 1:
        out_ref[...] = half
        return
    teacher_ref, pair_ref = refs[:2]
    count, told = n // 2, teacher_ref.shape[1]
    mine = jnp.where(core == 0, teacher_ref[:count, :], teacher_ref[count:, :])
    line = iota((count, 1), 0)
    pair = jnp.zeros((count, 1), jnp.int32)
    for i in range(count):
        pair = jnp.where(line == i, pair_ref.ref()[core * count + i], pair)
    pair = jnp.broadcast_to(pair.astype(F32), (count, rows.columns - told))
    mine = jnp.concatenate([mine, pair], axis=1)
    high = mine.astype(BF)
    mid = (mine - high.astype(F32)).astype(BF)
    low = (mine - high.astype(F32) - mid.astype(F32)).astype(BF)
    terms = jnp.concatenate([high, mid, low], axis=1)
    side = out_ref.shape[2] // 2
    terms = jnp.concatenate([terms, jnp.zeros((count, side - terms.shape[1]), BF)], axis=1)
    terms = jnp.concatenate([terms[: count // 2], terms[count // 2 :]], axis=1)
    full = jnp.concatenate([half, terms], axis=0)
    for b in range(rows.batch_n):
        out_ref[b] = full


def near_rows(own, *tokens):
    other = lax.ppermute(own, "side", CORE_SWAP)
    far = lax.ppermute(own, "side", CHIP_SWAP)
    if tokens:
        far = behind(far, *tokens)
    return own, other, far, lax.ppermute(far, "side", CORE_SWAP)


def join_halves(core, mine, theirs):
    return jnp.concatenate(
        [jnp.where(core == 0, mine, theirs), jnp.where(core == 0, theirs, mine)], axis=0
    )


def cls_forward_kernel(
    n_pass, x_ref, seg_ref, query_cls_ref, pass_cls_ref, wq_ref, bq_ref, wk_ref, wv_ref, bv_ref,
    rows_ref, query_ref, pick_ref, key_ref, value_ref, probs_ref,
):
    side = lax.axis_index("side")
    n_query, width = query_ref.shape
    slot = iota((n_query, 1), 0)
    cls = jnp.full((n_query, 1), -1, jnp.int32)
    for i in range(n_query):
        place = jnp.where(side == 0, query_cls_ref.ref()[0, i], pass_cls_ref.ref()[0, 0, i] if i < n_pass else -1)
        cls = jnp.where(slot == i, place, cls)
    pick = iota((n_query, x_ref.shape[0]), 1) == cls
    pick_low = jnp.where(pick, 1.0, 0.0).astype(BF)
    pick_ref[...] = pick_low
    x = x_ref.ref()
    key_ref[...] = dot(x[...], wk_ref[...]).astype(BF)
    key_ref.flush()
    value_ref[...] = (dot(x[...], wv_ref[...]) + bv_ref[...]).astype(BF)
    value_ref.flush()
    seg = seg_ref[0].astype(F32)
    cls_seg = jnp.sum(jnp.where(pick, seg, 0.0), axis=1, keepdims=True)
    tokens = dot(pick_low, x[...]).astype(BF)
    query = (dot(tokens, wq_ref[...]) + bq_ref[...]).astype(BF)
    query_ref[...] = query
    bias = jnp.where(cls_seg == seg, 0.0, NEG_FILL)
    scores = dot_t(spread_heads(query) * BF(HD**-0.5), key_ref[...])
    scores = scores + jnp.concatenate([bias] * HEADS, axis=0)
    expo = jnp.exp(scores - jnp.max(scores, axis=1, keepdims=True))
    probs = expo / jnp.sum(expo, axis=1, keepdims=True)
    probs_ref[...] = probs
    probs_ref.flush()
    rows_ref[:, :width] = fold_heads(dot(probs.astype(BF), value_ref[...])).astype(BF)
    rows_ref[:, width:] = tokens


def middle_kernel(
    rows, pass_count,
    mine_ref, theirs_ref, wo_ref, bo_ref, g1_ref, s1_ref, wi_ref, bi_ref, wu_ref, bu_ref, g2_ref, s2_ref,
    at_ref, value_ref, probs_ref, x_ref, key_ref, query_ref, cluster_ref,
    keep_ref, give_ref, low_ref, context_ref, gown_ref, scores_ref,
    loss_ref, small_ref, inner_bias_ref,
    both_ref, first_ref, active_ref, pre_ref, second_ref, attended_ref, slope_ref, told_ref,
):
    width = wo_ref.shape[0]
    n_queries, n_columns = told_ref.shape
    chunk = wi_ref.size
    side, batch = lax.axis_index("side"), lax.axis_index("batch")
    core = side % 2
    code_at, query_at, pass_at = at_ref[0:1, :], at_ref[1:2, :], at_ref[2:3, :]
    count = rows.n_query // 2
    for half in range(2):
        for b in range(rows.batch_n):
            one = jnp.where(core == half, mine_ref[b], theirs_ref[b])
            first_row = (half * rows.batch_n + b) * rows.half
            both_ref[first_row : first_row + rows.half, :] = one[: rows.half]
            terms = one[rows.half :].astype(F32)
            for part in range(2):
                begin = part * one.shape[1] // 2
                cut = [terms[:, begin + k * n_columns : begin + (k + 1) * n_columns] for k in range(3)]
                row = b * rows.n_query + half * count + part * count // 2
                told_ref[row : row + count // 2, :] = cut[0] + cut[1] + cut[2]
    attended = both_ref[:, width:].astype(F32) + (dot(both_ref[:, :width], wo_ref[...]) + bo_ref[...])
    first_hat, first_inv = norm_stats(attended)
    first = first_hat * g1_ref[...] + s1_ref[...]
    first_low = first.astype(BF)
    first_ref[...] = first_low
    second = first + bu_ref[...]
    for i in range(PARTS):
        c = i * chunk
        pre = dot(first_low, wi_ref.part(i)) + bi_ref[:, c : c + chunk]
        active, slope = gelu_parts(pre)
        active = active.astype(BF)
        active_ref[:, c : c + chunk] = active
        slope_ref[:, c : c + chunk] = slope
        second += dot(active, wu_ref.part(i))
    both_ref.flush()
    first_ref.flush()
    active_ref.flush()
    second_hat, second_inv = norm_stats(second)
    final = (second_hat * g2_ref[...] + s2_ref[...]).astype(BF)

    scale = width ** (-0.5)
    query_pick = one_hot(n_queries, rows.count, query_at)
    pass_pick = one_hot(n_columns, rows.count, pass_at)
    query_vec = dot(query_pick, final).astype(BF)
    pass_vec = dot(pass_pick, final).astype(BF)
    score = dot_t(query_vec, pass_vec) * scale
    column = iota((n_queries, n_columns), 1)
    is_pair = column == told_ref[:, n_columns - 1 :].astype(jnp.int32)
    cluster = jnp.full((1, n_columns), -1.0, F32)
    for j in range(pass_count):
        cluster = jnp.where(column[:1] == j, cluster_ref.ref()[j].astype(F32), cluster)
    query_cluster = jnp.sum(jnp.where(is_pair, cluster, 0.0), axis=1, keepdims=True)
    counted = (cluster == query_cluster) & jnp.logical_not(is_pair) & (column < pass_count)
    pair_score = jnp.sum(jnp.where(is_pair, score, 0.0), axis=1, keepdims=True)
    resid = jnp.where(counted, pair_score - score - told_ref[...], 0.0)
    squares = jnp.sum(jnp.sum(resid * resid, axis=1, keepdims=True), axis=0, keepdims=True)
    pairs = jnp.where(counted, 1.0, 0.0)
    pairs = jnp.sum(jnp.sum(pairs, axis=1, keepdims=True), axis=0, keepdims=True)
    loss_ref[...] = squares / jnp.maximum(pairs, 1.0)
    grad_score = jnp.where(is_pair, jnp.sum(resid, axis=1, keepdims=True), 0.0) - resid
    grad_low = (grad_score * scale).astype(BF)
    grad_rows = dot(t_dot(query_pick, grad_low).astype(BF), pass_pick).astype(BF)
    grad_final = dot(grad_rows, final) + t_dot(grad_rows, final)

    def note(at, value):
        small_ref[at : at + 1, :] = jnp.sum(value, axis=0, keepdims=True)

    grad_second = norm_back(grad_final, second_hat, second_inv, g2_ref[...])
    second_low = grad_second.astype(BF)
    second_ref[...] = second_low
    grad_first = grad_second
    for i in range(PARTS):
        c = i * chunk
        grad_pre = dot_t(second_low, wu_ref.part(i)) * slope_ref[:, c : c + chunk]
        inner_bias_ref[:, c : c + chunk] = jnp.sum(grad_pre, axis=0, keepdims=True)
        pre_low = grad_pre.astype(BF)
        pre_ref[:, c : c + chunk] = pre_low
        grad_first += dot_t(pre_low, wi_ref.part(i))
    pre_ref.flush()
    second_ref.flush()
    grad_attended = norm_back(grad_first, first_hat, first_inv, g1_ref[...])
    attended_low = grad_attended.astype(BF)
    attended_ref[...] = attended_low
    attended_ref.flush()
    grad_context = dot_t(attended_low, wo_ref[...]).astype(BF)
    note(0, grad_final * second_hat)
    note(1, grad_final)
    note(2, grad_second)
    note(3, grad_first * first_hat)
    note(4, grad_first)
    note(5, grad_attended)
    note(6, grad_context.astype(F32))
    small_ref[7:8, :] = jnp.zeros((1, width), F32)


    slot = iota((rows.n_query, 1), 0)
    base = batch * rows.block + jnp.where(side == 0, 0, rows.n_query + rows.n_pass * (side - 1))
    live = slot < jnp.where(side == 0, rows.n_query, rows.n_pass)
    own = (code_at == base + slot) & live
    high = grad_attended.astype(BF)
    rest = (grad_attended - high.astype(F32)).astype(BF)
    own = jnp.where(own, 1.0, 0.0).astype(BF)
    gown_ref[...] = dot(own, high) + dot(own, rest)
    context = dot(own, grad_context).astype(BF)
    context_ref[...] = context
    wide = spread_heads(context)
    probs = probs_ref[...]
    grad_probs = dot_t(wide, value_ref[...])
    row_dot = jnp.sum(probs * grad_probs, axis=1, keepdims=True)
    grad_scores = (probs * (grad_probs - row_dot)).astype(BF)
    scores_ref[...] = grad_scores
    scores_ref.flush()
    query_wide = spread_heads(query_ref[...]) * BF(HD**-0.5)
    x = x_ref.ref()
    key_side = dot(grad_scores, x[...]).astype(BF)
    value_side = dot(probs.astype(BF), x[...]).astype(BF)
    key_part = t_dot(key_side, query_wide)
    value_part = t_dot(value_side, wide)
    keep_ref[...] = jnp.where(core == 0, key_part, value_part)
    give_ref[...] = jnp.where(core == 0, value_part, key_part).astype(BF)
    low_ref[...] = (fold_heads(dot(grad_scores, key_ref[...])) * HD**-0.5).astype(BF)


def input_grad_kernel(
    pick_ref, scores_ref, probs_ref, context_ref, query_ref, low_ref, gown_ref,
    wq_ref, wk_ref, wv_ref, out_ref,
):
    query_wide = spread_heads(query_ref[...]) * BF(HD**-0.5)
    key_low = t_dot(scores_ref[...], query_wide).astype(BF)
    value_low = t_dot(probs_ref[...].astype(BF), spread_heads(context_ref[...])).astype(BF)
    sparse = gown_ref[...] + dot_t(low_ref[...], wq_ref[...])
    high = sparse.astype(BF)
    rest = (sparse - high.astype(F32)).astype(BF)
    pick = pick_ref[...]
    total = dot_t(key_low, wk_ref[...]) + dot_t(value_low, wv_ref[...])
    total += t_dot(jnp.concatenate([pick, pick], axis=0), jnp.concatenate([high, rest], axis=0))
    out_ref[...] = total.astype(BF)


def chip_sum_kernel(keep_ref, got_ref, out_ref):
    out_ref[...] = (keep_ref[...] + got_ref[...].astype(F32)).astype(BF)


def add_parts_kernel(rows, parts_ref, own_ref, other_ref, far_ref, far_other_ref, out_ref):
    core, chip = core_chip()
    peers, size = parts_ref.shape[:2]
    total = parts_ref[0].astype(F32)
    for i in range(1, peers):
        total += parts_ref[i].astype(F32)
    at = iota((rows.slot, 1), 0)
    source = block_source(rows, core * rows.half + chip * rows.quarter + at)
    source = jnp.where(at < rows.quarter, source, -1)
    low = take_rows(source, (own_ref, other_ref, far_ref, far_other_ref))
    total = jnp.concatenate([total.astype(BF), low], axis=0)
    for i in range(peers):
        out_ref[i] = total


def last_kernel(size, mine_ref, theirs_ref, x_ref, key_ref, value_ref, query_ref, bias_ref):
    core, _ = core_chip()
    peers = mine_ref.shape[0]
    step = peers // PARTS
    for i in range(PARTS):
        for j in range(i * step, i * step + step):
            mine, theirs = mine_ref[j, :size].astype(F32), theirs_ref[j, :size].astype(F32)
            key_ref[j * size : j * size + size, :] = jnp.where(core == 0, mine, theirs)
            value_ref[j * size : j * size + size, :] = jnp.where(core == 0, theirs, mine)
        key_ref.flush(i * step * size, step * size)
        value_ref.flush(i * step * size, step * size)
    mine = jnp.concatenate([mine_ref[j, size:] for j in range(peers)], axis=0)
    theirs = jnp.concatenate([theirs_ref[j, size:] for j in range(peers)], axis=0)
    low = join_halves(core, mine, theirs)
    bias_ref[...] = jnp.sum(low.astype(F32), axis=0, keepdims=True)
    part_rows(query_ref, x_ref, low)


def core_groups(batch_n):
    return [[(y * 2 + c) * batch_n + b for y in range(2) for b in range(batch_n)] for c in range(2)]


def exchange(sent, batch_n):
    return lax.all_to_all(
        sent, ("side", "batch"), split_axis=0, concat_axis=0, axis_index_groups=core_groups(batch_n)
    )


def scatter_sum(keep, give, batch_n):
    got = lax.ppermute(give, "side", CORE_SWAP)
    total, token = call(chip_sum_kernel, [(keep.shape, BF, True)], (keep, got), name="chip_sum")
    return exchange(total.reshape(2 * batch_n, keep.shape[0] // (2 * batch_n), keep.shape[1]), batch_n), token


def part_rows(result, left, right):
    size = result.shape[0] // PARTS
    for i in range(PARTS):
        result[i * size : i * size + size, :] = t_dot(left[:, i * size : i * size + size], right)
        result.flush(i * size, size)


def weight_grads_kernel(
    active_ref, second_ref, first_ref, pre_ref, both_ref, attended_ref, slots_ref,
    outer_ref, inner_ref, out_ref, x_ref,
):
    part_rows(outer_ref, active_ref, second_ref[...])
    part_rows(inner_ref, first_ref, pre_ref[...])
    part_rows(out_ref, both_ref, attended_ref[...])
    width = out_ref.shape[0]
    count = both_ref.shape[0]
    pick = one_hot(count, slots_ref.shape[1], slots_ref[...])
    x_ref[...] = t_dot(pick, both_ref[:, width:]).astype(BF)


def column_of(row):
    return jnp.transpose(jnp.broadcast_to(row, (128, row.shape[1])))[:, :1]


def attention_kernel(
    tile, sizes, x_ref, wq_ref, bq_ref, key_ref, value_ref, seg_ref, out_ref, q_scr, bias_scr
):
    count = x_ref.shape[0]
    x, wq, bq, seg = x_ref.ref(), wq_ref.ref(), bq_ref[...], seg_ref[0]
    places = iota((1, count), 1)
    keys, values = key_ref.ref(), value_ref.ref()

    @pl.loop(0, count // tile)
    def _(i):
        row = pl.multiple_of(i * tile, tile)
        q = (dot(x[pl.ds(row, tile), :], wq[...]) + bq).astype(BF)
        q_scr[...] = q * BF(HD**-0.5)
        first = jnp.max(jnp.where(places == row, seg, -2))
        last = jnp.max(jnp.where(places == row + (tile - 1), seg, -2))
        low = jnp.min(jnp.where(seg == first, places, count)) // 128 * 128
        high = jnp.max(jnp.where(seg == last, places, -1)) + 1
        own = seg_ref.ref()[0, :, pl.ds(row, tile)].astype(F32)
        own = column_of(own)
        before = jnp.int32(0)
        for size in sizes:
            start = jnp.minimum(low, count - size)
            fits = (high - start <= size) if size < count else jnp.bool_(True)

            @pl.when(jnp.logical_and(before == 0, fits))
            def _(size=size, start=start):
                at = pl.multiple_of(start, 128)
                near = seg_ref.ref()[0, :, pl.ds(at, size)].astype(F32)
                bias_scr[:, :size] = jnp.where(own == near, 0.0, NEG_FILL)
                half = iota((1, 2 * HD), 1) // HD
                slabs = [slice(h // 2 * 2 * HD, h // 2 * 2 * HD + 2 * HD) for h in range(HEADS)]
                scores = [
                    dot_t(
                        jnp.where(half == h % 2, q_scr[:, slabs[h]], BF(0)),
                        keys[pl.ds(at, size), slabs[h]],
                    )
                    + bias_scr[:, :size]
                    for h in range(HEADS)
                ]
                expos = [jnp.exp(s - jnp.max(s, axis=1, keepdims=True)).astype(BF) for s in scores]
                outs = []
                for h in range(HEADS):
                    ones = jnp.where(half == h % 2, values[pl.ds(at, size), slabs[h]], BF(1))
                    mixed = dot(expos[h], ones)
                    outs.append(mixed / pltpu.roll(mixed, HD, 1))
                for h in range(0, HEADS, 2):
                    out_ref.buffer[pl.ds(row, tile), slabs[h]] = jnp.where(
                        half == 0, outs[h], outs[h + 1]
                    ).astype(BF)

            before = jnp.where(fits, 1, before)


def attention(x, wq, bq, keys, values, seg, after, tile=256):
    t, d = x.shape
    sizes = [s for s in (384, 512, 768) if s < t] + [t]
    return call(
        functools.partial(attention_kernel, tile, sizes),
        [((t, d), BF, False)],
        (x, wq, bq, keys, values, seg),
        flops=8 * 10**9,
        far=range(6),
        limit=20,
        scratch=[pltpu.VMEM((tile, d), BF), pltpu.VMEM((tile, t), F32)],
        after=after,
        name="attention",
    )


def ffn_kernel(
    tile, x_ref, c_ref, wo_ref, bo_ref, g1_ref, s1_ref, wi_ref, bi_ref, wu_ref, bu_ref, g2_ref,
    s2_ref, out_ref,
):
    chunk = wi_ref.size
    for t in range(0, x_ref.shape[0], tile):
        part = slice(t, t + tile)
        attended = x_ref[part, :].astype(F32) + (dot(c_ref[part, :], wo_ref[...]) + bo_ref[...])
        first = norm_stats(attended)[0] * g1_ref[...] + s1_ref[...]
        first_low = first.astype(BF)
        second = first + bu_ref[...]
        for c in range(PARTS):
            pre = dot(first_low, wi_ref.part(c)) + bi_ref[:, c * chunk : c * chunk + chunk]
            second += dot(gelu(pre).astype(BF), wu_ref.part(c))
        out_ref[part, :] = (norm_stats(second)[0] * g2_ref[...] + s2_ref[...]).astype(BF)
        out_ref.flush(t, tile)


def ffn(x, context, weights, after, tile=512):
    return call(
        functools.partial(ffn_kernel, tile),
        [(x.shape, BF, False)],
        (x, context) + weights,
        flops=6 * 10**9,
        far=range(12),
        limit=20,
        split={6: (1, PARTS), 8: (0, PARTS)},
        after=after,
        name="feed_forward",
    )


def middle_large(
    rows, pass_count, core, mine, theirs, told, cluster, wo, bo, g1, s1, wi, bi, wu, bu, g2, s2
):
    width = wo.shape[0]
    both = join_halves(core, mine, theirs)
    attended = both[:, width:].astype(F32) + (dot(both[:, :width], wo) + bo)
    first_hat, first_inv = norm_stats(attended)
    first = first_hat * g1 + s1
    first_low = first.astype(BF)
    active, slope = gelu_parts(dot(first_low, wi) + bi)
    active_low = active.astype(BF)
    second = first + (dot(active_low, wu) + bu)
    second_hat, second_inv = norm_stats(second)
    final = (second_hat * g2 + s2).astype(BF)
    order_q = np.argsort(rows.query, kind="stable")[-rows.batch_n * rows.n_query :]
    order_p = np.argsort(rows.passage, kind="stable")[-pass_count:]
    query_vec, pass_vec = final[order_q], final[order_p]
    scale = width ** (-0.5)
    score = dot_t(query_vec, pass_vec) * scale
    is_pair = iota(score.shape, 1) == told[:, pass_count:].astype(jnp.int32)
    query_cluster = jnp.sum(jnp.where(is_pair, cluster, 0.0), axis=1, keepdims=True)
    counted = (cluster == query_cluster) & jnp.logical_not(is_pair)
    pair_score = jnp.sum(jnp.where(is_pair, score, 0.0), axis=1, keepdims=True)
    resid = jnp.where(counted, pair_score - score - told[:, :pass_count], 0.0)
    loss = jnp.sum(resid * resid) / jnp.maximum(jnp.sum(counted.astype(F32)), 1.0)
    grad_score = jnp.where(is_pair, jnp.sum(resid, axis=1, keepdims=True), 0.0) - resid
    grad_low = (grad_score * scale).astype(BF)
    grad_final = jnp.zeros((rows.count, width), F32)
    grad_final = grad_final.at[order_q].set(dot(grad_low, pass_vec))
    grad_final = grad_final.at[order_p].set(t_dot(grad_low, query_vec))
    grad_second = norm_back(grad_final, second_hat, second_inv, g2)
    second_low = grad_second.astype(BF)
    grad_pre = dot_t(second_low, wu) * slope
    pre_low = grad_pre.astype(BF)
    grad_first = dot_t(pre_low, wi) + grad_second
    grad_attended = norm_back(grad_first, first_hat, first_inv, g1)
    attended_low = grad_attended.astype(BF)
    grad_context = dot_t(attended_low, wo).astype(BF)
    small = jnp.stack(
        [
            jnp.sum(v, axis=0)
            for v in (
                grad_final * second_hat, grad_final, grad_second, grad_first * first_hat,
                grad_first, grad_attended, grad_context.astype(F32),
            )
        ]
    )
    inner_bias = jnp.sum(grad_pre, axis=0, keepdims=True)
    return (
        loss.reshape(1, 1), grad_attended, grad_context, small, inner_bias,
        both, first_low, active_low, pre_low, second_low, attended_low,
    )


def own_large(rows, side, batch, grad_attended, grad_context, tokens, keys, values, cls_query, probs):
    core = side % 2
    slot = jnp.arange(rows.n_query)[:, None]
    base = batch * rows.block + jnp.where(side == 0, 0, rows.n_query + rows.n_pass * (side - 1))
    live = slot < jnp.where(side == 0, rows.n_query, rows.n_pass)
    own = ((rows.code[None, :] == base + slot) & live).astype(F32)
    own_attended = dot(own, grad_attended, lax.Precision.HIGHEST)
    context = dot(own.astype(BF), grad_context).astype(BF)
    wide = spread_heads(context)
    grad_probs = dot_t(wide, values)
    row_dot = jnp.sum(probs * grad_probs, axis=1, keepdims=True)
    grad_scores = (probs * (grad_probs - row_dot)).astype(BF)
    query_wide = spread_heads(cls_query) * BF(HD**-0.5)
    key_part = t_dot(dot(grad_scores, tokens).astype(BF), query_wide)
    value_part = t_dot(dot(probs.astype(BF), tokens).astype(BF), wide)
    keep = jnp.where(core == 0, key_part, value_part)
    give = jnp.where(core == 0, value_part, key_part).astype(BF)
    low = (fold_heads(dot(grad_scores, keys)) * HD**-0.5).astype(BF)
    return keep, give, low, context, own_attended, grad_scores


def middle(rows, pass_count, mine, theirs, kept, weights, cluster, hidden, after):
    width, ff = weights[4].shape
    count = rows.count
    keys, values, cls_query, probs = kept
    at = np.stack([rows.code, rows.query, rows.passage])
    ins = (mine, theirs) + weights + (at, values, probs, hidden, keys, cls_query, cluster)
    outs = [
        ((width, width), F32, True), ((width, width), BF, True), ((rows.n_query, width), BF, True),
        ((rows.n_query, width), BF, False), ((rows.n_query, width), F32, False), (probs.shape, BF, False),
        ((1, 1), F32, False), ((8, width), F32, False), ((1, ff), F32, False),
        ((count, 2 * width), BF, False), ((count, width), BF, False), ((count, ff), BF, False),
        ((count, ff), BF, False), ((count, width), BF, False), ((count, width), BF, False),
    ]
    return call(
        functools.partial(middle_kernel, rows, pass_count),
        outs,
        ins,
        flops=12 * count * width * ff,
        scratch=[
            pltpu.VMEM((count, ff), F32),
            pltpu.VMEM((rows.batch_n * rows.n_query, rows.columns), F32),
        ],
        far=range(2, len(ins)),
        split={6: (1, PARTS), 8: (0, PARTS)},
        smem=(len(ins) - 1,),
        limit=40,
        after=after,
        name="cls_middle",
    )


def body(
    hidden_in,
    segments,
    query_cls,
    passage_cls,
    pair_passage,
    passage_cluster,
    teacher,
    query_weight,
    query_bias,
    key_weight,
    value_weight,
    value_bias,
    out_weight,
    out_bias,
    first_gain,
    first_shift,
    inner_weight,
    inner_bias,
    outer_weight,
    outer_bias,
    second_gain,
    second_shift,
):
    count_tok = hidden_in.shape[2]
    width = hidden_in.shape[3]
    n_query = query_cls.shape[1]
    n_pass = passage_cls.shape[2]
    batch_n = lax.axis_size("batch")
    side = lax.axis_index("side")
    pass_count = teacher.shape[1]
    rows = Rows(batch_n, n_query, n_pass, pass_count)

    hidden = hidden_in.reshape(count_tok, width)

    def vec(v):
        return v.reshape(1, -1)

    weights = (
        out_weight, vec(out_bias), vec(first_gain), vec(first_shift), inner_weight, vec(inner_bias),
        outer_weight, vec(outer_bias), vec(second_gain), vec(second_shift),
    )
    small_case = rows.count <= 512 and 3 * rows.columns <= width and n_query % 32 == 0

    token = ((count_tok, width), BF, False)
    own, cls_query, pick, keys, values, probs, _ = call(
        functools.partial(cls_forward_kernel, n_pass),
        [
            ((n_query, 2 * width), BF, True),
            ((n_query, width), BF, False),
            ((n_query, count_tok), BF, False),
            token,
            token,
            ((HEADS * n_query, count_tok), F32, False),
        ],
        (
            hidden, segments, query_cls, passage_cls, query_weight, vec(query_bias), key_weight,
            value_weight, vec(value_bias),
        ),
        flops=4 * count_tok * width * width,
        far=(0, 6, 1, 4, 5, 7, 8),
        smem=(2, 3),
        limit=20,
        name="cls_forward",
    )

    extra = n_query // 4 if small_case else 0
    near = near_rows(own)
    if small_case:
        sent, half_done = call(
            functools.partial(half_kernel, rows),
            [((batch_n, rows.half + extra, 2 * width), BF, True)],
            near + (teacher, pair_passage),
            far=(4,),
            smem=(5,),
            name="half_rows",
        )
    else:
        half, half_done = call(
            functools.partial(half_kernel, rows),
            [((rows.half, 2 * width), BF, True)],
            near,
            name="half_rows",
        )
        sent = jnp.broadcast_to(half[None], (batch_n,) + half.shape)
    mine = lax.all_to_all(sent, "batch", split_axis=0, concat_axis=0)
    context, attention_done = attention(
        hidden, query_weight, vec(query_bias), keys, values, segments, (half_done,)
    )
    if small_case:
        mine = behind(mine, attention_done)
    theirs = lax.ppermute(mine, "side", CORE_SWAP)

    if small_case:
        kept = (keys, values, cls_query, probs)
        (
            keep, give, query_low, own_context, own_attended, grad_scores, loss, small, grad_inner_bias,
            both, first_low, active_low, pre_low, second_low, attended_low, _,
        ) = middle(
            rows, pass_count, mine, theirs, kept, weights, passage_cluster, hidden, (attention_done,)
        )
    else:
        told = jnp.concatenate([teacher, pair_passage[:, None].astype(F32)], axis=1)
        told = lax.all_to_all(
            jnp.broadcast_to(told[None], (batch_n,) + told.shape), "batch", split_axis=0, concat_axis=0
        ).reshape(batch_n * n_query, pass_count + 1)
        flat = (batch_n * rows.half, 2 * width)
        (
            loss, grad_attended, grad_context, small, grad_inner_bias,
            both, first_low, active_low, pre_low, second_low, attended_low,
        ) = middle_large(
            rows, pass_count, side % 2, mine.reshape(flat), theirs.reshape(flat), told,
            passage_cluster.astype(F32)[None, :], *weights,
        )
        keep, give, query_low, own_context, own_attended, grad_scores = own_large(
            rows, side, lax.axis_index("batch"), grad_attended, grad_context,
            hidden, keys, values, cls_query, probs,
        )

    parts, sum_done = scatter_sum(keep, give, batch_n)
    input_grad, input_done = call(
        input_grad_kernel,
        [(hidden.shape, BF, False)],
        (
            pick, grad_scores, probs, own_context, cls_query, query_low, own_attended, query_weight,
            key_weight, value_weight,
        ),
        flops=6 * count_tok * width * width,
        far=(1, 4, 2, 3, 0, 6, 8, 9, 7),
        limit=20,
        after=(sum_done,),
        name="input_grad",
    )
    peers, size = parts.shape[:2]
    if small_case and size % 16 == 0:
        saved = (active_low, second_low, first_low, pre_low, both, attended_low, rows.slots[None, :])
        grad_outer_weight, grad_inner_weight, grad_out_weight, all_tokens, weight_done = call(
            weight_grads_kernel,
            [
                (outer_weight.shape, F32, False),
                (inner_weight.shape, F32, False),
                (out_weight.shape, F32, False),
                ((rows.slots.shape[0], width), BF, False),
            ],
            saved,
            flops=2 * rows.count * width * (4 * width + width),
            far=range(7),
            limit=32,
            after=(sum_done,),
            name="weight_grads",
        )
        low = near_rows(query_low, weight_done)
        sent, add_done = call(
            functools.partial(add_parts_kernel, rows),
            [((peers, size + rows.slot, width), BF, True)],
            (parts,) + low,
            after=(input_done, weight_done),
            name="add_parts",
        )
        whole = exchange(sent, batch_n)
        rows_out, ffn_done = ffn(hidden, context, weights, (add_done,))
        whole = behind(whole, ffn_done)
        other = lax.ppermute(whole, "side", CORE_SWAP)
        grad_key_weight, grad_value_weight, grad_query_weight, grad_query_bias, _ = call(
            functools.partial(last_kernel, size),
            [((width, width), F32, False)] * 3 + [((1, width), F32, False)],
            (whole, other, all_tokens),
            far=(2,),
            limit=12,
            name="last_grads",
        )
    else:
        rows_out, _ = ffn(hidden, context, weights, (sum_done,))
        part = jnp.sum(parts.astype(F32), axis=0).astype(BF)
        whole = exchange(jnp.broadcast_to(part[None], parts.shape), batch_n).reshape(width, width)
        grad_outer_weight = t_dot(active_low, second_low)
        grad_inner_weight = t_dot(first_low, pre_low)
        grad_out_weight = t_dot(both[:, :width], attended_low)
        half, _ = call(
            functools.partial(half_kernel, rows),
            [((rows.half, width), BF, True)],
            near_rows(query_low),
            name="low_rows",
        )
        flat = (batch_n * rows.half, width)
        half = jnp.broadcast_to(half[None], (batch_n,) + half.shape)
        low_mine = lax.all_to_all(half, "batch", split_axis=0, concat_axis=0).reshape(flat)
        low_theirs = lax.ppermute(low_mine, "side", CORE_SWAP)
        all_low = join_halves(side % 2, low_mine, low_theirs)
        grad_query_weight = t_dot(both[:, width:], all_low)
        grad_query_bias = jnp.sum(all_low.astype(F32), axis=0)
        other = lax.ppermute(whole, "side", CORE_SWAP)
        first_core = side % 2 == 0
        grad_key_weight = jnp.where(first_core, whole, other).astype(F32)
        grad_value_weight = jnp.where(first_core, other, whole).astype(F32)

    return (
        loss.reshape(()),
        rows_out.reshape(hidden_in.shape),
        input_grad.reshape(hidden_in.shape),
        grad_query_weight,
        grad_query_bias.reshape(-1),
        grad_key_weight,
        grad_value_weight,
        small[6],
        grad_out_weight,
        small[5],
        small[3],
        small[4],
        grad_inner_weight,
        grad_inner_bias.reshape(-1),
        grad_outer_weight,
        small[2],
        small[0],
        small[1],
    )


def solution(mesh):
    rows = P("side", "batch", None, None)
    in_specs = (
        rows,
        P("side", "batch", None),
        P("batch", None),
        P("side", "batch", None),
        P("batch"),
        P(),
        P("batch", None),
    ) + (P(),) * 15
    out_specs = (P(), rows, rows) + (P(),) * 15
    return jax.shard_map(body, mesh=mesh, in_specs=in_specs, out_specs=out_specs, check_vma=False)
```

```python
import functools

import jax
import jax.numpy as jnp
import numpy as np
from jax import lax
from jax.experimental import pallas as pl
from jax.experimental.pallas import tpu as pltpu
from jax.sharding import PartitionSpec as P

HEADS = 8
HD = 64
EPSILON = 1e-05
NEG_FILL = -1e30
BF = jnp.bfloat16
F32 = jnp.float32
CORE_SWAP = [(0, 1), (1, 0), (2, 3), (3, 2)]
CHIP_SWAP = [(0, 2), (2, 0), (1, 3), (3, 1)]
MIB = 1 << 20
VM = pl.BlockSpec(memory_space=pltpu.VMEM)


def dot(left, right, precision=None):
    return jnp.dot(left, right, preferred_element_type=F32, precision=precision)


def dot_t(left, right):
    return lax.dot_general(left, right, (((1,), (1,)), ((), ())), preferred_element_type=F32)


def t_dot(left, right):
    return lax.dot_general(left, right, (((0,), (0,)), ((), ())), preferred_element_type=F32)


def iota(shape, axis):
    return lax.broadcasted_iota(jnp.int32, shape, axis)


def one_hot(rows, cols, row_of_col):
    return jnp.where(iota((rows, cols), 0) == row_of_col, 1.0, 0.0).astype(BF)


def norm_stats(summed):
    centre = jnp.mean(summed, axis=1, keepdims=True)
    deviation = summed - centre
    inverse = lax.rsqrt(jnp.mean(deviation * deviation, axis=1, keepdims=True) + EPSILON)
    return deviation * inverse, inverse


def norm_back(upstream, normed, inverse, gain):
    scaled = upstream * gain
    inner = jnp.mean(scaled, axis=1, keepdims=True)
    cross = jnp.mean(scaled * normed, axis=1, keepdims=True)
    return inverse * (scaled - inner - normed * cross)


def gelu(pre):
    return (0.5 * pre) * (1.0 + lax.erf(pre * (0.5**0.5)))


def gelu_parts(pre):
    phi = 0.5 + 0.5 * lax.erf(pre * (0.5**0.5))
    density = jnp.exp(-0.5 * (pre * pre)) * 0.3989422804014327
    return pre * phi, phi + pre * density


def spread_heads(rows):
    head = iota((1, rows.shape[1]), 1) // HD
    return jnp.concatenate(
        [jnp.where(head == h, rows, jnp.zeros_like(rows)) for h in range(HEADS)], axis=0
    )


def fold_heads(wide):
    count = wide.shape[0] // HEADS
    head = iota((1, wide.shape[1]), 1) // HD
    total = jnp.zeros((count, wide.shape[1]), wide.dtype)
    for h in range(HEADS):
        total = jnp.where(head == h, wide[h * count : (h + 1) * count], total)
    return total


class Fetched:
    def __init__(self, source, buffer, semaphores, axis=0, parts=1):
        self.buffer, self.shape = buffer, buffer.shape
        self.axis, self.size = axis, buffer.shape[axis] // parts
        self.waiting, self.copies = {}, []
        for i in range(parts):
            at = self.place(i) if parts > 1 else (Ellipsis,)
            self.copies.append(pltpu.make_async_copy(source.at[at], buffer.at[at], semaphores.at[i]))

    def start(self):
        if not self.waiting and self.copies:
            self.waiting = dict(enumerate(self.copies))
            self.copies = []
            for copy in self.waiting.values():
                copy.start()

    def place(self, i):
        return (slice(None),) * self.axis + (pl.ds(i * self.size, self.size),)

    def part(self, i):
        self.start()
        if i in self.waiting:
            self.waiting.pop(i).wait()
        return self.buffer[self.place(i)]

    def ref(self):
        self.start()
        for i in sorted(self.waiting):
            self.waiting.pop(i).wait()
        return self.buffer

    def __getitem__(self, index):
        return self.ref()[index]


class Result:
    def __init__(self, buffer, target, semaphores):
        self.buffer, self.target, self.semaphores = buffer, target, semaphores
        self.shape, self.dtype, self.copies = buffer.shape, buffer.dtype, []

    def __setitem__(self, index, value):
        self.buffer[index] = value

    def __getitem__(self, index):
        return self.buffer[index]

    def flush(self, first=None, size=None):
        source, target = self.buffer, self.target
        if first is not None:
            source, target = source.at[pl.ds(first, size)], target.at[pl.ds(first, size)]
        copy = pltpu.make_async_copy(source, target, self.semaphores.at[len(self.copies)])
        copy.start()
        self.copies.append(copy)


PARTS = 4
TOKEN = ((8, 128), F32, False)


def call(kernel, outs, ins, flops=0, scratch=(), limit=8, far=(), smem=(), split=None, late=(), after=(), name=None):
    n_in, n_out, n_after = len(ins), len(outs), len(after)
    split = split or {}
    far_in = list(smem) + [i for i in far if i not in smem]
    far_out = [i for i in range(n_out) if not outs[i][2]]
    shapes = [(pltpu.VMEM if near else pltpu.HBM)(s, d) for s, d, near in list(outs) + [TOKEN]]
    moved = sum(x.size * x.dtype.itemsize for x in ins)
    moved += sum(int(np.prod(s)) * jnp.dtype(d).itemsize for s, d, _ in outs)
    ins = [pltpu.with_memory_space_constraint(x, pltpu.HBM) if i in far_in else x for i, x in enumerate(ins)]
    after = [pltpu.with_memory_space_constraint(x, pltpu.HBM) for x in after]

    def wrapped(*refs):
        refs = list(refs)
        in_refs, refs = refs[:n_in], refs[n_in + n_after :]
        out_refs, refs = refs[:n_out], refs[n_out + 1 :]
        in_bufs, refs = refs[: len(far_in)], refs[len(far_in) :]
        out_bufs, refs = refs[: len(far_out)], refs[len(far_out) :]
        if far_in:
            semaphores, refs = refs[0], refs[1:]
            for k, i in enumerate(far_in):
                in_refs[i] = Fetched(in_refs[i], in_bufs[k], semaphores.at[k], *split.get(i, ()))
                if i not in late:
                    in_refs[i].start()
        if far_out:
            semaphores, refs = refs[0], refs[1:]
            for k, i in enumerate(far_out):
                out_refs[i] = Result(out_bufs[k], out_refs[i], semaphores.at[k])
        kernel(*in_refs, *out_refs, *refs)
        for i in far_in:
            in_refs[i].ref()
        for i in far_out:
            if not out_refs[i].copies:
                out_refs[i].flush()
        for i in far_out:
            for copy in out_refs[i].copies:
                copy.wait()

    hbm = pl.BlockSpec(memory_space=pltpu.HBM)
    spaces = [hbm if i in far_in else VM for i in range(n_in)] + [hbm] * n_after
    out_spaces = [hbm if i in far_out else VM for i in range(n_out)] + [hbm]
    buffers = [(pltpu.SMEM if i in smem else pltpu.VMEM)(ins[i].shape, ins[i].dtype) for i in far_in]
    buffers += [pltpu.VMEM(outs[i][0], outs[i][1]) for i in far_out]
    if far_in:
        buffers.append(pltpu.SemaphoreType.DMA((len(far_in), PARTS)))
    if far_out:
        buffers.append(pltpu.SemaphoreType.DMA((len(far_out), PARTS)))
    return pl.pallas_call(
        wrapped,
        out_shape=shapes,
        in_specs=spaces,
        out_specs=out_spaces,
        scratch_shapes=buffers + list(scratch),
        compiler_params=pltpu.CompilerParams(vmem_limit_bytes=limit * MIB),
        cost_estimate=pl.CostEstimate(
            flops=int(flops), bytes_accessed=int(moved), transcendentals=0
        ),
        name=name,
    )(*ins, *after)


def behind(value, *tokens):
    tokens = [pltpu.with_memory_space_constraint(x, pltpu.HBM) for x in tokens]
    return pl.pallas_call(
        lambda *refs: None,
        out_shape=pltpu.VMEM(value.shape, value.dtype),
        in_specs=[VM] + [pl.BlockSpec(memory_space=pltpu.HBM)] * len(tokens),
        out_specs=VM,
        input_output_aliases={0: 0},
        compiler_params=pltpu.CompilerParams(vmem_limit_bytes=MIB),
        name="hand_on",
    )(value, *tokens)


class Rows:
    def __init__(self, batch_n, n_query, n_pass, pass_count):
        block = n_query + 3 * n_pass
        block += -block % 16
        self.batch_n, self.n_query, self.n_pass, self.block = batch_n, n_query, n_pass, block
        self.half = block // 2
        self.columns = pass_count + 1 + -(pass_count + 1) % 128
        self.count = batch_n * block
        self.quarter = block // 4
        self.slot = self.quarter + -self.quarter % 16
        core, batch, rest = np.meshgrid(
            np.arange(2), np.arange(batch_n), np.arange(self.half), indexing="ij"
        )
        place = (core * self.half + rest).reshape(-1)
        batch = batch.reshape(-1)
        self.code = (batch * block + place).astype(np.int32)
        y, peer, spot = np.meshgrid(
            np.arange(2), np.arange(batch_n), np.arange(self.slot), indexing="ij"
        )
        spot = np.where(spot < self.quarter, peer * self.half + y * self.quarter + spot, -1).reshape(-1)
        self.slots = np.concatenate([spot, np.where(spot < 0, -1, spot + batch_n * self.half)])
        self.slots = self.slots.astype(np.int32)
        self.query = np.where(place < n_query, batch * n_query + place, -1).astype(np.int32)
        group, slot = (place - n_query) // n_pass, (place - n_query) % n_pass
        is_pass = (place >= n_query) & (group < 3)
        self.passage = np.where(is_pass, (group * batch_n + batch) * n_pass + slot, -1).astype(np.int32)


def core_chip():
    side = lax.axis_index("side")
    return side % 2, side // 2


def block_source(rows, at):
    core, chip = core_chip()
    n, p = rows.n_query, rows.n_pass
    begin = lambda c, y: jnp.where(y == chip, 0, 2 * n) + jnp.where(c == core, 0, n)
    source = jnp.where(at < n + 3 * p, begin(1, 1) + at - (n + 2 * p), -1)
    source = jnp.where(at < n + 2 * p, begin(0, 1) + at - (n + p), source)
    source = jnp.where(at < n + p, begin(1, 0) + at - n, source)
    return jnp.where(at < n, begin(0, 0) + at, source)


def take_rows(source, parts):
    total = sum(p.shape[0] for p in parts)
    pick = jnp.where(iota((source.shape[0], total), 1) == source, 1.0, 0.0).astype(BF)
    return dot(pick, jnp.concatenate([p[...] for p in parts], axis=0)).astype(BF)


def half_kernel(rows, own_ref, other_ref, far_ref, far_other_ref, *refs):
    core, chip = core_chip()
    n = rows.n_query
    at = iota((rows.half, 1), 0) + core * rows.half
    half = take_rows(block_source(rows, at), (own_ref, other_ref, far_ref, far_other_ref))
    out_ref = refs[-1]
    if len(refs) == 1:
        out_ref[...] = half
        return
    full = jnp.concatenate([half, refs[0][...]], axis=0)
    for b in range(rows.batch_n):
        out_ref[b] = full


def teacher_terms(rows, teacher_ref, pair_ref, out_ref):
    core, _ = core_chip()
    count, told = rows.n_query // 2, teacher_ref.shape[1]
    line = iota((count, 1), 0)
    pair = jnp.zeros((count, 1), jnp.int32)
    for i in range(count):
        pair = jnp.where(line == i, pair_ref.ref()[core * count + i], pair)
    pair = jnp.broadcast_to(pair.astype(F32), (count, rows.columns - told))
    mine = jnp.where(core == 0, teacher_ref[:count, :], teacher_ref[count:, :])
    mine = jnp.concatenate([mine, pair], axis=1)
    high = mine.astype(BF)
    mid = (mine - high.astype(F32)).astype(BF)
    low = (mine - high.astype(F32) - mid.astype(F32)).astype(BF)
    terms = jnp.concatenate([high, mid, low], axis=1)
    side = out_ref.shape[1] // 2
    terms = jnp.concatenate([terms, jnp.zeros((count, side - terms.shape[1]), BF)], axis=1)
    out_ref[...] = jnp.concatenate([terms[: count // 2], terms[count // 2 :]], axis=1)


def near_rows(own, *tokens):
    other = lax.ppermute(own, "side", CORE_SWAP)
    far = lax.ppermute(own, "side", CHIP_SWAP)
    if tokens:
        far = behind(far, *tokens)
    return own, other, far, lax.ppermute(far, "side", CORE_SWAP)


def join_halves(core, mine, theirs):
    return jnp.concatenate(
        [jnp.where(core == 0, mine, theirs), jnp.where(core == 0, theirs, mine)], axis=0
    )


def cls_probs(pick, query, key_ref, seg_ref):
    seg = seg_ref[0].astype(F32)
    cls_seg = jnp.sum(jnp.where(pick, seg, 0.0), axis=1, keepdims=True)
    bias = jnp.where(cls_seg == seg, 0.0, NEG_FILL)
    scores = dot_t(spread_heads(query) * BF(HD**-0.5), key_ref[...])
    scores = scores + jnp.concatenate([bias] * HEADS, axis=0)
    expo = jnp.exp(scores - jnp.max(scores, axis=1, keepdims=True))
    return expo / jnp.sum(expo, axis=1, keepdims=True)


def cls_forward_kernel(
    rows, with_terms, x_ref, seg_ref, query_cls_ref, pass_cls_ref, wq_ref, bq_ref, wk_ref, wv_ref, bv_ref,
    teacher_ref, pair_ref, rows_ref, query_ref, pick_ref, key_ref, value_ref, terms_ref,
):
    n_pass = rows.n_pass
    side = lax.axis_index("side")
    n_query, width = query_ref.shape
    slot = iota((n_query, 1), 0)
    cls = jnp.full((n_query, 1), -1, jnp.int32)
    for i in range(n_query):
        place = jnp.where(side == 0, query_cls_ref.ref()[0, i], pass_cls_ref.ref()[0, 0, i] if i < n_pass else -1)
        cls = jnp.where(slot == i, place, cls)
    pick = iota((n_query, x_ref.shape[0]), 1) == cls
    pick_low = jnp.where(pick, 1.0, 0.0).astype(BF)
    pick_ref[...] = pick_low
    pick_ref.flush()
    if with_terms:
        teacher_terms(rows, teacher_ref, pair_ref, terms_ref)
    for i in range(PARTS):
        part = slice(i * x_ref.size, i * x_ref.size + x_ref.size)
        key_ref[part, :] = dot(x_ref.part(i), wk_ref[...]).astype(BF)
    key_ref.flush()
    x = x_ref.ref()
    value_ref[...] = (dot(x[...], wv_ref[...]) + bv_ref[...]).astype(BF)
    value_ref.flush()
    tokens = dot(pick_low, x[...]).astype(BF)
    query = (dot(tokens, wq_ref[...]) + bq_ref[...]).astype(BF)
    query_ref[...] = query
    query_ref.flush()
    probs = cls_probs(pick, query, key_ref, seg_ref)
    rows_ref[:, :width] = fold_heads(dot(probs.astype(BF), value_ref[...])).astype(BF)
    rows_ref[:, width:] = tokens


def middle_kernel(
    rows, pass_count,
    mine_ref, theirs_ref, wo_ref, vector_ref, wi_ref, wu_ref, at_ref, value_ref, probs_ref, x_ref, key_ref, query_ref, cluster_ref,
    keep_ref, give_ref, low_ref, context_ref, gown_ref, scores_ref,
    loss_ref, small_ref, inner_bias_ref,
    both_ref, first_ref, active_ref, pre_ref, second_ref, attended_ref, slope_ref, told_ref,
):
    width = wo_ref.shape[0]
    bo_ref, g1_ref, s1_ref, bu_ref, g2_ref, s2_ref, bi_ref = vectors_of(vector_ref, width)
    n_queries, n_columns = told_ref.shape
    chunk = wi_ref.shape[1] // PARTS
    side, batch = lax.axis_index("side"), lax.axis_index("batch")
    core = side % 2
    code_at, query_at, pass_at = at_ref[0:1, :], at_ref[1:2, :], at_ref[2:3, :]
    count = rows.n_query // 2
    for half in range(2):
        for b in range(rows.batch_n):
            one = jnp.where(core == half, mine_ref[b], theirs_ref[b])
            first_row = (half * rows.batch_n + b) * rows.half
            both_ref[first_row : first_row + rows.half, :] = one[: rows.half]
            terms = one[rows.half :].astype(F32)
            for part in range(2):
                begin = part * one.shape[1] // 2
                cut = [terms[:, begin + k * n_columns : begin + (k + 1) * n_columns] for k in range(3)]
                row = b * rows.n_query + half * count + part * count // 2
                told_ref[row : row + count // 2, :] = cut[0] + cut[1] + cut[2]
    attended = both_ref[:, width:].astype(F32) + (dot(both_ref[:, :width], wo_ref[...]) + bo_ref[...])
    first_hat, first_inv = norm_stats(attended)
    for ref in (value_ref, probs_ref, x_ref, key_ref, query_ref):
        ref.start()
    first = first_hat * g1_ref[...] + s1_ref[...]
    first_low = first.astype(BF)
    first_ref[...] = first_low
    second = first + bu_ref[...]
    for i in range(PARTS):
        c = i * chunk
        pre = dot(first_low, wi_ref[:, c : c + chunk]) + bi_ref[:, c : c + chunk]
        active, slope = gelu_parts(pre)
        active = active.astype(BF)
        active_ref[:, c : c + chunk] = active
        slope_ref[:, c : c + chunk] = slope
        second += dot(active, wu_ref[c : c + chunk, :])
    both_ref.flush()
    first_ref.flush()
    active_ref.flush()
    second_hat, second_inv = norm_stats(second)
    final = (second_hat * g2_ref[...] + s2_ref[...]).astype(BF)

    scale = width ** (-0.5)
    query_pick = one_hot(n_queries, rows.count, query_at)
    pass_pick = one_hot(n_columns, rows.count, pass_at)
    query_vec = dot(query_pick, final).astype(BF)
    pass_vec = dot(pass_pick, final).astype(BF)
    score = dot_t(query_vec, pass_vec) * scale
    column = iota((n_queries, n_columns), 1)
    is_pair = column == told_ref[:, n_columns - 1 :].astype(jnp.int32)
    cluster = jnp.full((1, n_columns), -1.0, F32)
    for j in range(pass_count):
        cluster = jnp.where(column[:1] == j, cluster_ref.ref()[j].astype(F32), cluster)
    query_cluster = jnp.sum(jnp.where(is_pair, cluster, 0.0), axis=1, keepdims=True)
    counted = (cluster == query_cluster) & jnp.logical_not(is_pair) & (column < pass_count)
    pair_score = jnp.sum(jnp.where(is_pair, score, 0.0), axis=1, keepdims=True)
    resid = jnp.where(counted, pair_score - score - told_ref[...], 0.0)
    squares = jnp.sum(jnp.sum(resid * resid, axis=1, keepdims=True), axis=0, keepdims=True)
    pairs = jnp.where(counted, 1.0, 0.0)
    pairs = jnp.sum(jnp.sum(pairs, axis=1, keepdims=True), axis=0, keepdims=True)
    loss_ref[...] = squares / jnp.maximum(pairs, 1.0)
    loss_ref.flush()
    grad_score = jnp.where(is_pair, jnp.sum(resid, axis=1, keepdims=True), 0.0) - resid
    grad_low = (grad_score * scale).astype(BF)
    grad_rows = dot(t_dot(query_pick, grad_low).astype(BF), pass_pick).astype(BF)
    grad_final = dot(grad_rows, final) + t_dot(grad_rows, final)

    def note(at, value):
        small_ref[at : at + 1, :] = jnp.sum(value, axis=0, keepdims=True)

    grad_second = norm_back(grad_final, second_hat, second_inv, g2_ref[...])
    second_low = grad_second.astype(BF)
    second_ref[...] = second_low
    grad_first = grad_second
    for i in range(PARTS):
        c = i * chunk
        grad_pre = dot_t(second_low, wu_ref[c : c + chunk, :]) * slope_ref[:, c : c + chunk]
        inner_bias_ref[:, c : c + chunk] = jnp.sum(grad_pre, axis=0, keepdims=True)
        pre_low = grad_pre.astype(BF)
        pre_ref[:, c : c + chunk] = pre_low
        grad_first += dot_t(pre_low, wi_ref[:, c : c + chunk])
    inner_bias_ref.flush()
    pre_ref.flush()
    second_ref.flush()
    grad_attended = norm_back(grad_first, first_hat, first_inv, g1_ref[...])
    attended_low = grad_attended.astype(BF)
    attended_ref[...] = attended_low
    attended_ref.flush()
    grad_context = dot_t(attended_low, wo_ref[...]).astype(BF)
    note(0, grad_final * second_hat)
    note(1, grad_final)
    note(2, grad_second)
    note(3, grad_first * first_hat)
    note(4, grad_first)
    note(5, grad_attended)
    note(6, grad_context.astype(F32))
    small_ref[7:8, :] = jnp.zeros((1, width), F32)
    small_ref.flush()


    slot = iota((rows.n_query, 1), 0)
    base = batch * rows.block + jnp.where(side == 0, 0, rows.n_query + rows.n_pass * (side - 1))
    live = slot < jnp.where(side == 0, rows.n_query, rows.n_pass)
    own = (code_at == base + slot) & live
    high = grad_attended.astype(BF)
    rest = (grad_attended - high.astype(F32)).astype(BF)
    own = jnp.where(own, 1.0, 0.0).astype(BF)
    gown_ref[...] = dot(own, high) + dot(own, rest)
    gown_ref.flush()
    context = dot(own, grad_context).astype(BF)
    context_ref[...] = context
    context_ref.flush()
    wide = spread_heads(context)
    probs = probs_ref[...]
    grad_probs = dot_t(wide, value_ref[...])
    row_dot = jnp.sum(probs * grad_probs, axis=1, keepdims=True)
    grad_scores = (probs * (grad_probs - row_dot)).astype(BF)
    scores_ref[...] = grad_scores
    scores_ref.flush()
    query_wide = spread_heads(query_ref[...]) * BF(HD**-0.5)
    x = x_ref.ref()
    key_side = dot(grad_scores, x[...]).astype(BF)
    value_side = dot(probs.astype(BF), x[...]).astype(BF)
    key_part = t_dot(key_side, query_wide)
    value_part = t_dot(value_side, wide)
    keep_ref[...] = jnp.where(core == 0, key_part, value_part)
    give_ref[...] = jnp.where(core == 0, value_part, key_part).astype(BF)
    low_ref[...] = (fold_heads(dot(grad_scores, key_ref[...])) * HD**-0.5).astype(BF)


def input_grad_kernel(
    pick_ref, scores_ref, probs_ref, context_ref, query_ref, low_ref, gown_ref,
    wq_ref, wk_ref, wv_ref, out_ref,
):
    query_wide = spread_heads(query_ref[...]) * BF(HD**-0.5)
    key_low = t_dot(scores_ref[...], query_wide).astype(BF)
    value_low = t_dot(probs_ref[...].astype(BF), spread_heads(context_ref[...])).astype(BF)
    sparse = gown_ref[...] + dot_t(low_ref[...], wq_ref[...])
    high = sparse.astype(BF)
    rest = (sparse - high.astype(F32)).astype(BF)
    pick = pick_ref[...]
    total = dot_t(key_low, wk_ref[...]) + dot_t(value_low, wv_ref[...])
    total += t_dot(jnp.concatenate([pick, pick], axis=0), jnp.concatenate([high, rest], axis=0))
    out_ref[...] = total.astype(BF)


def chip_sum_kernel(keep_ref, got_ref, out_ref):
    out_ref[...] = (keep_ref[...] + got_ref[...].astype(F32)).astype(BF)


def add_parts_kernel(rows, parts_ref, own_ref, other_ref, far_ref, far_other_ref, out_ref):
    core, chip = core_chip()
    peers, size = parts_ref.shape[:2]
    total = parts_ref[0].astype(F32)
    for i in range(1, peers):
        total += parts_ref[i].astype(F32)
    at = iota((rows.slot, 1), 0)
    source = block_source(rows, core * rows.half + chip * rows.quarter + at)
    source = jnp.where(at < rows.quarter, source, -1)
    low = take_rows(source, (own_ref, other_ref, far_ref, far_other_ref))
    total = jnp.concatenate([total.astype(BF), low], axis=0)
    for i in range(peers):
        out_ref[i] = total


def last_kernel(size, mine_ref, theirs_ref, x_ref, key_ref, value_ref, query_ref, bias_ref):
    core, _ = core_chip()
    peers = mine_ref.shape[0]
    step = peers // PARTS
    for i in range(PARTS):
        for j in range(i * step, i * step + step):
            mine, theirs = mine_ref[j, :size].astype(F32), theirs_ref[j, :size].astype(F32)
            key_ref[j * size : j * size + size, :] = jnp.where(core == 0, mine, theirs)
            value_ref[j * size : j * size + size, :] = jnp.where(core == 0, theirs, mine)
        key_ref.flush(i * step * size, step * size)
        value_ref.flush(i * step * size, step * size)
    mine = jnp.concatenate([mine_ref[j, size:] for j in range(peers)], axis=0)
    theirs = jnp.concatenate([theirs_ref[j, size:] for j in range(peers)], axis=0)
    low = join_halves(core, mine, theirs)
    bias_ref[...] = jnp.sum(low.astype(F32), axis=0, keepdims=True)
    part_rows(query_ref, x_ref, low)


def core_groups(batch_n):
    return [[(y * 2 + c) * batch_n + b for y in range(2) for b in range(batch_n)] for c in range(2)]


def exchange(sent, batch_n):
    return lax.all_to_all(
        sent, ("side", "batch"), split_axis=0, concat_axis=0, axis_index_groups=core_groups(batch_n)
    )


def scatter_sum(keep, give, batch_n):
    got = lax.ppermute(give, "side", CORE_SWAP)
    total, token = call(chip_sum_kernel, [(keep.shape, BF, True)], (keep, got), name="chip_sum")
    return exchange(total.reshape(2 * batch_n, keep.shape[0] // (2 * batch_n), keep.shape[1]), batch_n), token


def part_rows(result, left, right):
    size = result.shape[0] // PARTS
    for i in range(PARTS):
        result[i * size : i * size + size, :] = t_dot(left[:, i * size : i * size + size], right)
        result.flush(i * size, size)


def weight_grads_kernel(
    active_ref, second_ref, first_ref, pre_ref, both_ref, attended_ref, slots_ref,
    outer_ref, inner_ref, out_ref, x_ref,
):
    part_rows(outer_ref, active_ref, second_ref[...])
    part_rows(inner_ref, first_ref, pre_ref[...])
    part_rows(out_ref, both_ref, attended_ref[...])
    width = out_ref.shape[0]
    count = both_ref.shape[0]
    pick = one_hot(count, slots_ref.shape[1], slots_ref[...])
    x_ref[...] = t_dot(pick, both_ref[:, width:]).astype(BF)


class Row:
    def __init__(self, source, at, width):
        self.source, self.at, self.width = source, at, width

    def __getitem__(self, index):
        first, last = 0, self.width
        if index is not Ellipsis:
            first, last = index[1].start, index[1].stop
        return self.source[self.at : self.at + 1, first:last]


def vectors_of(source, width):
    return [Row(source, i, width) for i in range(6)] + [Row(source, 6, source.shape[1])]


def column_of(row):
    return jnp.transpose(jnp.broadcast_to(row, (128, row.shape[1])))[:, :1]


def attention_kernel(
    tile, sizes, x_ref, wq_ref, bq_ref, key_ref, value_ref, seg_ref, *refs
):
    pick_ref, query_ref = refs[:2]
    out_ref, vector_ref, probs_ref, q_scr, bias_scr = refs[-5:]
    count = x_ref.shape[0]
    x, wq, bq, seg = x_ref.ref(), wq_ref.ref(), bq_ref[...], seg_ref[0]
    places = iota((1, count), 1)
    keys, values = key_ref.ref(), value_ref.ref()

    for i, ref in enumerate(refs[2:-5]):
        vector_ref[i : i + 1, : ref.shape[1]] = ref[...]
    vector_ref.flush()
    probs_ref[...] = cls_probs(pick_ref[...].astype(F32) > 0.5, query_ref[...], key_ref, seg_ref)
    probs_ref.flush()

    @pl.loop(0, count // tile)
    def _(i):
        row = pl.multiple_of(i * tile, tile)
        q = (dot(x[pl.ds(row, tile), :], wq[...]) + bq).astype(BF)
        q_scr[...] = q * BF(HD**-0.5)
        first = jnp.max(jnp.where(places == row, seg, -2))
        last = jnp.max(jnp.where(places == row + (tile - 1), seg, -2))
        low = jnp.min(jnp.where(seg == first, places, count)) // 128 * 128
        high = jnp.max(jnp.where(seg == last, places, -1)) + 1
        own = seg_ref.ref()[0, :, pl.ds(row, tile)].astype(F32)
        own = column_of(own)
        before = jnp.int32(0)
        for size in sizes:
            start = jnp.minimum(low, count - size)
            fits = (high - start <= size) if size < count else jnp.bool_(True)

            @pl.when(jnp.logical_and(before == 0, fits))
            def _(size=size, start=start):
                at = pl.multiple_of(start, 128)
                near = seg_ref.ref()[0, :, pl.ds(at, size)].astype(F32)
                bias_scr[:, :size] = jnp.where(own == near, 0.0, NEG_FILL)
                half = iota((1, 2 * HD), 1) // HD
                slabs = [slice(h // 2 * 2 * HD, h // 2 * 2 * HD + 2 * HD) for h in range(HEADS)]
                scores = [
                    dot_t(
                        jnp.where(half == h % 2, q_scr[:, slabs[h]], BF(0)),
                        keys[pl.ds(at, size), slabs[h]],
                    )
                    + bias_scr[:, :size]
                    for h in range(HEADS)
                ]
                expos = [jnp.exp(s - jnp.max(s, axis=1, keepdims=True)).astype(BF) for s in scores]
                outs = []
                for h in range(HEADS):
                    ones = jnp.where(half == h % 2, values[pl.ds(at, size), slabs[h]], BF(1))
                    mixed = dot(expos[h], ones)
                    outs.append(mixed / pltpu.roll(mixed, HD, 1))
                for h in range(0, HEADS, 2):
                    out_ref.buffer[pl.ds(row, tile), slabs[h]] = jnp.where(
                        half == 0, outs[h], outs[h + 1]
                    ).astype(BF)

            before = jnp.where(fits, 1, before)


def attention(x, wq, bq, keys, values, seg, pick, query, vectors, after, tile=256):
    t, d = x.shape
    sizes = [s for s in (384, 512, 768) if s < t] + [t]
    return call(
        functools.partial(attention_kernel, tile, sizes),
        [
            ((t, d), BF, False),
            ((8, vectors[-1].shape[1]), F32, False),
            ((HEADS * query.shape[0], t), F32, False),
        ],
        (x, wq, bq, keys, values, seg, pick, query) + vectors,
        flops=8 * 10**9,
        far=range(8 + len(vectors)),
        scratch=[pltpu.VMEM((tile, d), BF), pltpu.VMEM((tile, t), F32)],
        limit=20,
        after=after,
        name="attention",
    )


def ffn_kernel(
    tile, x_ref, c_ref, wo_ref, vector_ref, wi_ref, wu_ref, out_ref,
):
    bo_ref, g1_ref, s1_ref, bu_ref, g2_ref, s2_ref, bi_ref = vectors_of(vector_ref, x_ref.shape[1])
    chunk = wi_ref.size
    for t in range(0, x_ref.shape[0], tile):
        part = slice(t, t + tile)
        attended = x_ref[part, :].astype(F32) + (dot(c_ref[part, :], wo_ref[...]) + bo_ref[...])
        first = norm_stats(attended)[0] * g1_ref[...] + s1_ref[...]
        first_low = first.astype(BF)
        second = first + bu_ref[...]
        for c in range(PARTS):
            pre = dot(first_low, wi_ref.part(c)) + bi_ref[:, c * chunk : c * chunk + chunk]
            second += dot(gelu(pre).astype(BF), wu_ref.part(c))
        out_ref[part, :] = (norm_stats(second)[0] * g2_ref[...] + s2_ref[...]).astype(BF)
        out_ref.flush(t, tile)


def ffn(x, context, weights, after, tile=512):
    return call(
        functools.partial(ffn_kernel, tile),
        [(x.shape, BF, False)],
        (x, context) + weights,
        flops=6 * 10**9,
        far=range(6),
        limit=20,
        split={4: (1, PARTS), 5: (0, PARTS)},
        after=after,
        name="feed_forward",
    )


def middle_large(
    rows, pass_count, core, mine, theirs, told, cluster, wo, bo, g1, s1, wi, bi, wu, bu, g2, s2
):
    width = wo.shape[0]
    both = join_halves(core, mine, theirs)
    attended = both[:, width:].astype(F32) + (dot(both[:, :width], wo) + bo)
    first_hat, first_inv = norm_stats(attended)
    first = first_hat * g1 + s1
    first_low = first.astype(BF)
    active, slope = gelu_parts(dot(first_low, wi) + bi)
    active_low = active.astype(BF)
    second = first + (dot(active_low, wu) + bu)
    second_hat, second_inv = norm_stats(second)
    final = (second_hat * g2 + s2).astype(BF)
    order_q = np.argsort(rows.query, kind="stable")[-rows.batch_n * rows.n_query :]
    order_p = np.argsort(rows.passage, kind="stable")[-pass_count:]
    query_vec, pass_vec = final[order_q], final[order_p]
    scale = width ** (-0.5)
    score = dot_t(query_vec, pass_vec) * scale
    is_pair = iota(score.shape, 1) == told[:, pass_count:].astype(jnp.int32)
    query_cluster = jnp.sum(jnp.where(is_pair, cluster, 0.0), axis=1, keepdims=True)
    counted = (cluster == query_cluster) & jnp.logical_not(is_pair)
    pair_score = jnp.sum(jnp.where(is_pair, score, 0.0), axis=1, keepdims=True)
    resid = jnp.where(counted, pair_score - score - told[:, :pass_count], 0.0)
    loss = jnp.sum(resid * resid) / jnp.maximum(jnp.sum(counted.astype(F32)), 1.0)
    grad_score = jnp.where(is_pair, jnp.sum(resid, axis=1, keepdims=True), 0.0) - resid
    grad_low = (grad_score * scale).astype(BF)
    grad_final = jnp.zeros((rows.count, width), F32)
    grad_final = grad_final.at[order_q].set(dot(grad_low, pass_vec))
    grad_final = grad_final.at[order_p].set(t_dot(grad_low, query_vec))
    grad_second = norm_back(grad_final, second_hat, second_inv, g2)
    second_low = grad_second.astype(BF)
    grad_pre = dot_t(second_low, wu) * slope
    pre_low = grad_pre.astype(BF)
    grad_first = dot_t(pre_low, wi) + grad_second
    grad_attended = norm_back(grad_first, first_hat, first_inv, g1)
    attended_low = grad_attended.astype(BF)
    grad_context = dot_t(attended_low, wo).astype(BF)
    small = jnp.stack(
        [
            jnp.sum(v, axis=0)
            for v in (
                grad_final * second_hat, grad_final, grad_second, grad_first * first_hat,
                grad_first, grad_attended, grad_context.astype(F32),
            )
        ]
    )
    inner_bias = jnp.sum(grad_pre, axis=0, keepdims=True)
    return (
        loss.reshape(1, 1), grad_attended, grad_context, small, inner_bias,
        both, first_low, active_low, pre_low, second_low, attended_low,
    )


def own_large(rows, side, batch, grad_attended, grad_context, tokens, keys, values, cls_query, probs):
    core = side % 2
    slot = jnp.arange(rows.n_query)[:, None]
    base = batch * rows.block + jnp.where(side == 0, 0, rows.n_query + rows.n_pass * (side - 1))
    live = slot < jnp.where(side == 0, rows.n_query, rows.n_pass)
    own = ((rows.code[None, :] == base + slot) & live).astype(F32)
    own_attended = dot(own, grad_attended, lax.Precision.HIGHEST)
    context = dot(own.astype(BF), grad_context).astype(BF)
    wide = spread_heads(context)
    grad_probs = dot_t(wide, values)
    row_dot = jnp.sum(probs * grad_probs, axis=1, keepdims=True)
    grad_scores = (probs * (grad_probs - row_dot)).astype(BF)
    query_wide = spread_heads(cls_query) * BF(HD**-0.5)
    key_part = t_dot(dot(grad_scores, tokens).astype(BF), query_wide)
    value_part = t_dot(dot(probs.astype(BF), tokens).astype(BF), wide)
    keep = jnp.where(core == 0, key_part, value_part)
    give = jnp.where(core == 0, value_part, key_part).astype(BF)
    low = (fold_heads(dot(grad_scores, keys)) * HD**-0.5).astype(BF)
    return keep, give, low, context, own_attended, grad_scores


def fetch(arrays, behind_this):
    hbm = pl.BlockSpec(memory_space=pltpu.HBM)
    count = len(arrays)

    def kernel(*refs):
        semaphores = refs[-1]
        copies = [
            pltpu.make_async_copy(refs[i], refs[count + 1 + i], semaphores.at[i]) for i in range(count)
        ]
        for copy in copies:
            copy.start()
        for copy in copies:
            copy.wait()

    return pl.pallas_call(
        kernel,
        out_shape=[pltpu.VMEM(x.shape, x.dtype) for x in arrays],
        in_specs=[hbm] * count + [VM],
        out_specs=[VM] * count,
        scratch_shapes=[pltpu.SemaphoreType.DMA((count,))],
        compiler_params=pltpu.CompilerParams(vmem_limit_bytes=4 * MIB),
        name="fetch",
    )(*[pltpu.with_memory_space_constraint(x, pltpu.HBM) for x in arrays], behind_this)


def middle(rows, pass_count, mine, theirs, kept, weights, cluster, hidden, after):
    width, ff = weights[2].shape
    count = rows.count
    keys, values, cls_query, probs = kept
    at = np.stack([rows.code, rows.query, rows.passage])
    ins = (mine, theirs) + weights + (at, values, probs, hidden, keys, cls_query, cluster)
    outs = [
        ((width, width), F32, True), ((width, width), BF, True), ((rows.n_query, width), BF, True),
        ((rows.n_query, width), BF, False), ((rows.n_query, width), F32, False), (probs.shape, BF, False),
        ((1, 1), F32, False), ((8, width), F32, False), ((1, ff), F32, False),
        ((count, 2 * width), BF, False), ((count, width), BF, False), ((count, ff), BF, False),
        ((count, ff), BF, False), ((count, width), BF, False), ((count, width), BF, False),
    ]
    return call(
        functools.partial(middle_kernel, rows, pass_count),
        outs,
        ins,
        flops=12 * count * width * ff,
        scratch=[
            pltpu.VMEM((count, ff), F32),
            pltpu.VMEM((rows.batch_n * rows.n_query, rows.columns), F32),
        ],
        far=range(6, len(ins)),
        smem=(len(ins) - 1,),
        late=range(7, len(ins) - 1),
        limit=32,
        after=after,
        name="cls_middle",
    )


def body(
    hidden_in,
    segments,
    query_cls,
    passage_cls,
    pair_passage,
    passage_cluster,
    teacher,
    query_weight,
    query_bias,
    key_weight,
    value_weight,
    value_bias,
    out_weight,
    out_bias,
    first_gain,
    first_shift,
    inner_weight,
    inner_bias,
    outer_weight,
    outer_bias,
    second_gain,
    second_shift,
):
    count_tok = hidden_in.shape[2]
    width = hidden_in.shape[3]
    n_query = query_cls.shape[1]
    n_pass = passage_cls.shape[2]
    batch_n = lax.axis_size("batch")
    side = lax.axis_index("side")
    pass_count = teacher.shape[1]
    rows = Rows(batch_n, n_query, n_pass, pass_count)

    hidden = hidden_in.reshape(count_tok, width)

    def vec(v):
        return v.reshape(1, -1)

    weights = (
        out_weight, vec(out_bias), vec(first_gain), vec(first_shift), inner_weight, vec(inner_bias),
        outer_weight, vec(outer_bias), vec(second_gain), vec(second_shift),
    )
    small_case = rows.count <= 512 and 3 * rows.columns <= width and n_query % 32 == 0

    token = ((count_tok, width), BF, False)
    extra = n_query // 4 if small_case else 8
    own, cls_query, pick, keys, values, terms, _ = call(
        functools.partial(cls_forward_kernel, rows, small_case),
        [
            ((n_query, 2 * width), BF, True),
            ((n_query, width), BF, False),
            ((n_query, count_tok), BF, False),
            token,
            token,
            ((extra, 2 * width), BF, True),
        ],
        (
            hidden, segments, query_cls, passage_cls, query_weight, vec(query_bias), key_weight,
            value_weight, vec(value_bias), teacher, pair_passage,
        ),
        flops=4 * count_tok * width * width,
        far=(6, 0, 9, 7, 1, 4, 5, 8),
        smem=(2, 3, 10),
        split={0: (0, PARTS)},
        limit=24,
        name="cls_forward",
    )

    near = near_rows(own)
    if small_case:
        sent, half_done = call(
            functools.partial(half_kernel, rows),
            [((batch_n, rows.half + extra, 2 * width), BF, True)],
            near + (terms,),
            name="half_rows",
        )
    else:
        half, half_done = call(
            functools.partial(half_kernel, rows),
            [((rows.half, 2 * width), BF, True)],
            near,
            name="half_rows",
        )
        sent = jnp.broadcast_to(half[None], (batch_n,) + half.shape)
    mine = lax.all_to_all(sent, "batch", split_axis=0, concat_axis=0)
    vectors = (weights[1], weights[2], weights[3], weights[7], weights[8], weights[9], weights[5])
    context, vectors, probs, attention_done = attention(
        hidden, query_weight, vec(query_bias), keys, values, segments, pick, cls_query, vectors, (half_done,)
    )
    matrices = (out_weight, vectors, inner_weight, outer_weight)
    if small_case:
        mine = behind(mine, attention_done)
    theirs = lax.ppermute(mine, "side", CORE_SWAP)

    if small_case:
        kept = (keys, values, cls_query, probs)
        (
            keep, give, query_low, own_context, own_attended, grad_scores, loss, small, grad_inner_bias,
            both, first_low, active_low, pre_low, second_low, attended_low, _,
        ) = middle(
            rows, pass_count, mine, theirs, kept, tuple(fetch(matrices, mine)), passage_cluster, hidden, ()
        )
    else:
        told = jnp.concatenate([teacher, pair_passage[:, None].astype(F32)], axis=1)
        told = lax.all_to_all(
            jnp.broadcast_to(told[None], (batch_n,) + told.shape), "batch", split_axis=0, concat_axis=0
        ).reshape(batch_n * n_query, pass_count + 1)
        flat = (batch_n * rows.half, 2 * width)
        (
            loss, grad_attended, grad_context, small, grad_inner_bias,
            both, first_low, active_low, pre_low, second_low, attended_low,
        ) = middle_large(
            rows, pass_count, side % 2, mine.reshape(flat), theirs.reshape(flat), told,
            passage_cluster.astype(F32)[None, :], *weights,
        )
        keep, give, query_low, own_context, own_attended, grad_scores = own_large(
            rows, side, lax.axis_index("batch"), grad_attended, grad_context,
            hidden, keys, values, cls_query, probs,
        )

    parts, sum_done = scatter_sum(keep, give, batch_n)
    input_grad, input_done = call(
        input_grad_kernel,
        [(hidden.shape, BF, False)],
        (
            pick, grad_scores, probs, own_context, cls_query, query_low, own_attended, query_weight,
            key_weight, value_weight,
        ),
        flops=6 * count_tok * width * width,
        far=(1, 4, 2, 3, 0, 6, 8, 9, 7),
        limit=20,
        after=(sum_done,),
        name="input_grad",
    )
    peers, size = parts.shape[:2]
    if small_case and size % 16 == 0:
        saved = (active_low, second_low, first_low, pre_low, both, attended_low, rows.slots[None, :])
        grad_outer_weight, grad_inner_weight, grad_out_weight, all_tokens, weight_done = call(
            weight_grads_kernel,
            [
                (outer_weight.shape, F32, False),
                (inner_weight.shape, F32, False),
                (out_weight.shape, F32, False),
                ((rows.slots.shape[0], width), BF, False),
            ],
            saved,
            flops=2 * rows.count * width * (4 * width + width),
            far=range(7),
            limit=32,
            after=(sum_done,),
            name="weight_grads",
        )
        low = near_rows(query_low, weight_done)
        sent, add_done = call(
            functools.partial(add_parts_kernel, rows),
            [((peers, size + rows.slot, width), BF, True)],
            (parts,) + low,
            after=(input_done, weight_done),
            name="add_parts",
        )
        whole = exchange(sent, batch_n)
        rows_out, ffn_done = ffn(hidden, context, matrices, (add_done,))
        whole = behind(whole, ffn_done)
        other = lax.ppermute(whole, "side", CORE_SWAP)
        grad_key_weight, grad_value_weight, grad_query_weight, grad_query_bias, _ = call(
            functools.partial(last_kernel, size),
            [((width, width), F32, False)] * 3 + [((1, width), F32, False)],
            (whole, other, all_tokens),
            far=(2,),
            limit=12,
            name="last_grads",
        )
    else:
        rows_out, _ = ffn(hidden, context, matrices, (sum_done,))
        part = jnp.sum(parts.astype(F32), axis=0).astype(BF)
        whole = exchange(jnp.broadcast_to(part[None], parts.shape), batch_n).reshape(width, width)
        grad_outer_weight = t_dot(active_low, second_low)
        grad_inner_weight = t_dot(first_low, pre_low)
        grad_out_weight = t_dot(both[:, :width], attended_low)
        half, _ = call(
            functools.partial(half_kernel, rows),
            [((rows.half, width), BF, True)],
            near_rows(query_low),
            name="low_rows",
        )
        flat = (batch_n * rows.half, width)
        half = jnp.broadcast_to(half[None], (batch_n,) + half.shape)
        low_mine = lax.all_to_all(half, "batch", split_axis=0, concat_axis=0).reshape(flat)
        low_theirs = lax.ppermute(low_mine, "side", CORE_SWAP)
        all_low = join_halves(side % 2, low_mine, low_theirs)
        grad_query_weight = t_dot(both[:, width:], all_low)
        grad_query_bias = jnp.sum(all_low.astype(F32), axis=0)
        other = lax.ppermute(whole, "side", CORE_SWAP)
        first_core = side % 2 == 0
        grad_key_weight = jnp.where(first_core, whole, other).astype(F32)
        grad_value_weight = jnp.where(first_core, other, whole).astype(F32)

    return (
        loss.reshape(()),
        rows_out.reshape(hidden_in.shape),
        input_grad.reshape(hidden_in.shape),
        grad_query_weight,
        grad_query_bias.reshape(-1),
        grad_key_weight,
        grad_value_weight,
        small[6],
        grad_out_weight,
        small[5],
        small[3],
        small[4],
        grad_inner_weight,
        grad_inner_bias.reshape(-1),
        grad_outer_weight,
        small[2],
        small[0],
        small[1],
    )


def solution(mesh):
    rows = P("side", "batch", None, None)
    in_specs = (
        rows,
        P("side", "batch", None),
        P("batch", None),
        P("side", "batch", None),
        P("batch"),
        P(),
        P("batch", None),
    ) + (P(),) * 15
    out_specs = (P(), rows, rows) + (P(),) * 15
    return jax.shard_map(body, mesh=mesh, in_specs=in_specs, out_specs=out_specs, check_vma=False)
```

```python
import functools

import jax
import jax.numpy as jnp
import numpy as np
from jax import lax
from jax.experimental import pallas as pl
from jax.experimental.pallas import tpu as pltpu
from jax.sharding import PartitionSpec as P

HEADS = 8
HD = 64
EPSILON = 1e-05
NEG_FILL = -1e30
BF = jnp.bfloat16
F32 = jnp.float32
CORE_SWAP = [(0, 1), (1, 0), (2, 3), (3, 2)]
CHIP_SWAP = [(0, 2), (2, 0), (1, 3), (3, 1)]
MIB = 1 << 20
VM = pl.BlockSpec(memory_space=pltpu.VMEM)


def dot(left, right, precision=None):
    return jnp.dot(left, right, preferred_element_type=F32, precision=precision)


def dot_t(left, right):
    return lax.dot_general(left, right, (((1,), (1,)), ((), ())), preferred_element_type=F32)


def t_dot(left, right):
    return lax.dot_general(left, right, (((0,), (0,)), ((), ())), preferred_element_type=F32)


def iota(shape, axis):
    return lax.broadcasted_iota(jnp.int32, shape, axis)


def one_hot(rows, cols, row_of_col):
    return jnp.where(iota((rows, cols), 0) == row_of_col, 1.0, 0.0).astype(BF)


def norm_stats(summed):
    centre = jnp.mean(summed, axis=1, keepdims=True)
    deviation = summed - centre
    inverse = lax.rsqrt(jnp.mean(deviation * deviation, axis=1, keepdims=True) + EPSILON)
    return deviation * inverse, inverse


def norm_back(upstream, normed, inverse, gain):
    scaled = upstream * gain
    inner = jnp.mean(scaled, axis=1, keepdims=True)
    cross = jnp.mean(scaled * normed, axis=1, keepdims=True)
    return inverse * (scaled - inner - normed * cross)


def gelu(pre):
    return (0.5 * pre) * (1.0 + lax.erf(pre * (0.5**0.5)))


def gelu_parts(pre):
    phi = 0.5 + 0.5 * lax.erf(pre * (0.5**0.5))
    density = jnp.exp(-0.5 * (pre * pre)) * 0.3989422804014327
    return pre * phi, phi + pre * density


def spread_heads(rows):
    head = iota((1, rows.shape[1]), 1) // HD
    return jnp.concatenate(
        [jnp.where(head == h, rows, jnp.zeros_like(rows)) for h in range(HEADS)], axis=0
    )


def fold_heads(wide):
    count = wide.shape[0] // HEADS
    head = iota((1, wide.shape[1]), 1) // HD
    total = jnp.zeros((count, wide.shape[1]), wide.dtype)
    for h in range(HEADS):
        total = jnp.where(head == h, wide[h * count : (h + 1) * count], total)
    return total


class Fetched:
    def __init__(self, source, buffer, semaphores, axis=0, parts=1):
        self.buffer, self.shape = buffer, buffer.shape
        self.axis, self.size = axis, buffer.shape[axis] // parts
        self.waiting, self.copies = {}, []
        for i in range(parts):
            at = self.place(i) if parts > 1 else (Ellipsis,)
            self.copies.append(pltpu.make_async_copy(source.at[at], buffer.at[at], semaphores.at[i]))

    def start(self):
        if not self.waiting and self.copies:
            self.waiting = dict(enumerate(self.copies))
            self.copies = []
            for copy in self.waiting.values():
                copy.start()

    def place(self, i):
        return (slice(None),) * self.axis + (pl.ds(i * self.size, self.size),)

    def part(self, i):
        self.start()
        if i in self.waiting:
            self.waiting.pop(i).wait()
        return self.buffer[self.place(i)]

    def ref(self):
        self.start()
        for i in sorted(self.waiting):
            self.waiting.pop(i).wait()
        return self.buffer

    def __getitem__(self, index):
        return self.ref()[index]


def ref_of(x):
    return x.ref() if isinstance(x, Fetched) else x.buffer if isinstance(x, Result) else x


class Result:
    def __init__(self, buffer, target, semaphores):
        self.buffer, self.target, self.semaphores = buffer, target, semaphores
        self.shape, self.dtype, self.copies = buffer.shape, buffer.dtype, []

    def __setitem__(self, index, value):
        self.buffer[index] = value

    def __getitem__(self, index):
        return self.buffer[index]

    def flush(self, first=None, size=None):
        source, target = self.buffer, self.target
        if first is not None:
            source, target = source.at[pl.ds(first, size)], target.at[pl.ds(first, size)]
        copy = pltpu.make_async_copy(source, target, self.semaphores.at[len(self.copies)])
        copy.start()
        self.copies.append(copy)


PARTS = 4
SLABS_AT_ONCE = {384: 2, 512: 2, 768: 2}
TOKEN = ((8, 128), F32, False)


def call(kernel, outs, ins, flops=0, scratch=(), limit=8, far=(), smem=(), split=None, late=(), after=(), name=None):
    n_in, n_out, n_after = len(ins), len(outs), len(after)
    split = split or {}
    far_in = list(smem) + [i for i in far if i not in smem]
    far_out = [i for i in range(n_out) if not outs[i][2]]
    shapes = [(pltpu.VMEM if near else pltpu.HBM)(s, d) for s, d, near in list(outs) + [TOKEN]]
    moved = sum(x.size * x.dtype.itemsize for x in ins)
    moved += sum(int(np.prod(s)) * jnp.dtype(d).itemsize for s, d, _ in outs)
    ins = [pltpu.with_memory_space_constraint(x, pltpu.HBM) if i in far_in else x for i, x in enumerate(ins)]
    after = [pltpu.with_memory_space_constraint(x, pltpu.HBM) for x in after]

    def wrapped(*refs):
        refs = list(refs)
        in_refs, refs = refs[:n_in], refs[n_in + n_after :]
        out_refs, refs = refs[:n_out], refs[n_out + 1 :]
        in_bufs, refs = refs[: len(far_in)], refs[len(far_in) :]
        out_bufs, refs = refs[: len(far_out)], refs[len(far_out) :]
        if far_in:
            semaphores, refs = refs[0], refs[1:]
            for k, i in enumerate(far_in):
                in_refs[i] = Fetched(in_refs[i], in_bufs[k], semaphores.at[k], *split.get(i, ()))
                if i not in late:
                    in_refs[i].start()
        if far_out:
            semaphores, refs = refs[0], refs[1:]
            for k, i in enumerate(far_out):
                out_refs[i] = Result(out_bufs[k], out_refs[i], semaphores.at[k])
        kernel(*in_refs, *out_refs, *refs)
        for i in far_in:
            in_refs[i].ref()
        for i in far_out:
            if not out_refs[i].copies:
                out_refs[i].flush()
        for i in far_out:
            for copy in out_refs[i].copies:
                copy.wait()

    hbm = pl.BlockSpec(memory_space=pltpu.HBM)
    spaces = [hbm if i in far_in else VM for i in range(n_in)] + [hbm] * n_after
    out_spaces = [hbm if i in far_out else VM for i in range(n_out)] + [hbm]
    buffers = [(pltpu.SMEM if i in smem else pltpu.VMEM)(ins[i].shape, ins[i].dtype) for i in far_in]
    buffers += [pltpu.VMEM(outs[i][0], outs[i][1]) for i in far_out]
    if far_in:
        buffers.append(pltpu.SemaphoreType.DMA((len(far_in), PARTS)))
    if far_out:
        buffers.append(pltpu.SemaphoreType.DMA((len(far_out), PARTS)))
    return pl.pallas_call(
        wrapped,
        out_shape=shapes,
        in_specs=spaces,
        out_specs=out_spaces,
        scratch_shapes=buffers + list(scratch),
        compiler_params=pltpu.CompilerParams(vmem_limit_bytes=limit * MIB),
        cost_estimate=pl.CostEstimate(
            flops=int(flops), bytes_accessed=int(moved), transcendentals=0
        ),
        name=name,
    )(*ins, *after)


def behind(value, *tokens):
    tokens = [pltpu.with_memory_space_constraint(x, pltpu.HBM) for x in tokens]
    return pl.pallas_call(
        lambda *refs: None,
        out_shape=pltpu.VMEM(value.shape, value.dtype),
        in_specs=[VM] + [pl.BlockSpec(memory_space=pltpu.HBM)] * len(tokens),
        out_specs=VM,
        input_output_aliases={0: 0},
        compiler_params=pltpu.CompilerParams(vmem_limit_bytes=MIB),
        name="hand_on",
    )(value, *tokens)


class Rows:
    def __init__(self, batch_n, n_query, n_pass, pass_count):
        block = n_query + 3 * n_pass
        block += -block % 16
        self.batch_n, self.n_query, self.n_pass, self.block = batch_n, n_query, n_pass, block
        self.half = block // 2
        self.columns = pass_count + 1 + -(pass_count + 1) % 128
        self.count = batch_n * block
        self.queries = batch_n * n_query
        self.quarter = block // 4
        self.slot = self.quarter + -self.quarter % 16
        batch, place = np.meshgrid(np.arange(batch_n), np.arange(block), indexing="ij")
        group, slot = (place - n_query) // n_pass, (place - n_query) % n_pass
        order = self.queries + (group * batch_n + batch) * n_pass + slot
        order = np.where(place < n_query, batch * n_query + place, order)
        order = np.where(group < 3, order, self.queries + pass_count + batch)
        self.order = order
        self.code = np.empty(self.count, np.int32)
        self.code[order.reshape(-1)] = np.arange(self.count)

    def landed(self):
        halves = self.order.reshape(self.batch_n, 2, self.half).transpose(1, 0, 2)
        return halves.reshape(-1).astype(np.int32)

    def slots(self):
        quarters = self.order.reshape(self.batch_n, 2, 2, self.quarter).transpose(1, 2, 0, 3)
        none = np.full((2, 2, self.batch_n, self.slot - self.quarter), -1)
        return np.concatenate([quarters, none], axis=3).reshape(-1).astype(np.int32)


def core_chip():
    side = lax.axis_index("side")
    return side % 2, side // 2


def block_source(rows, at):
    core, chip = core_chip()
    n, p = rows.n_query, rows.n_pass
    begin = lambda c, y: jnp.where(y == chip, 0, 2 * n) + jnp.where(c == core, 0, n)
    source = jnp.where(at < n + 3 * p, begin(1, 1) + at - (n + 2 * p), -1)
    source = jnp.where(at < n + 2 * p, begin(0, 1) + at - (n + p), source)
    source = jnp.where(at < n + p, begin(1, 0) + at - n, source)
    return jnp.where(at < n, begin(0, 0) + at, source)


def take_rows(source, parts):
    total = sum(p.shape[0] for p in parts)
    pick = jnp.where(iota((source.shape[0], total), 1) == source, 1.0, 0.0).astype(BF)
    return dot(pick, jnp.concatenate([p[...] for p in parts], axis=0)).astype(BF)


def half_kernel(rows, own_ref, other_ref, far_ref, far_other_ref, *refs):
    core, chip = core_chip()
    n = rows.n_query
    at = iota((rows.half, 1), 0) + core * rows.half
    half = take_rows(block_source(rows, at), (own_ref, other_ref, far_ref, far_other_ref))
    out_ref = refs[-1]
    if len(refs) == 1:
        out_ref[...] = half
        return
    full = jnp.concatenate([half, refs[0][...]], axis=1)
    for b in range(rows.batch_n):
        out_ref[b] = full


def teacher_rows(rows, teacher_ref, pair_ref, out_ref):
    core, _ = core_chip()
    count, told = teacher_ref.shape
    line = iota((count, 1), 0)
    pair = jnp.zeros((count, 1), jnp.int32)
    for i in range(count):
        pair = jnp.where(line == i, pair_ref.ref()[i], pair)
    pair = jnp.broadcast_to(pair.astype(F32), (count, rows.columns - told))
    whole = jnp.concatenate([teacher_ref[...], pair], axis=1).astype(BF)
    place = iota((rows.half, 1), 0) + core * rows.half
    out_ref[...] = take_rows(jnp.where(place < count, place, -1), (whole,))


def near_rows(own, *tokens):
    other = lax.ppermute(own, "side", CORE_SWAP)
    far = lax.ppermute(own, "side", CHIP_SWAP)
    if tokens:
        far = behind(far, *tokens)
    return own, other, far, lax.ppermute(far, "side", CORE_SWAP)


def join_halves(core, mine, theirs):
    return jnp.concatenate(
        [jnp.where(core == 0, mine, theirs), jnp.where(core == 0, theirs, mine)], axis=0
    )


def softmax_of(scores, pick, seg_ref):
    seg = seg_ref[0].astype(F32)
    cls_seg = jnp.sum(jnp.where(pick, seg, 0.0), axis=1, keepdims=True)
    bias = jnp.where(cls_seg == seg, 0.0, NEG_FILL)
    scores = scores + jnp.concatenate([bias] * HEADS, axis=0)
    expo = jnp.exp(scores - jnp.max(scores, axis=1, keepdims=True))
    return expo / jnp.sum(expo, axis=1, keepdims=True)


def cls_forward_kernel(
    rows, with_teacher, x_ref, seg_ref, query_cls_ref, pass_cls_ref, wq_ref, bq_ref, wk_ref, wv_ref, bv_ref,
    teacher_ref, pair_ref, rows_ref, query_ref, pick_ref, told_ref, key_ref,
):
    n_pass = rows.n_pass
    side = lax.axis_index("side")
    n_query, width = query_ref.shape
    slot = iota((n_query, 1), 0)
    cls = jnp.full((n_query, 1), -1, jnp.int32)
    for i in range(n_query):
        first = query_cls_ref.ref()[0, i]
        place = jnp.where(side == 0, first, pass_cls_ref.ref()[0, 0, i] if i < n_pass else -1)
        cls = jnp.where(slot == i, place, cls)
    pick = iota((n_query, x_ref.shape[0]), 1) == cls
    pick_low = jnp.where(pick, 1.0, 0.0).astype(BF)
    pick_ref[...] = pick_low
    pick_ref.flush()
    if with_teacher:
        teacher_rows(rows, teacher_ref, pair_ref, told_ref)
    key_ref[...] = dot(x_ref[...], wk_ref[...]).astype(BF)
    key_ref.flush()
    tokens = dot(pick_low, x_ref[...]).astype(BF)
    query = (dot(tokens, wq_ref[...]) + bq_ref[...]).astype(BF)
    query_ref[...] = query
    query_ref.flush()
    rows_ref[:, width:] = tokens
    probs = softmax_of(dot_t(spread_heads(query) * BF(HD**-0.5), key_ref[...]), pick, seg_ref)
    mixed = dot(probs.astype(BF), x_ref[...])
    high = mixed.astype(BF)
    rest = (mixed - high.astype(F32)).astype(BF)
    context = fold_heads(dot(high, wv_ref[...]) + dot(rest, wv_ref[...])) + bv_ref[...]
    rows_ref[:, :width] = context.astype(BF)


def middle_kernel(
    rows, pass_count,
    mine_ref, theirs_ref, wo_ref, vector_ref, wi_ref, wu_ref, code_ref, landed_ref, value_ref, probs_ref, x_ref, key_ref, query_ref, cluster_ref,
    keep_ref, give_ref, low_ref, context_ref, gown_ref, scores_ref,
    loss_ref, small_ref, inner_bias_ref,
    both_ref, first_ref, active_ref, pre_ref, second_ref, attended_ref, slope_ref,
):
    width = wo_ref.shape[0]
    bo_ref, g1_ref, s1_ref, bu_ref, g2_ref, s2_ref, bi_ref = vectors_of(vector_ref, width)
    n_queries, n_columns = rows.queries, rows.columns
    chunk = wi_ref.shape[1] // PARTS
    side, batch = lax.axis_index("side"), lax.axis_index("batch")
    core = side % 2
    order = one_hot(rows.count, rows.count, landed_ref[...])
    placed = dot(order, join_halves(core, mine_ref[...], theirs_ref[...]))
    both_ref[...] = placed[:, : 2 * width].astype(BF)
    told = placed[: rows.queries, 2 * width :]
    attended = both_ref[:, width:].astype(F32) + (dot(both_ref[:, :width], wo_ref[...]) + bo_ref[...])
    first_hat, first_inv = norm_stats(attended)
    for ref in (value_ref, probs_ref, x_ref, key_ref, query_ref):
        ref.start()
    first = first_hat * g1_ref[...] + s1_ref[...]
    first_low = first.astype(BF)
    first_ref[...] = first_low
    second = first + bu_ref[...]
    for i in range(PARTS):
        c = i * chunk
        pre = dot(first_low, wi_ref[:, c : c + chunk]) + bi_ref[:, c : c + chunk]
        active, slope = gelu_parts(pre)
        active = active.astype(BF)
        active_ref[:, c : c + chunk] = active
        slope_ref[:, c : c + chunk] = slope
        second += dot(active, wu_ref[c : c + chunk, :])
    both_ref.flush()
    first_ref.flush()
    active_ref.flush()
    second_hat, second_inv = norm_stats(second)
    final = (second_hat * g2_ref[...] + s2_ref[...]).astype(BF)

    scale = width ** (-0.5)
    query_vec, pass_vec = final[:n_queries], final[n_queries:]
    score = dot_t(query_vec, pass_vec) * scale
    column = iota((n_queries, n_columns), 1)
    is_pair = column == told[:, n_columns - 1 :].astype(jnp.int32)
    none = jnp.full((1, n_columns - pass_count), -1.0, F32)
    cluster = jnp.concatenate([cluster_ref[...].astype(F32), none], axis=1)
    query_cluster = jnp.sum(jnp.where(is_pair, cluster, 0.0), axis=1, keepdims=True)
    counted = (cluster == query_cluster) & jnp.logical_not(is_pair) & (column < pass_count)
    pair_score = jnp.sum(jnp.where(is_pair, score, 0.0), axis=1, keepdims=True)
    resid = jnp.where(counted, pair_score - score - told, 0.0)
    squares = jnp.sum(jnp.sum(resid * resid, axis=1, keepdims=True), axis=0, keepdims=True)
    pairs = jnp.where(counted, 1.0, 0.0)
    pairs = jnp.sum(jnp.sum(pairs, axis=1, keepdims=True), axis=0, keepdims=True)
    loss_ref[...] = squares / jnp.maximum(pairs, 1.0)
    loss_ref.flush()
    grad_score = jnp.where(is_pair, jnp.sum(resid, axis=1, keepdims=True), 0.0) - resid
    grad_low = (grad_score * scale).astype(BF)
    grad_final = jnp.concatenate([dot(grad_low, pass_vec), t_dot(grad_low, query_vec)], axis=0)

    def note(at, value):
        small_ref[at : at + 1, :] = jnp.sum(value, axis=0, keepdims=True)

    grad_second = norm_back(grad_final, second_hat, second_inv, g2_ref[...])
    second_low = grad_second.astype(BF)
    second_ref[...] = second_low
    grad_first = grad_second
    for i in range(PARTS):
        c = i * chunk
        grad_pre = dot_t(second_low, wu_ref[c : c + chunk, :]) * slope_ref[:, c : c + chunk]
        inner_bias_ref[:, c : c + chunk] = jnp.sum(grad_pre, axis=0, keepdims=True)
        pre_low = grad_pre.astype(BF)
        pre_ref[:, c : c + chunk] = pre_low
        grad_first += dot_t(pre_low, wi_ref[:, c : c + chunk])
    inner_bias_ref.flush()
    pre_ref.flush()
    second_ref.flush()
    grad_attended = norm_back(grad_first, first_hat, first_inv, g1_ref[...])
    attended_low = grad_attended.astype(BF)
    attended_ref[...] = attended_low
    attended_ref.flush()
    grad_context = dot_t(attended_low, wo_ref[...]).astype(BF)
    note(0, grad_final * second_hat)
    note(1, grad_final)
    note(2, grad_second)
    note(3, grad_first * first_hat)
    note(4, grad_first)
    note(5, grad_attended)
    note(6, grad_context.astype(F32))
    small_ref[7:8, :] = jnp.zeros((1, width), F32)
    small_ref.flush()


    slot = iota((rows.n_query, 1), 0)
    base = batch * rows.block + jnp.where(side == 0, 0, rows.n_query + rows.n_pass * (side - 1))
    live = slot < jnp.where(side == 0, rows.n_query, rows.n_pass)
    own = (code_ref[...] == base + slot) & live
    high = grad_attended.astype(BF)
    rest = (grad_attended - high.astype(F32)).astype(BF)
    own = jnp.where(own, 1.0, 0.0).astype(BF)
    gown_ref[...] = dot(own, high) + dot(own, rest)
    gown_ref.flush()
    context = dot(own, grad_context).astype(BF)
    context_ref[...] = context
    context_ref.flush()
    wide = spread_heads(context)
    probs = probs_ref[...]
    grad_probs = dot_t(wide, value_ref[...])
    row_dot = jnp.sum(probs * grad_probs, axis=1, keepdims=True)
    grad_scores = (probs * (grad_probs - row_dot)).astype(BF)
    scores_ref[...] = grad_scores
    scores_ref.flush()
    query_wide = spread_heads(query_ref[...]) * BF(HD**-0.5)
    x = x_ref.ref()
    key_side = dot(grad_scores, x[...]).astype(BF)
    value_side = dot(probs.astype(BF), x[...]).astype(BF)
    key_part = t_dot(key_side, query_wide)
    value_part = t_dot(value_side, wide)
    keep_ref[...] = jnp.where(core == 0, key_part, value_part)
    give_ref[...] = jnp.where(core == 0, value_part, key_part).astype(BF)
    low_ref[...] = (fold_heads(dot(grad_scores, key_ref[...])) * HD**-0.5).astype(BF)


def input_grad_kernel(
    pick_ref, scores_ref, probs_ref, context_ref, query_ref, low_ref, gown_ref,
    wq_ref, wk_ref, wv_ref, out_ref,
):
    query_wide = spread_heads(query_ref[...]) * BF(HD**-0.5)
    key_low = t_dot(scores_ref[...], query_wide).astype(BF)
    value_low = t_dot(probs_ref[...].astype(BF), spread_heads(context_ref[...])).astype(BF)
    sparse = gown_ref[...] + dot_t(low_ref[...], wq_ref[...])
    high = sparse.astype(BF)
    rest = (sparse - high.astype(F32)).astype(BF)
    pick = pick_ref[...]
    total = dot_t(key_low, wk_ref[...]) + dot_t(value_low, wv_ref[...])
    total += t_dot(jnp.concatenate([pick, pick], axis=0), jnp.concatenate([high, rest], axis=0))
    out_ref[...] = total.astype(BF)


def chip_sum_kernel(keep_ref, got_ref, out_ref):
    out_ref[...] = (keep_ref[...] + got_ref[...].astype(F32)).astype(BF)


def add_parts_kernel(rows, parts_ref, own_ref, other_ref, far_ref, far_other_ref, out_ref):
    core, chip = core_chip()
    peers, size = parts_ref.shape[:2]
    total = parts_ref[0].astype(F32)
    for i in range(1, peers):
        total += parts_ref[i].astype(F32)
    at = iota((rows.slot, 1), 0)
    source = block_source(rows, core * rows.half + chip * rows.quarter + at)
    source = jnp.where(at < rows.quarter, source, -1)
    low = take_rows(source, (own_ref, other_ref, far_ref, far_other_ref))
    total = jnp.concatenate([total.astype(BF), low], axis=0)
    for i in range(peers):
        out_ref[i] = total


def last_kernel(size, mine_ref, theirs_ref, x_ref, key_ref, value_ref, query_ref, bias_ref):
    core, _ = core_chip()
    peers = mine_ref.shape[0]
    step = peers // PARTS
    for i in range(PARTS):
        for j in range(i * step, i * step + step):
            mine, theirs = mine_ref[j, :size].astype(F32), theirs_ref[j, :size].astype(F32)
            key_ref[j * size : j * size + size, :] = jnp.where(core == 0, mine, theirs)
            value_ref[j * size : j * size + size, :] = jnp.where(core == 0, theirs, mine)
        key_ref.flush(i * step * size, step * size)
        value_ref.flush(i * step * size, step * size)
    mine = jnp.concatenate([mine_ref[j, size:] for j in range(peers)], axis=0)
    theirs = jnp.concatenate([theirs_ref[j, size:] for j in range(peers)], axis=0)
    low = join_halves(core, mine, theirs)
    bias_ref[...] = jnp.sum(low.astype(F32), axis=0, keepdims=True)
    part_rows(query_ref, x_ref, low)


def core_groups(batch_n):
    return [[(y * 2 + c) * batch_n + b for y in range(2) for b in range(batch_n)] for c in range(2)]


def exchange(sent, batch_n):
    return lax.all_to_all(
        sent, ("side", "batch"), split_axis=0, concat_axis=0, axis_index_groups=core_groups(batch_n)
    )


def scatter_sum(keep, give, batch_n):
    got = lax.ppermute(give, "side", CORE_SWAP)
    total, token = call(chip_sum_kernel, [(keep.shape, BF, True)], (keep, got), name="chip_sum")
    return exchange(total.reshape(2 * batch_n, keep.shape[0] // (2 * batch_n), keep.shape[1]), batch_n), token


def part_rows(result, left, right):
    size = result.shape[0] // PARTS
    for i in range(PARTS):
        result[i * size : i * size + size, :] = t_dot(left[:, i * size : i * size + size], right)
        result.flush(i * size, size)


def weight_grads_kernel(
    active_ref, second_ref, first_ref, pre_ref, both_ref, attended_ref, slots_ref,
    outer_ref, inner_ref, out_ref, x_ref,
):
    part_rows(outer_ref, active_ref, second_ref[...])
    part_rows(inner_ref, first_ref, pre_ref[...])
    part_rows(out_ref, both_ref, attended_ref[...])
    width = out_ref.shape[0]
    count = both_ref.shape[0]
    pick = one_hot(count, slots_ref.shape[1], slots_ref[...])
    x_ref[...] = t_dot(pick, both_ref[:, width:]).astype(BF)


class Row:
    def __init__(self, source, at, width):
        self.source, self.at, self.width = source, at, width

    def __getitem__(self, index):
        first, last = 0, self.width
        if index is not Ellipsis:
            first, last = index[1].start, index[1].stop
        return self.source[self.at : self.at + 1, first:last]


def vectors_of(source, width):
    return [Row(source, i, width) for i in range(6)] + [Row(source, 6, source.shape[1])]


def column_of(row):
    return jnp.transpose(jnp.broadcast_to(row, (128, row.shape[1])))[:, :1]


def attention_kernel(
    tile, tiles, sizes, x_ref, wq_ref, bq_ref, key_ref, value_ref, seg_ref, out_ref, q_scr, bias_scr
):
    count = x_ref.shape[0]
    x, wq, bq, seg = ref_of(x_ref), ref_of(wq_ref), bq_ref[...], seg_ref[0]
    places = iota((1, count), 1)
    keys, values, seg_whole = ref_of(key_ref), ref_of(value_ref), ref_of(seg_ref)

    @pl.loop(*tiles)
    def _(i):
        row = pl.multiple_of(i * tile, tile)
        q = (dot(x[pl.ds(row, tile), :], wq[...]) + bq).astype(BF)
        q_scr[...] = q * BF(HD**-0.5)
        first = jnp.max(jnp.where(places == row, seg, -2))
        last = jnp.max(jnp.where(places == row + (tile - 1), seg, -2))
        low = jnp.min(jnp.where(seg == first, places, count)) // 128 * 128
        high = jnp.max(jnp.where(seg == last, places, -1)) + 1
        own = seg_whole[0, :, pl.ds(row, tile)].astype(F32)
        own = column_of(own)
        before = jnp.int32(0)
        for size in sizes:
            start = jnp.minimum(low, count - size)
            fits = (high - start <= size) if size < count else jnp.bool_(True)

            @pl.when(jnp.logical_and(before == 0, fits))
            def _(size=size, start=start):
                at = pl.multiple_of(start, 128)
                near = seg_whole[0, :, pl.ds(at, size)].astype(F32)
                bias_scr[:, :size] = jnp.where(own == near, 0.0, NEG_FILL)
                half = iota((1, 2 * HD), 1) // HD
                here = pl.ds(row - tiles[0] * tile, tile)

                def heads(first):
                    slabs = [pl.ds(first + k * 2 * HD, 2 * HD) for k in range(together)]
                    both = [(slab, h) for slab in slabs for h in range(2)]
                    scores = [
                        dot_t(jnp.where(half == h, q_scr[:, slab], BF(0)), keys[pl.ds(at, size), slab])
                        + bias_scr[:, :size]
                        for slab, h in both
                    ]
                    expos = [jnp.exp(s - jnp.max(s, axis=1, keepdims=True)).astype(BF) for s in scores]
                    outs = []
                    for (slab, h), expo in zip(both, expos):
                        mixed = dot(expo, jnp.where(half == h, values[pl.ds(at, size), slab], BF(1)))
                        outs.append(mixed / pltpu.roll(mixed, HD, 1))
                    for k, slab in enumerate(slabs):
                        out = jnp.where(half == 0, outs[2 * k], outs[2 * k + 1])
                        out_ref.buffer[here, slab] = out.astype(BF)

                together = SLABS_AT_ONCE.get(size, 1 if size > 512 else HEADS // 2)
                if together == HEADS // 2:
                    heads(0)
                else:

                    @pl.loop(0, HEADS // 2 // together)
                    def _(j):
                        heads(pl.multiple_of(j * (together * 2 * HD), together * 2 * HD))

            before = jnp.where(fits, 1, before)


def window_sizes(count):
    return [size for size in (384, 512, 768) if size < count] + [count]


def first_attention_kernel(
    tile, tiles, x_ref, key_ref, wv_ref, bv_ref, wq_ref, bq_ref, seg_ref, pick_ref, query_ref, *refs
):
    out_ref, value_ref, probs_ref, vector_ref, q_scr, bias_scr = refs[-6:]
    value_ref[...] = (dot(x_ref[...], wv_ref[...]) + bv_ref[...]).astype(BF)
    value_ref.flush()
    scores = dot_t(spread_heads(query_ref[...]) * BF(HD**-0.5), key_ref[...])
    probs_ref[...] = softmax_of(scores, pick_ref[...].astype(F32) > 0.5, seg_ref)
    probs_ref.flush()
    for i, ref in enumerate(refs[:-6]):
        vector_ref[i : i + 1, : ref.shape[1]] = ref[...]
    vector_ref.flush()
    sizes = window_sizes(x_ref.shape[0])
    attention_kernel(
        tile, tiles, sizes, x_ref, wq_ref, bq_ref, key_ref, value_ref, seg_ref, out_ref, q_scr, bias_scr
    )


def first_attention(x, keys, wv, bv, wq, bq, seg, pick, query, vectors, after, share, tile=256):
    t, d = x.shape
    return call(
        functools.partial(first_attention_kernel, tile, (0, share // tile)),
        [
            ((share, d), BF, False),
            ((t, d), BF, False),
            ((HEADS * query.shape[0], t), F32, False),
            ((8, vectors[-1].shape[1]), F32, False),
        ],
        (x, keys, wv, bv, wq, bq, seg, pick, query) + vectors,
        flops=6 * 10**9,
        far=range(9 + len(vectors)),
        scratch=[pltpu.VMEM((tile, d), BF), pltpu.VMEM((tile, t), F32)],
        limit=24,
        after=after,
        name="first_attention",
    )


def rest_attention(x, wq, bq, keys, values, seg, after, share, tile=256):
    t, d = x.shape
    return call(
        functools.partial(attention_kernel, tile, (share // tile, t // tile), window_sizes(t)),
        [((t - share, d), BF, False)],
        (x, wq, bq, keys, values, seg),
        flops=4 * 10**9,
        far=range(6),
        scratch=[pltpu.VMEM((tile, d), BF), pltpu.VMEM((tile, t), F32)],
        limit=20,
        after=after,
        name="rest_attention",
    )


def ffn_kernel(
    tile, x_ref, first_ref, rest_ref, wo_ref, vector_ref, wi_ref, wu_ref, out_ref,
):
    bo_ref, g1_ref, s1_ref, bu_ref, g2_ref, s2_ref, bi_ref = vectors_of(vector_ref, x_ref.shape[1])
    chunk = wi_ref.size
    for t in range(0, x_ref.shape[0], tile):
        part = slice(t, t + tile)
        share = first_ref.shape[0]
        near = first_ref[part, :] if t < share else rest_ref[t - share : t - share + tile, :]
        attended = x_ref[part, :].astype(F32) + (dot(near, wo_ref[...]) + bo_ref[...])
        first = norm_stats(attended)[0] * g1_ref[...] + s1_ref[...]
        first_low = first.astype(BF)
        second = first + bu_ref[...]
        for c in range(PARTS):
            pre = dot(first_low, wi_ref.part(c)) + bi_ref[:, c * chunk : c * chunk + chunk]
            second += dot(gelu(pre).astype(BF), wu_ref.part(c))
        out_ref[part, :] = (norm_stats(second)[0] * g2_ref[...] + s2_ref[...]).astype(BF)
        out_ref.flush(t, tile)


def ffn(x, context, weights, after, tile=512):
    return call(
        functools.partial(ffn_kernel, tile),
        [(x.shape, BF, False)],
        (x,) + context + weights,
        flops=6 * 10**9,
        far=range(7),
        limit=20,
        split={5: (1, PARTS), 6: (0, PARTS)},
        after=after,
        name="feed_forward",
    )


def middle_large(
    rows, pass_count, core, mine, theirs, told, cluster, wo, bo, g1, s1, wi, bi, wu, bu, g2, s2
):
    width = wo.shape[0]
    both = join_halves(core, mine, theirs)[np.argsort(rows.landed())]
    attended = both[:, width:].astype(F32) + (dot(both[:, :width], wo) + bo)
    first_hat, first_inv = norm_stats(attended)
    first = first_hat * g1 + s1
    first_low = first.astype(BF)
    active, slope = gelu_parts(dot(first_low, wi) + bi)
    active_low = active.astype(BF)
    second = first + (dot(active_low, wu) + bu)
    second_hat, second_inv = norm_stats(second)
    final = (second_hat * g2 + s2).astype(BF)
    query_vec, pass_vec = final[: rows.queries], final[rows.queries : rows.queries + pass_count]
    scale = width ** (-0.5)
    score = dot_t(query_vec, pass_vec) * scale
    is_pair = iota(score.shape, 1) == told[:, pass_count:].astype(jnp.int32)
    query_cluster = jnp.sum(jnp.where(is_pair, cluster, 0.0), axis=1, keepdims=True)
    counted = (cluster == query_cluster) & jnp.logical_not(is_pair)
    pair_score = jnp.sum(jnp.where(is_pair, score, 0.0), axis=1, keepdims=True)
    resid = jnp.where(counted, pair_score - score - told[:, :pass_count], 0.0)
    loss = jnp.sum(resid * resid) / jnp.maximum(jnp.sum(counted.astype(F32)), 1.0)
    grad_score = jnp.where(is_pair, jnp.sum(resid, axis=1, keepdims=True), 0.0) - resid
    grad_low = (grad_score * scale).astype(BF)
    none = jnp.zeros((rows.count - rows.queries - pass_count, width), F32)
    grad_final = jnp.concatenate([dot(grad_low, pass_vec), t_dot(grad_low, query_vec), none], axis=0)
    grad_second = norm_back(grad_final, second_hat, second_inv, g2)
    second_low = grad_second.astype(BF)
    grad_pre = dot_t(second_low, wu) * slope
    pre_low = grad_pre.astype(BF)
    grad_first = dot_t(pre_low, wi) + grad_second
    grad_attended = norm_back(grad_first, first_hat, first_inv, g1)
    attended_low = grad_attended.astype(BF)
    grad_context = dot_t(attended_low, wo).astype(BF)
    small = jnp.stack(
        [
            jnp.sum(v, axis=0)
            for v in (
                grad_final * second_hat, grad_final, grad_second, grad_first * first_hat,
                grad_first, grad_attended, grad_context.astype(F32),
            )
        ]
    )
    inner_bias = jnp.sum(grad_pre, axis=0, keepdims=True)
    return (
        loss.reshape(1, 1), grad_attended, grad_context, small, inner_bias,
        both, first_low, active_low, pre_low, second_low, attended_low,
    )


def own_large(rows, side, batch, grad_attended, grad_context, tokens, keys, values, cls_query, probs):
    core = side % 2
    slot = jnp.arange(rows.n_query)[:, None]
    base = batch * rows.block + jnp.where(side == 0, 0, rows.n_query + rows.n_pass * (side - 1))
    live = slot < jnp.where(side == 0, rows.n_query, rows.n_pass)
    own = ((rows.code[None, :] == base + slot) & live).astype(F32)
    own_attended = dot(own, grad_attended, lax.Precision.HIGHEST)
    context = dot(own.astype(BF), grad_context).astype(BF)
    wide = spread_heads(context)
    grad_probs = dot_t(wide, values)
    row_dot = jnp.sum(probs * grad_probs, axis=1, keepdims=True)
    grad_scores = (probs * (grad_probs - row_dot)).astype(BF)
    query_wide = spread_heads(cls_query) * BF(HD**-0.5)
    key_part = t_dot(dot(grad_scores, tokens).astype(BF), query_wide)
    value_part = t_dot(dot(probs.astype(BF), tokens).astype(BF), wide)
    keep = jnp.where(core == 0, key_part, value_part)
    give = jnp.where(core == 0, value_part, key_part).astype(BF)
    low = (fold_heads(dot(grad_scores, keys)) * HD**-0.5).astype(BF)
    return keep, give, low, context, own_attended, grad_scores


def fetch(arrays, behind_this):
    hbm = pl.BlockSpec(memory_space=pltpu.HBM)
    count = len(arrays)

    def kernel(*refs):
        semaphores = refs[-1]
        copies = [
            pltpu.make_async_copy(refs[i], refs[count + 1 + i], semaphores.at[i]) for i in range(count)
        ]
        for copy in copies:
            copy.start()
        for copy in copies:
            copy.wait()

    return pl.pallas_call(
        kernel,
        out_shape=[pltpu.VMEM(x.shape, x.dtype) for x in arrays],
        in_specs=[hbm] * count + [VM],
        out_specs=[VM] * count,
        scratch_shapes=[pltpu.SemaphoreType.DMA((count,))],
        compiler_params=pltpu.CompilerParams(vmem_limit_bytes=4 * MIB),
        name="fetch",
    )(*[pltpu.with_memory_space_constraint(x, pltpu.HBM) for x in arrays], behind_this)


def middle(rows, pass_count, mine, theirs, kept, weights, cluster, hidden, after):
    width, ff = weights[2].shape
    count = rows.count
    keys, values, cls_query, probs = kept
    landed = rows.landed()
    ins = (mine, theirs) + weights
    ins += (rows.code[None, :], landed[None, :], values, probs, hidden, keys, cls_query, cluster[None, :])
    outs = [
        ((width, width), F32, True), ((width, width), BF, True), ((rows.n_query, width), BF, True),
        ((rows.n_query, width), BF, False), ((rows.n_query, width), F32, False), (probs.shape, BF, False),
        ((1, 1), F32, False), ((8, width), F32, False), ((1, ff), F32, False),
        ((count, 2 * width), BF, False), ((count, width), BF, False), ((count, ff), BF, False),
        ((count, ff), BF, False), ((count, width), BF, False), ((count, width), BF, False),
    ]
    return call(
        functools.partial(middle_kernel, rows, pass_count),
        outs,
        ins,
        flops=12 * count * width * ff,
        scratch=[pltpu.VMEM((count, ff), F32)],
        far=(7, 6) + tuple(range(8, len(ins))),
        late=range(8, len(ins) - 1),
        limit=32,
        after=after,
        name="cls_middle",
    )


def body(
    hidden_in,
    segments,
    query_cls,
    passage_cls,
    pair_passage,
    passage_cluster,
    teacher,
    query_weight,
    query_bias,
    key_weight,
    value_weight,
    value_bias,
    out_weight,
    out_bias,
    first_gain,
    first_shift,
    inner_weight,
    inner_bias,
    outer_weight,
    outer_bias,
    second_gain,
    second_shift,
):
    count_tok = hidden_in.shape[2]
    width = hidden_in.shape[3]
    n_query = query_cls.shape[1]
    n_pass = passage_cls.shape[2]
    batch_n = lax.axis_size("batch")
    side = lax.axis_index("side")
    pass_count = teacher.shape[1]
    rows = Rows(batch_n, n_query, n_pass, pass_count)

    hidden = hidden_in.reshape(count_tok, width)

    def vec(v):
        return v.reshape(1, -1)

    weights = (
        out_weight, vec(out_bias), vec(first_gain), vec(first_shift), inner_weight, vec(inner_bias),
        outer_weight, vec(outer_bias), vec(second_gain), vec(second_shift),
    )
    small_case = rows.count <= 512 and rows.columns == 128 and count_tok % 512 == 0

    own, cls_query, pick, told, keys, _ = call(
        functools.partial(cls_forward_kernel, rows, small_case),
        [
            ((n_query, 2 * width), BF, True),
            ((n_query, width), BF, False),
            ((n_query, count_tok), BF, False),
            ((rows.half, rows.columns), BF, True),
            ((count_tok, width), BF, False),
        ],
        (
            hidden, segments, query_cls, passage_cls, query_weight, vec(query_bias), key_weight,
            value_weight, vec(value_bias), teacher, pair_passage,
        ),
        flops=2 * count_tok * width * width,
        far=(6, 0, 4, 1, 5, 9, 7, 8),
        smem=(2, 3, 10),
        limit=24,
        name="cls_forward",
    )

    near = near_rows(own)
    if small_case:
        sent, half_done = call(
            functools.partial(half_kernel, rows),
            [((batch_n, rows.half, 2 * width + rows.columns), BF, True)],
            near + (told,),
            name="half_rows",
        )
    else:
        half, half_done = call(
            functools.partial(half_kernel, rows),
            [((rows.half, 2 * width), BF, True)],
            near,
            name="half_rows",
        )
        sent = jnp.broadcast_to(half[None], (batch_n,) + half.shape)
    mine = lax.all_to_all(sent, "batch", split_axis=0, concat_axis=0)
    vectors = (weights[1], weights[2], weights[3], weights[7], weights[8], weights[9], weights[5])
    share = count_tok // 2
    first_context, values, probs, vectors, attention_done = first_attention(
        hidden, keys, value_weight, vec(value_bias), query_weight, vec(query_bias), segments, pick,
        cls_query, vectors, (half_done,), share,
    )
    matrices = (out_weight, vectors, inner_weight, outer_weight)
    if small_case:
        mine = behind(mine, attention_done)
    theirs = lax.ppermute(mine, "side", CORE_SWAP)

    if small_case:
        kept = (keys, values, cls_query, probs)
        flat = (batch_n * rows.half, mine.shape[2])
        (
            keep, give, query_low, own_context, own_attended, grad_scores, loss, small, grad_inner_bias,
            both, first_low, active_low, pre_low, second_low, attended_low, _,
        ) = middle(
            rows, pass_count, mine.reshape(flat), theirs.reshape(flat), kept, tuple(fetch(matrices, mine)),
            passage_cluster, hidden, (),
        )
    else:
        told = jnp.concatenate([teacher, pair_passage[:, None].astype(F32)], axis=1)
        told = lax.all_to_all(
            jnp.broadcast_to(told[None], (batch_n,) + told.shape), "batch", split_axis=0, concat_axis=0
        ).reshape(batch_n * n_query, pass_count + 1)
        flat = (batch_n * rows.half, 2 * width)
        (
            loss, grad_attended, grad_context, small, grad_inner_bias,
            both, first_low, active_low, pre_low, second_low, attended_low,
        ) = middle_large(
            rows, pass_count, side % 2, mine.reshape(flat), theirs.reshape(flat), told,
            passage_cluster.astype(F32)[None, :], *weights,
        )
        keep, give, query_low, own_context, own_attended, grad_scores = own_large(
            rows, side, lax.axis_index("batch"), grad_attended, grad_context,
            hidden, keys, values, cls_query, probs,
        )

    parts, sum_done = scatter_sum(keep, give, batch_n)
    input_grad, input_done = call(
        input_grad_kernel,
        [(hidden.shape, BF, False)],
        (
            pick, grad_scores, probs, own_context, cls_query, query_low, own_attended, query_weight,
            key_weight, value_weight,
        ),
        flops=6 * count_tok * width * width,
        far=(1, 4, 2, 3, 0, 6, 8, 9, 7),
        limit=20,
        after=(sum_done,),
        name="input_grad",
    )
    peers, size = parts.shape[:2]
    if small_case and size % 16 == 0:
        saved = (active_low, second_low, first_low, pre_low, both, attended_low, rows.slots()[None, :])
        grad_outer_weight, grad_inner_weight, grad_out_weight, all_tokens, weight_done = call(
            weight_grads_kernel,
            [
                (outer_weight.shape, F32, False),
                (inner_weight.shape, F32, False),
                (out_weight.shape, F32, False),
                ((4 * rows.batch_n * rows.slot, width), BF, False),
            ],
            saved,
            flops=2 * rows.count * width * (4 * width + width),
            far=range(7),
            limit=32,
            after=(sum_done,),
            name="weight_grads",
        )
        low = near_rows(query_low, weight_done)
        sent, add_done = call(
            functools.partial(add_parts_kernel, rows),
            [((peers, size + rows.slot, width), BF, True)],
            (parts,) + low,
            after=(input_done, weight_done),
            name="add_parts",
        )
        whole = exchange(sent, batch_n)
        rest_context, _ = rest_attention(
            hidden, query_weight, vec(query_bias), keys, values, segments, (add_done,), share
        )
        rows_out, ffn_done = ffn(hidden, (first_context, rest_context), matrices, (add_done,))
        whole = behind(whole, ffn_done)
        other = lax.ppermute(whole, "side", CORE_SWAP)
        grad_key_weight, grad_value_weight, grad_query_weight, grad_query_bias, _ = call(
            functools.partial(last_kernel, size),
            [((width, width), F32, False)] * 3 + [((1, width), F32, False)],
            (whole, other, all_tokens),
            far=(2,),
            limit=12,
            name="last_grads",
        )
    else:
        rest_context, _ = rest_attention(
            hidden, query_weight, vec(query_bias), keys, values, segments, (sum_done,), share
        )
        rows_out, _ = ffn(hidden, (first_context, rest_context), matrices, (sum_done,))
        part = jnp.sum(parts.astype(F32), axis=0).astype(BF)
        whole = exchange(jnp.broadcast_to(part[None], parts.shape), batch_n).reshape(width, width)
        grad_outer_weight = t_dot(active_low, second_low)
        grad_inner_weight = t_dot(first_low, pre_low)
        grad_out_weight = t_dot(both[:, :width], attended_low)
        half, _ = call(
            functools.partial(half_kernel, rows),
            [((rows.half, width), BF, True)],
            near_rows(query_low),
            name="low_rows",
        )
        flat = (batch_n * rows.half, width)
        half = jnp.broadcast_to(half[None], (batch_n,) + half.shape)
        low_mine = lax.all_to_all(half, "batch", split_axis=0, concat_axis=0).reshape(flat)
        low_theirs = lax.ppermute(low_mine, "side", CORE_SWAP)
        all_low = join_halves(side % 2, low_mine, low_theirs)[np.argsort(rows.landed())]
        grad_query_weight = t_dot(both[:, width:], all_low)
        grad_query_bias = jnp.sum(all_low.astype(F32), axis=0)
        other = lax.ppermute(whole, "side", CORE_SWAP)
        first_core = side % 2 == 0
        grad_key_weight = jnp.where(first_core, whole, other).astype(F32)
        grad_value_weight = jnp.where(first_core, other, whole).astype(F32)

    return (
        loss.reshape(()),
        rows_out.reshape(hidden_in.shape),
        input_grad.reshape(hidden_in.shape),
        grad_query_weight,
        grad_query_bias.reshape(-1),
        grad_key_weight,
        grad_value_weight,
        small[6],
        grad_out_weight,
        small[5],
        small[3],
        small[4],
        grad_inner_weight,
        grad_inner_bias.reshape(-1),
        grad_outer_weight,
        small[2],
        small[0],
        small[1],
    )


def solution(mesh):
    rows = P("side", "batch", None, None)
    in_specs = (
        rows,
        P("side", "batch", None),
        P("batch", None),
        P("side", "batch", None),
        P("batch"),
        P(),
        P("batch", None),
    ) + (P(),) * 15
    out_specs = (P(), rows, rows) + (P(),) * 15
    return jax.shard_map(body, mesh=mesh, in_specs=in_specs, out_specs=out_specs, check_vma=False)
```

```python
import functools

import jax
import jax.numpy as jnp
import numpy as np
from jax import lax
from jax.experimental import pallas as pl
from jax.experimental.pallas import tpu as pltpu
from jax.sharding import PartitionSpec as P

HEADS = 8
HD = 64
EPSILON = 1e-05
NEG_FILL = -1e30
BF = jnp.bfloat16
F32 = jnp.float32
CORE_SWAP = [(0, 1), (1, 0), (2, 3), (3, 2)]
CHIP_SWAP = [(0, 2), (2, 0), (1, 3), (3, 1)]
MIB = 1 << 20
VM = pl.BlockSpec(memory_space=pltpu.VMEM)


def dot(left, right, precision=None):
    return jnp.dot(left, right, preferred_element_type=F32, precision=precision)


def dot_t(left, right):
    return lax.dot_general(left, right, (((1,), (1,)), ((), ())), preferred_element_type=F32)


def t_dot(left, right):
    return lax.dot_general(left, right, (((0,), (0,)), ((), ())), preferred_element_type=F32)


def iota(shape, axis):
    return lax.broadcasted_iota(jnp.int32, shape, axis)


def one_hot(rows, cols, row_of_col):
    return jnp.where(iota((rows, cols), 0) == row_of_col, 1.0, 0.0).astype(BF)


def norm_stats(summed):
    centre = jnp.mean(summed, axis=1, keepdims=True)
    deviation = summed - centre
    inverse = lax.rsqrt(jnp.mean(deviation * deviation, axis=1, keepdims=True) + EPSILON)
    return deviation * inverse, inverse


def norm_back(upstream, normed, inverse, gain):
    scaled = upstream * gain
    inner = jnp.mean(scaled, axis=1, keepdims=True)
    cross = jnp.mean(scaled * normed, axis=1, keepdims=True)
    return inverse * (scaled - inner - normed * cross)


def gelu(pre):
    return (0.5 * pre) * (1.0 + lax.erf(pre * (0.5**0.5)))


def gelu_parts(pre):
    phi = 0.5 + 0.5 * lax.erf(pre * (0.5**0.5))
    density = jnp.exp(-0.5 * (pre * pre)) * 0.3989422804014327
    return pre * phi, phi + pre * density


def spread_heads(rows):
    head = iota((1, rows.shape[1]), 1) // HD
    return jnp.concatenate(
        [jnp.where(head == h, rows, jnp.zeros_like(rows)) for h in range(HEADS)], axis=0
    )


def fold_heads(wide):
    count = wide.shape[0] // HEADS
    head = iota((1, wide.shape[1]), 1) // HD
    total = jnp.zeros((count, wide.shape[1]), wide.dtype)
    for h in range(HEADS):
        total = jnp.where(head == h, wide[h * count : (h + 1) * count], total)
    return total


class Fetched:
    def __init__(self, source, buffer, semaphores, axis=0, parts=1):
        self.buffer, self.shape = buffer, buffer.shape
        self.axis, self.size = axis, buffer.shape[axis] // parts
        self.waiting, self.copies = {}, []
        for i in range(parts):
            at = self.place(i) if parts > 1 else (Ellipsis,)
            self.copies.append(pltpu.make_async_copy(source.at[at], buffer.at[at], semaphores.at[i]))

    def start(self):
        if not self.waiting and self.copies:
            self.waiting = dict(enumerate(self.copies))
            self.copies = []
            for copy in self.waiting.values():
                copy.start()

    def place(self, i):
        return (slice(None),) * self.axis + (pl.ds(i * self.size, self.size),)

    def part(self, i):
        self.start()
        if i in self.waiting:
            self.waiting.pop(i).wait()
        return self.buffer[self.place(i)]

    def ref(self):
        self.start()
        for i in sorted(self.waiting):
            self.waiting.pop(i).wait()
        return self.buffer

    def __getitem__(self, index):
        return self.ref()[index]


def ref_of(x):
    return x.ref() if isinstance(x, Fetched) else x.buffer if isinstance(x, Result) else x


class Result:
    def __init__(self, buffer, target, semaphores):
        self.buffer, self.target, self.semaphores = buffer, target, semaphores
        self.shape, self.dtype, self.copies = buffer.shape, buffer.dtype, []

    def __setitem__(self, index, value):
        self.buffer[index] = value

    def __getitem__(self, index):
        return self.buffer[index]

    def flush(self, first=None, size=None):
        source, target = self.buffer, self.target
        if first is not None:
            source, target = source.at[pl.ds(first, size)], target.at[pl.ds(first, size)]
        copy = pltpu.make_async_copy(source, target, self.semaphores.at[len(self.copies)])
        copy.start()
        self.copies.append(copy)


PARTS = 4
SLABS_AT_ONCE = {384: 2, 512: 2, 768: 2}
TOKEN = ((8, 128), F32, False)


def call(kernel, outs, ins, flops=0, scratch=(), limit=8, far=(), smem=(), split=None, late=(), after=(), name=None):
    n_in, n_out, n_after = len(ins), len(outs), len(after)
    split = split or {}
    far_in = list(smem) + [i for i in far if i not in smem]
    far_out = [i for i in range(n_out) if not outs[i][2]]
    shapes = [(pltpu.VMEM if near else pltpu.HBM)(s, d) for s, d, near in list(outs) + [TOKEN]]
    moved = sum(x.size * x.dtype.itemsize for x in ins)
    moved += sum(int(np.prod(s)) * jnp.dtype(d).itemsize for s, d, _ in outs)
    ins = [pltpu.with_memory_space_constraint(x, pltpu.HBM) if i in far_in else x for i, x in enumerate(ins)]
    after = [pltpu.with_memory_space_constraint(x, pltpu.HBM) for x in after]

    def wrapped(*refs):
        refs = list(refs)
        in_refs, refs = refs[:n_in], refs[n_in + n_after :]
        out_refs, refs = refs[:n_out], refs[n_out + 1 :]
        in_bufs, refs = refs[: len(far_in)], refs[len(far_in) :]
        out_bufs, refs = refs[: len(far_out)], refs[len(far_out) :]
        if far_in:
            semaphores, refs = refs[0], refs[1:]
            for k, i in enumerate(far_in):
                in_refs[i] = Fetched(in_refs[i], in_bufs[k], semaphores.at[k], *split.get(i, ()))
                if i not in late:
                    in_refs[i].start()
        if far_out:
            semaphores, refs = refs[0], refs[1:]
            for k, i in enumerate(far_out):
                out_refs[i] = Result(out_bufs[k], out_refs[i], semaphores.at[k])
        kernel(*in_refs, *out_refs, *refs)
        for i in far_in:
            in_refs[i].ref()
        for i in far_out:
            if not out_refs[i].copies:
                out_refs[i].flush()
        for i in far_out:
            for copy in out_refs[i].copies:
                copy.wait()

    hbm = pl.BlockSpec(memory_space=pltpu.HBM)
    spaces = [hbm if i in far_in else VM for i in range(n_in)] + [hbm] * n_after
    out_spaces = [hbm if i in far_out else VM for i in range(n_out)] + [hbm]
    buffers = [(pltpu.SMEM if i in smem else pltpu.VMEM)(ins[i].shape, ins[i].dtype) for i in far_in]
    buffers += [pltpu.VMEM(outs[i][0], outs[i][1]) for i in far_out]
    if far_in:
        buffers.append(pltpu.SemaphoreType.DMA((len(far_in), PARTS)))
    if far_out:
        buffers.append(pltpu.SemaphoreType.DMA((len(far_out), PARTS)))
    return pl.pallas_call(
        wrapped,
        out_shape=shapes,
        in_specs=spaces,
        out_specs=out_spaces,
        scratch_shapes=buffers + list(scratch),
        compiler_params=pltpu.CompilerParams(vmem_limit_bytes=limit * MIB),
        cost_estimate=pl.CostEstimate(
            flops=int(flops), bytes_accessed=int(moved), transcendentals=0
        ),
        name=name,
    )(*ins, *after)


def behind(value, *tokens):
    tokens = [pltpu.with_memory_space_constraint(x, pltpu.HBM) for x in tokens]
    return pl.pallas_call(
        lambda *refs: None,
        out_shape=pltpu.VMEM(value.shape, value.dtype),
        in_specs=[VM] + [pl.BlockSpec(memory_space=pltpu.HBM)] * len(tokens),
        out_specs=VM,
        input_output_aliases={0: 0},
        compiler_params=pltpu.CompilerParams(vmem_limit_bytes=MIB),
        name="hand_on",
    )(value, *tokens)


def exchange_order(batch_n, turn=0):
    order = []
    for x in range(2):
        run = [b for b in range(batch_n) if b % 2 == x][::-1]
        order += run[turn:] + run[:turn]
    return order


class Rows:
    def __init__(self, batch_n, n_query, n_pass, pass_count):
        block = n_query + 3 * n_pass
        block += -block % 16
        self.batch_n, self.n_query, self.n_pass, self.block = batch_n, n_query, n_pass, block
        self.half = block // 2
        self.columns = pass_count + 1 + -(pass_count + 1) % 128
        self.count = batch_n * block
        self.queries = batch_n * n_query
        self.quarter = block // 4
        self.slot = self.quarter + -self.quarter % 16
        batch, place = np.meshgrid(np.arange(batch_n), np.arange(block), indexing="ij")
        group, slot = (place - n_query) // n_pass, (place - n_query) % n_pass
        order = self.queries + (group * batch_n + batch) * n_pass + slot
        order = np.where(place < n_query, batch * n_query + place, order)
        order = np.where(group < 3, order, self.queries + pass_count + batch)
        self.order = order
        self.code = np.empty(self.count, np.int32)
        self.code[order.reshape(-1)] = np.arange(self.count)

    def landed(self, batches):
        halves = self.order.reshape(self.batch_n, 2, self.half).transpose(1, 0, 2)[:, batches]
        return halves.reshape(-1).astype(np.int32)

    def slots(self):
        quarters = self.order.reshape(self.batch_n, 2, 2, self.quarter).transpose(1, 2, 0, 3)
        quarters = quarters[:, :, exchange_order(self.batch_n)]
        none = np.full((2, 2, self.batch_n, self.slot - self.quarter), -1)
        return np.concatenate([quarters, none], axis=3).reshape(-1).astype(np.int32)


def core_chip():
    side = lax.axis_index("side")
    return side % 2, side // 2


def block_source(rows, at):
    core, chip = core_chip()
    n, p = rows.n_query, rows.n_pass
    begin = lambda c, y: jnp.where(y == chip, 0, 2 * n) + jnp.where(c == core, 0, n)
    source = jnp.where(at < n + 3 * p, begin(1, 1) + at - (n + 2 * p), -1)
    source = jnp.where(at < n + 2 * p, begin(0, 1) + at - (n + p), source)
    source = jnp.where(at < n + p, begin(1, 0) + at - n, source)
    return jnp.where(at < n, begin(0, 0) + at, source)


def take_rows(source, parts):
    total = sum(p.shape[0] for p in parts)
    pick = jnp.where(iota((source.shape[0], total), 1) == source, 1.0, 0.0).astype(BF)
    return dot(pick, jnp.concatenate([p[...] for p in parts], axis=0)).astype(BF)


def half_kernel(rows, own_ref, other_ref, far_ref, far_other_ref, *refs):
    core, chip = core_chip()
    n = rows.n_query
    at = iota((rows.half, 1), 0) + core * rows.half
    half = take_rows(block_source(rows, at), (own_ref, other_ref, far_ref, far_other_ref))
    out_ref = refs[-1]
    if len(refs) == 1:
        out_ref[...] = half
        return
    full = jnp.concatenate([half, refs[0][...]], axis=1)
    for b in range(rows.batch_n):
        out_ref[b] = full


def teacher_rows(rows, teacher_ref, pair_ref, out_ref):
    core, _ = core_chip()
    count, told = teacher_ref.shape
    line = iota((count, 1), 0)
    pair = jnp.zeros((count, 1), jnp.int32)
    for i in range(count):
        pair = jnp.where(line == i, pair_ref.ref()[i], pair)
    pair = jnp.broadcast_to(pair.astype(F32), (count, rows.columns - told))
    whole = jnp.concatenate([teacher_ref[...], pair], axis=1).astype(BF)
    place = iota((rows.half, 1), 0) + core * rows.half
    out_ref[...] = take_rows(jnp.where(place < count, place, -1), (whole,))


def near_rows(own, *tokens):
    other = lax.ppermute(own, "side", CORE_SWAP)
    far = lax.ppermute(own, "side", CHIP_SWAP)
    if tokens:
        far = behind(far, *tokens)
    return own, other, far, lax.ppermute(far, "side", CORE_SWAP)


def join_halves(core, mine, theirs):
    return jnp.concatenate(
        [jnp.where(core == 0, mine, theirs), jnp.where(core == 0, theirs, mine)], axis=0
    )


def softmax_of(scores, pick, seg_ref):
    seg = seg_ref[0].astype(F32)
    cls_seg = jnp.sum(jnp.where(pick, seg, 0.0), axis=1, keepdims=True)
    bias = jnp.where(cls_seg == seg, 0.0, NEG_FILL)
    scores = scores + jnp.concatenate([bias] * HEADS, axis=0)
    expo = jnp.exp(scores - jnp.max(scores, axis=1, keepdims=True))
    return expo / jnp.sum(expo, axis=1, keepdims=True)


def cls_forward_kernel(
    rows, with_teacher, x_ref, seg_ref, query_cls_ref, pass_cls_ref, wq_ref, bq_ref, wk_ref, wv_ref, bv_ref,
    teacher_ref, pair_ref, rows_ref, query_ref, pick_ref, told_ref, key_ref,
):
    n_pass = rows.n_pass
    side = lax.axis_index("side")
    n_query, width = query_ref.shape
    slot = iota((n_query, 1), 0)
    cls = jnp.full((n_query, 1), -1, jnp.int32)
    for i in range(n_query):
        first = query_cls_ref.ref()[0, i]
        place = jnp.where(side == 0, first, pass_cls_ref.ref()[0, 0, i] if i < n_pass else -1)
        cls = jnp.where(slot == i, place, cls)
    pick = iota((n_query, x_ref.shape[0]), 1) == cls
    pick_low = jnp.where(pick, 1.0, 0.0).astype(BF)
    pick_ref[...] = pick_low
    pick_ref.flush()
    if with_teacher:
        teacher_rows(rows, teacher_ref, pair_ref, told_ref)
    key_ref[...] = dot(x_ref[...], wk_ref[...]).astype(BF)
    key_ref.flush()
    tokens = dot(pick_low, x_ref[...]).astype(BF)
    query = (dot(tokens, wq_ref[...]) + bq_ref[...]).astype(BF)
    query_ref[...] = query
    query_ref.flush()
    rows_ref[:, width:] = tokens
    probs = softmax_of(dot_t(spread_heads(query) * BF(HD**-0.5), key_ref[...]), pick, seg_ref)
    mixed = dot(probs.astype(BF), x_ref[...])
    high = mixed.astype(BF)
    rest = (mixed - high.astype(F32)).astype(BF)
    context = fold_heads(dot(high, wv_ref[...]) + dot(rest, wv_ref[...])) + bv_ref[...]
    rows_ref[:, :width] = context.astype(BF)


def middle_kernel(
    rows, pass_count,
    mine_ref, theirs_ref, wo_ref, vector_ref, wi_ref, wu_ref, code_ref, landed_ref, value_ref, probs_ref, x_ref, key_ref, query_ref, cluster_ref,
    keep_ref, give_ref, low_ref, context_ref, gown_ref, scores_ref,
    loss_ref, small_ref, inner_bias_ref,
    both_ref, first_ref, active_ref, pre_ref, second_ref, attended_ref, slope_ref,
):
    width = wo_ref.shape[0]
    bo_ref, g1_ref, s1_ref, bu_ref, g2_ref, s2_ref, bi_ref = vectors_of(vector_ref, width)
    n_queries, n_columns = rows.queries, rows.columns
    chunk = wi_ref.shape[1] // PARTS
    side, batch = lax.axis_index("side"), lax.axis_index("batch")
    core = side % 2
    order = one_hot(rows.count, rows.count, landed_ref[...])
    placed = dot(order, join_halves(core, mine_ref[...], theirs_ref[...]))
    both_ref[...] = placed[:, : 2 * width].astype(BF)
    told = placed[: rows.queries, 2 * width :]
    attended = both_ref[:, width:].astype(F32) + (dot(both_ref[:, :width], wo_ref[...]) + bo_ref[...])
    first_hat, first_inv = norm_stats(attended)
    for ref in (value_ref, probs_ref, x_ref, key_ref, query_ref):
        ref.start()
    first = first_hat * g1_ref[...] + s1_ref[...]
    first_low = first.astype(BF)
    first_ref[...] = first_low
    second = first + bu_ref[...]
    for i in range(PARTS):
        c = i * chunk
        pre = dot(first_low, wi_ref[:, c : c + chunk]) + bi_ref[:, c : c + chunk]
        active, slope = gelu_parts(pre)
        active = active.astype(BF)
        active_ref[:, c : c + chunk] = active
        slope_ref[:, c : c + chunk] = slope
        second += dot(active, wu_ref[c : c + chunk, :])
    both_ref.flush()
    first_ref.flush()
    active_ref.flush()
    second_hat, second_inv = norm_stats(second)
    final = (second_hat * g2_ref[...] + s2_ref[...]).astype(BF)

    scale = width ** (-0.5)
    query_vec, pass_vec = final[:n_queries], final[n_queries:]
    score = dot_t(query_vec, pass_vec) * scale
    column = iota((n_queries, n_columns), 1)
    is_pair = column == told[:, n_columns - 1 :].astype(jnp.int32)
    none = jnp.full((1, n_columns - pass_count), -1.0, F32)
    cluster = jnp.concatenate([cluster_ref[...].astype(F32), none], axis=1)
    query_cluster = jnp.sum(jnp.where(is_pair, cluster, 0.0), axis=1, keepdims=True)
    counted = (cluster == query_cluster) & jnp.logical_not(is_pair) & (column < pass_count)
    pair_score = jnp.sum(jnp.where(is_pair, score, 0.0), axis=1, keepdims=True)
    resid = jnp.where(counted, pair_score - score - told, 0.0)
    squares = jnp.sum(jnp.sum(resid * resid, axis=1, keepdims=True), axis=0, keepdims=True)
    pairs = jnp.where(counted, 1.0, 0.0)
    pairs = jnp.sum(jnp.sum(pairs, axis=1, keepdims=True), axis=0, keepdims=True)
    loss_ref[...] = squares / jnp.maximum(pairs, 1.0)
    loss_ref.flush()
    grad_score = jnp.where(is_pair, jnp.sum(resid, axis=1, keepdims=True), 0.0) - resid
    grad_low = (grad_score * scale).astype(BF)
    grad_final = jnp.concatenate([dot(grad_low, pass_vec), t_dot(grad_low, query_vec)], axis=0)

    def note(at, value):
        small_ref[at : at + 1, :] = jnp.sum(value, axis=0, keepdims=True)

    grad_second = norm_back(grad_final, second_hat, second_inv, g2_ref[...])
    second_low = grad_second.astype(BF)
    second_ref[...] = second_low
    grad_first = grad_second
    for i in range(PARTS):
        c = i * chunk
        grad_pre = dot_t(second_low, wu_ref[c : c + chunk, :]) * slope_ref[:, c : c + chunk]
        inner_bias_ref[:, c : c + chunk] = jnp.sum(grad_pre, axis=0, keepdims=True)
        pre_low = grad_pre.astype(BF)
        pre_ref[:, c : c + chunk] = pre_low
        grad_first += dot_t(pre_low, wi_ref[:, c : c + chunk])
    inner_bias_ref.flush()
    pre_ref.flush()
    second_ref.flush()
    grad_attended = norm_back(grad_first, first_hat, first_inv, g1_ref[...])
    attended_low = grad_attended.astype(BF)
    attended_ref[...] = attended_low
    attended_ref.flush()
    grad_context = dot_t(attended_low, wo_ref[...]).astype(BF)
    note(0, grad_final * second_hat)
    note(1, grad_final)
    note(2, grad_second)
    note(3, grad_first * first_hat)
    note(4, grad_first)
    note(5, grad_attended)
    note(6, grad_context.astype(F32))
    small_ref[7:8, :] = jnp.zeros((1, width), F32)
    small_ref.flush()


    slot = iota((rows.n_query, 1), 0)
    base = batch * rows.block + jnp.where(side == 0, 0, rows.n_query + rows.n_pass * (side - 1))
    live = slot < jnp.where(side == 0, rows.n_query, rows.n_pass)
    own = (code_ref[...] == base + slot) & live
    high = grad_attended.astype(BF)
    rest = (grad_attended - high.astype(F32)).astype(BF)
    own = jnp.where(own, 1.0, 0.0).astype(BF)
    gown_ref[...] = dot(own, high) + dot(own, rest)
    gown_ref.flush()
    context = dot(own, grad_context).astype(BF)
    context_ref[...] = context
    context_ref.flush()
    wide = spread_heads(context)
    probs = probs_ref[...]
    grad_probs = dot_t(wide, value_ref[...])
    row_dot = jnp.sum(probs * grad_probs, axis=1, keepdims=True)
    grad_scores = (probs * (grad_probs - row_dot)).astype(BF)
    scores_ref[...] = grad_scores
    scores_ref.flush()
    query_wide = spread_heads(query_ref[...]) * BF(HD**-0.5)
    x = x_ref.ref()
    key_side = dot(grad_scores, x[...]).astype(BF)
    value_side = dot(probs.astype(BF), x[...]).astype(BF)
    key_part = t_dot(key_side, query_wide)
    value_part = t_dot(value_side, wide)
    keep_ref[...] = jnp.where(core == 0, key_part, value_part)
    give_ref[...] = jnp.where(core == 0, value_part, key_part).astype(BF)
    low_ref[...] = (fold_heads(dot(grad_scores, key_ref[...])) * HD**-0.5).astype(BF)


def grads_kernel(*refs):
    weights, inputs, outs = refs[:7], refs[7:17], refs[17:]
    weights[0].ref(), weights[1].ref()
    for ref in weights[2:] + inputs:
        if isinstance(ref, Fetched):
            ref.start()
    weight_grads_kernel(*weights, *outs[:4])
    input_grad_kernel(*inputs, outs[4])


def input_grad_kernel(
    pick_ref, scores_ref, probs_ref, context_ref, query_ref, low_ref, gown_ref,
    wq_ref, wk_ref, wv_ref, out_ref,
):
    query_wide = spread_heads(query_ref[...]) * BF(HD**-0.5)
    key_low = t_dot(scores_ref[...], query_wide).astype(BF)
    value_low = t_dot(probs_ref[...].astype(BF), spread_heads(context_ref[...])).astype(BF)
    sparse = gown_ref[...] + dot_t(low_ref[...], wq_ref[...])
    high = sparse.astype(BF)
    rest = (sparse - high.astype(F32)).astype(BF)
    pick = pick_ref[...]
    total = dot_t(key_low, wk_ref[...]) + dot_t(value_low, wv_ref[...])
    total += t_dot(jnp.concatenate([pick, pick], axis=0), jnp.concatenate([high, rest], axis=0))
    out_ref[...] = total.astype(BF)


def chip_sum_kernel(keep_ref, got_ref, out_ref):
    out_ref[...] = (keep_ref[...] + got_ref[...].astype(F32)).astype(BF)


def add_parts_kernel(rows, parts_ref, own_ref, other_ref, far_ref, far_other_ref, out_ref):
    core, chip = core_chip()
    peers, size = parts_ref.shape[:2]
    total = parts_ref[0].astype(F32)
    for i in range(1, peers):
        total += parts_ref[i].astype(F32)
    at = iota((rows.slot, 1), 0)
    source = block_source(rows, core * rows.half + chip * rows.quarter + at)
    source = jnp.where(at < rows.quarter, source, -1)
    low = take_rows(source, (own_ref, other_ref, far_ref, far_other_ref))
    total = jnp.concatenate([total.astype(BF), low], axis=0)
    for i in range(peers):
        out_ref[i] = total


def last_kernel(size, mine_ref, theirs_ref, x_ref, key_ref, value_ref, query_ref, bias_ref):
    core, _ = core_chip()
    peers = mine_ref.shape[0]
    step = peers // PARTS
    for i in range(PARTS):
        for j in range(i * step, i * step + step):
            mine, theirs = mine_ref[j, :size].astype(F32), theirs_ref[j, :size].astype(F32)
            key_ref[j * size : j * size + size, :] = jnp.where(core == 0, mine, theirs)
            value_ref[j * size : j * size + size, :] = jnp.where(core == 0, theirs, mine)
        key_ref.flush(i * step * size, step * size)
        value_ref.flush(i * step * size, step * size)
    mine = jnp.concatenate([mine_ref[j, size:] for j in range(peers)], axis=0)
    theirs = jnp.concatenate([theirs_ref[j, size:] for j in range(peers)], axis=0)
    low = join_halves(core, mine, theirs)
    bias_ref[...] = jnp.sum(low.astype(F32), axis=0, keepdims=True)
    part_rows(query_ref, x_ref, low)


def core_groups(batch_n):
    order = exchange_order(batch_n)
    return [[(y * 2 + c) * batch_n + b for y in range(2) for b in order] for c in range(2)]


def exchange(sent, batch_n):
    return lax.all_to_all(
        sent, ("side", "batch"), split_axis=0, concat_axis=0, axis_index_groups=core_groups(batch_n)
    )


def scatter_sum(keep, give, batch_n):
    got = lax.ppermute(give, "side", CORE_SWAP)
    total, token = call(chip_sum_kernel, [(keep.shape, BF, True)], (keep, got), name="chip_sum")
    return exchange(total.reshape(2 * batch_n, keep.shape[0] // (2 * batch_n), keep.shape[1]), batch_n), token


def part_rows(result, left, right):
    size = result.shape[0] // PARTS
    for i in range(PARTS):
        result[i * size : i * size + size, :] = t_dot(left[:, i * size : i * size + size], right)
        result.flush(i * size, size)


def weight_grads_kernel(
    active_ref, second_ref, first_ref, pre_ref, both_ref, attended_ref, slots_ref,
    outer_ref, inner_ref, out_ref, x_ref,
):
    part_rows(outer_ref, active_ref, second_ref[...])
    part_rows(inner_ref, first_ref, pre_ref[...])
    part_rows(out_ref, both_ref, attended_ref[...])
    width = out_ref.shape[0]
    count = both_ref.shape[0]
    pick = one_hot(count, slots_ref.shape[1], slots_ref[...])
    x_ref[...] = t_dot(pick, both_ref[:, width:]).astype(BF)


class Row:
    def __init__(self, source, at, width):
        self.source, self.at, self.width = source, at, width

    def __getitem__(self, index):
        first, last = 0, self.width
        if index is not Ellipsis:
            first, last = index[1].start, index[1].stop
        return self.source[self.at : self.at + 1, first:last]


def vectors_of(source, width):
    return [Row(source, i, width) for i in range(6)] + [Row(source, 6, source.shape[1])]


def column_of(row):
    return jnp.transpose(jnp.broadcast_to(row, (128, row.shape[1])))[:, :1]


def attention_kernel(
    tile, tiles, sizes, x_ref, wq_ref, bq_ref, key_ref, value_ref, seg_ref, out_ref, q_scr, bias_scr
):
    count = x_ref.shape[0]
    x, wq, bq, seg = ref_of(x_ref), ref_of(wq_ref), bq_ref[...], seg_ref[0]
    places = iota((1, count), 1)
    keys, values, seg_whole = ref_of(key_ref), ref_of(value_ref), ref_of(seg_ref)

    @pl.loop(*tiles)
    def _(i):
        row = pl.multiple_of(i * tile, tile)
        q = (dot(x[pl.ds(row, tile), :], wq[...]) + bq).astype(BF)
        q_scr[...] = q * BF(HD**-0.5)
        first = jnp.max(jnp.where(places == row, seg, -2))
        last = jnp.max(jnp.where(places == row + (tile - 1), seg, -2))
        low = jnp.min(jnp.where(seg == first, places, count)) // 128 * 128
        high = jnp.max(jnp.where(seg == last, places, -1)) + 1
        own = seg_whole[0, :, pl.ds(row, tile)].astype(F32)
        own = column_of(own)
        before = jnp.int32(0)
        for size in sizes:
            start = jnp.minimum(low, count - size)
            fits = (high - start <= size) if size < count else jnp.bool_(True)

            @pl.when(jnp.logical_and(before == 0, fits))
            def _(size=size, start=start):
                at = pl.multiple_of(start, 128)
                near = seg_whole[0, :, pl.ds(at, size)].astype(F32)
                bias_scr[:, :size] = jnp.where(own == near, 0.0, NEG_FILL)
                half = iota((1, 2 * HD), 1) // HD
                here = pl.ds(row - tiles[0] * tile, tile)

                def heads(first):
                    slabs = [pl.ds(first + k * 2 * HD, 2 * HD) for k in range(together)]
                    both = [(slab, h) for slab in slabs for h in range(2)]
                    scores = [
                        dot_t(jnp.where(half == h, q_scr[:, slab], BF(0)), keys[pl.ds(at, size), slab])
                        + bias_scr[:, :size]
                        for slab, h in both
                    ]
                    expos = [jnp.exp(s - jnp.max(s, axis=1, keepdims=True)).astype(BF) for s in scores]
                    outs = []
                    for (slab, h), expo in zip(both, expos):
                        mixed = dot(expo, jnp.where(half == h, values[pl.ds(at, size), slab], BF(1)))
                        outs.append(mixed / pltpu.roll(mixed, HD, 1))
                    for k, slab in enumerate(slabs):
                        out = jnp.where(half == 0, outs[2 * k], outs[2 * k + 1])
                        ref_of(out_ref)[here, slab] = out.astype(BF)

                together = SLABS_AT_ONCE.get(size, 1 if size > 512 else HEADS // 2)
                if together == HEADS // 2:
                    heads(0)
                else:

                    @pl.loop(0, HEADS // 2 // together)
                    def _(j):
                        heads(pl.multiple_of(j * (together * 2 * HD), together * 2 * HD))

            before = jnp.where(fits, 1, before)


def window_sizes(count):
    return [size for size in (384, 512, 768) if size < count] + [count]


def first_attention_kernel(
    tile, tiles, x_ref, key_ref, wv_ref, bv_ref, wq_ref, bq_ref, seg_ref, pick_ref, query_ref, *refs
):
    out_ref, value_ref, probs_ref, vector_ref, q_scr, bias_scr = refs[-6:]
    value_ref[...] = (dot(x_ref[...], wv_ref[...]) + bv_ref[...]).astype(BF)
    value_ref.flush()
    scores = dot_t(spread_heads(query_ref[...]) * BF(HD**-0.5), key_ref[...])
    probs_ref[...] = softmax_of(scores, pick_ref[...].astype(F32) > 0.5, seg_ref)
    probs_ref.flush()
    for i, ref in enumerate(refs[:-6]):
        vector_ref[i : i + 1, : ref.shape[1]] = ref[...]
    vector_ref.flush()
    sizes = window_sizes(x_ref.shape[0])
    attention_kernel(
        tile, tiles, sizes, x_ref, wq_ref, bq_ref, key_ref, value_ref, seg_ref, out_ref, q_scr, bias_scr
    )


def first_attention(x, keys, wv, bv, wq, bq, seg, pick, query, vectors, after, share, tile=256):
    t, d = x.shape
    return call(
        functools.partial(first_attention_kernel, tile, (0, share // tile)),
        [
            ((share, d), BF, False),
            ((t, d), BF, False),
            ((HEADS * query.shape[0], t), F32, False),
            ((8, vectors[-1].shape[1]), F32, False),
        ],
        (x, keys, wv, bv, wq, bq, seg, pick, query) + vectors,
        flops=6 * 10**9,
        far=range(9 + len(vectors)),
        scratch=[pltpu.VMEM((tile, d), BF), pltpu.VMEM((tile, t), F32)],
        limit=24,
        after=after,
        name="first_attention",
    )


def ffn_kernel(
    tile, x_ref, first_ref, rest_ref, wo_ref, vector_ref, wi_ref, wu_ref, out_ref,
):
    bo_ref, g1_ref, s1_ref, bu_ref, g2_ref, s2_ref, bi_ref = vectors_of(vector_ref, x_ref.shape[1])
    chunk = wi_ref.size
    for t in range(0, x_ref.shape[0], tile):
        part = slice(t, t + tile)
        share = first_ref.shape[0]
        near = first_ref[part, :] if t < share else rest_ref[t - share : t - share + tile, :]
        attended = x_ref[part, :].astype(F32) + (dot(near, wo_ref[...]) + bo_ref[...])
        first = norm_stats(attended)[0] * g1_ref[...] + s1_ref[...]
        first_low = first.astype(BF)
        second = first + bu_ref[...]
        for c in range(PARTS):
            pre = dot(first_low, wi_ref.part(c)) + bi_ref[:, c * chunk : c * chunk + chunk]
            second += dot(gelu(pre).astype(BF), wu_ref.part(c))
        out_ref[part, :] = (norm_stats(second)[0] * g2_ref[...] + s2_ref[...]).astype(BF)
        out_ref.flush(t, tile)


def dense_kernel(
    tile, tiles, x_ref, wq_ref, bq_ref, key_ref, value_ref, seg_ref, first_ref, wo_ref, vector_ref, wi_ref,
    wu_ref, out_ref, rest_ref, q_scr, bias_scr,
):
    for ref in (x_ref, wq_ref, bq_ref, key_ref, value_ref, seg_ref):
        ref.ref()
    for ref in (first_ref, wo_ref, vector_ref, wi_ref, wu_ref):
        ref.start()
    count = x_ref.shape[0]
    attention_kernel(
        tile, tiles, window_sizes(count), x_ref, wq_ref, bq_ref, key_ref, value_ref, seg_ref, rest_ref,
        q_scr, bias_scr,
    )
    ffn_kernel(512, x_ref, first_ref, rest_ref, wo_ref, vector_ref, wi_ref, wu_ref, out_ref)


def dense_rest(x, wq, bq, keys, values, seg, context, weights, after, tile=256):
    t, d = x.shape
    share = context.shape[0]
    return call(
        functools.partial(dense_kernel, tile, (share // tile, t // tile)),
        [(x.shape, BF, False)],
        (x, wq, bq, keys, values, seg, context) + weights,
        flops=8 * 10**9,
        far=(0, 1, 2, 5, 3, 4, 6, 7, 8, 9, 10),
        late=range(6, 11),
        split={9: (1, PARTS), 10: (0, PARTS)},
        scratch=[pltpu.VMEM((t - share, d), BF), pltpu.VMEM((tile, d), BF), pltpu.VMEM((tile, t), F32)],
        limit=40,
        after=after,
        name="dense_rest",
    )


def middle_large(
    rows, pass_count, core, mine, theirs, told, cluster, wo, bo, g1, s1, wi, bi, wu, bu, g2, s2
):
    width = wo.shape[0]
    both = join_halves(core, mine, theirs)[np.argsort(rows.landed(np.arange(rows.batch_n)))]
    attended = both[:, width:].astype(F32) + (dot(both[:, :width], wo) + bo)
    first_hat, first_inv = norm_stats(attended)
    first = first_hat * g1 + s1
    first_low = first.astype(BF)
    active, slope = gelu_parts(dot(first_low, wi) + bi)
    active_low = active.astype(BF)
    second = first + (dot(active_low, wu) + bu)
    second_hat, second_inv = norm_stats(second)
    final = (second_hat * g2 + s2).astype(BF)
    query_vec, pass_vec = final[: rows.queries], final[rows.queries : rows.queries + pass_count]
    scale = width ** (-0.5)
    score = dot_t(query_vec, pass_vec) * scale
    is_pair = iota(score.shape, 1) == told[:, pass_count:].astype(jnp.int32)
    query_cluster = jnp.sum(jnp.where(is_pair, cluster, 0.0), axis=1, keepdims=True)
    counted = (cluster == query_cluster) & jnp.logical_not(is_pair)
    pair_score = jnp.sum(jnp.where(is_pair, score, 0.0), axis=1, keepdims=True)
    resid = jnp.where(counted, pair_score - score - told[:, :pass_count], 0.0)
    loss = jnp.sum(resid * resid) / jnp.maximum(jnp.sum(counted.astype(F32)), 1.0)
    grad_score = jnp.where(is_pair, jnp.sum(resid, axis=1, keepdims=True), 0.0) - resid
    grad_low = (grad_score * scale).astype(BF)
    none = jnp.zeros((rows.count - rows.queries - pass_count, width), F32)
    grad_final = jnp.concatenate([dot(grad_low, pass_vec), t_dot(grad_low, query_vec), none], axis=0)
    grad_second = norm_back(grad_final, second_hat, second_inv, g2)
    second_low = grad_second.astype(BF)
    grad_pre = dot_t(second_low, wu) * slope
    pre_low = grad_pre.astype(BF)
    grad_first = dot_t(pre_low, wi) + grad_second
    grad_attended = norm_back(grad_first, first_hat, first_inv, g1)
    attended_low = grad_attended.astype(BF)
    grad_context = dot_t(attended_low, wo).astype(BF)
    small = jnp.stack(
        [
            jnp.sum(v, axis=0)
            for v in (
                grad_final * second_hat, grad_final, grad_second, grad_first * first_hat,
                grad_first, grad_attended, grad_context.astype(F32),
            )
        ]
    )
    inner_bias = jnp.sum(grad_pre, axis=0, keepdims=True)
    return (
        loss.reshape(1, 1), grad_attended, grad_context, small, inner_bias,
        both, first_low, active_low, pre_low, second_low, attended_low,
    )


def own_large(rows, side, batch, grad_attended, grad_context, tokens, keys, values, cls_query, probs):
    core = side % 2
    slot = jnp.arange(rows.n_query)[:, None]
    base = batch * rows.block + jnp.where(side == 0, 0, rows.n_query + rows.n_pass * (side - 1))
    live = slot < jnp.where(side == 0, rows.n_query, rows.n_pass)
    own = ((rows.code[None, :] == base + slot) & live).astype(F32)
    own_attended = dot(own, grad_attended, lax.Precision.HIGHEST)
    context = dot(own.astype(BF), grad_context).astype(BF)
    wide = spread_heads(context)
    grad_probs = dot_t(wide, values)
    row_dot = jnp.sum(probs * grad_probs, axis=1, keepdims=True)
    grad_scores = (probs * (grad_probs - row_dot)).astype(BF)
    query_wide = spread_heads(cls_query) * BF(HD**-0.5)
    key_part = t_dot(dot(grad_scores, tokens).astype(BF), query_wide)
    value_part = t_dot(dot(probs.astype(BF), tokens).astype(BF), wide)
    keep = jnp.where(core == 0, key_part, value_part)
    give = jnp.where(core == 0, value_part, key_part).astype(BF)
    low = (fold_heads(dot(grad_scores, keys)) * HD**-0.5).astype(BF)
    return keep, give, low, context, own_attended, grad_scores


def fetch(arrays, behind_this):
    hbm = pl.BlockSpec(memory_space=pltpu.HBM)
    count = len(arrays)

    def kernel(*refs):
        semaphores = refs[-1]
        copies = [
            pltpu.make_async_copy(refs[i], refs[count + 1 + i], semaphores.at[i]) for i in range(count)
        ]
        for copy in copies:
            copy.start()
        for copy in copies:
            copy.wait()

    return pl.pallas_call(
        kernel,
        out_shape=[pltpu.VMEM(x.shape, x.dtype) for x in arrays],
        in_specs=[hbm] * count + [VM],
        out_specs=[VM] * count,
        scratch_shapes=[pltpu.SemaphoreType.DMA((count,))],
        compiler_params=pltpu.CompilerParams(vmem_limit_bytes=4 * MIB),
        name="fetch",
    )(*[pltpu.with_memory_space_constraint(x, pltpu.HBM) for x in arrays], behind_this)


def middle(rows, pass_count, mine, theirs, kept, weights, cluster, hidden, after):
    width, ff = weights[2].shape
    count = rows.count
    keys, values, cls_query, probs = kept
    landed = rows.landed(exchange_order(rows.batch_n, 1))
    ins = (mine, theirs) + weights
    ins += (rows.code[None, :], landed[None, :], values, probs, hidden, keys, cls_query, cluster[None, :])
    outs = [
        ((width, width), F32, True), ((width, width), BF, True), ((rows.n_query, width), BF, True),
        ((rows.n_query, width), BF, False), ((rows.n_query, width), F32, False), (probs.shape, BF, False),
        ((1, 1), F32, False), ((8, width), F32, False), ((1, ff), F32, False),
        ((count, 2 * width), BF, False), ((count, width), BF, False), ((count, ff), BF, False),
        ((count, ff), BF, False), ((count, width), BF, False), ((count, width), BF, False),
    ]
    return call(
        functools.partial(middle_kernel, rows, pass_count),
        outs,
        ins,
        flops=12 * count * width * ff,
        scratch=[pltpu.VMEM((count, ff), F32)],
        far=(7, 6) + tuple(range(8, len(ins))),
        late=range(8, len(ins) - 1),
        limit=32,
        after=after,
        name="cls_middle",
    )


def body(
    hidden_in,
    segments,
    query_cls,
    passage_cls,
    pair_passage,
    passage_cluster,
    teacher,
    query_weight,
    query_bias,
    key_weight,
    value_weight,
    value_bias,
    out_weight,
    out_bias,
    first_gain,
    first_shift,
    inner_weight,
    inner_bias,
    outer_weight,
    outer_bias,
    second_gain,
    second_shift,
):
    count_tok = hidden_in.shape[2]
    width = hidden_in.shape[3]
    n_query = query_cls.shape[1]
    n_pass = passage_cls.shape[2]
    batch_n = lax.axis_size("batch")
    side = lax.axis_index("side")
    pass_count = teacher.shape[1]
    rows = Rows(batch_n, n_query, n_pass, pass_count)

    hidden = hidden_in.reshape(count_tok, width)

    def vec(v):
        return v.reshape(1, -1)

    weights = (
        out_weight, vec(out_bias), vec(first_gain), vec(first_shift), inner_weight, vec(inner_bias),
        outer_weight, vec(outer_bias), vec(second_gain), vec(second_shift),
    )
    small_case = rows.count <= 512 and rows.columns == 128 and count_tok % 512 == 0

    own, cls_query, pick, told, keys, _ = call(
        functools.partial(cls_forward_kernel, rows, small_case),
        [
            ((n_query, 2 * width), BF, True),
            ((n_query, width), BF, False),
            ((n_query, count_tok), BF, False),
            ((rows.half, rows.columns), BF, True),
            ((count_tok, width), BF, False),
        ],
        (
            hidden, segments, query_cls, passage_cls, query_weight, vec(query_bias), key_weight,
            value_weight, vec(value_bias), teacher, pair_passage,
        ),
        flops=2 * count_tok * width * width,
        far=(6, 0, 4, 1, 5, 9, 7, 8),
        smem=(2, 3, 10),
        limit=24,
        name="cls_forward",
    )

    near = near_rows(own)
    if small_case:
        sent, half_done = call(
            functools.partial(half_kernel, rows),
            [((batch_n, rows.half, 2 * width + rows.columns), BF, True)],
            near + (told,),
            name="half_rows",
        )
    else:
        half, half_done = call(
            functools.partial(half_kernel, rows),
            [((rows.half, 2 * width), BF, True)],
            near,
            name="half_rows",
        )
        sent = jnp.broadcast_to(half[None], (batch_n,) + half.shape)
    batches = exchange_order(batch_n, 1)
    mine = lax.all_to_all(
        sent, "batch", split_axis=0, concat_axis=0, axis_index_groups=[batches] if small_case else None
    )
    vectors = (weights[1], weights[2], weights[3], weights[7], weights[8], weights[9], weights[5])
    share = count_tok // 2
    first_context, values, probs, vectors, attention_done = first_attention(
        hidden, keys, value_weight, vec(value_bias), query_weight, vec(query_bias), segments, pick,
        cls_query, vectors, (half_done,), share,
    )
    matrices = (out_weight, vectors, inner_weight, outer_weight)
    if small_case:
        mine = behind(mine, attention_done)
    theirs = lax.ppermute(mine, "side", CORE_SWAP)

    if small_case:
        kept = (keys, values, cls_query, probs)
        flat = (batch_n * rows.half, mine.shape[2])
        (
            keep, give, query_low, own_context, own_attended, grad_scores, loss, small, grad_inner_bias,
            both, first_low, active_low, pre_low, second_low, attended_low, _,
        ) = middle(
            rows, pass_count, mine.reshape(flat), theirs.reshape(flat), kept, tuple(fetch(matrices, mine)),
            passage_cluster, hidden, (),
        )
    else:
        told = jnp.concatenate([teacher, pair_passage[:, None].astype(F32)], axis=1)
        told = lax.all_to_all(
            jnp.broadcast_to(told[None], (batch_n,) + told.shape), "batch", split_axis=0, concat_axis=0
        ).reshape(batch_n * n_query, pass_count + 1)
        flat = (batch_n * rows.half, 2 * width)
        (
            loss, grad_attended, grad_context, small, grad_inner_bias,
            both, first_low, active_low, pre_low, second_low, attended_low,
        ) = middle_large(
            rows, pass_count, side % 2, mine.reshape(flat), theirs.reshape(flat), told,
            passage_cluster.astype(F32)[None, :], *weights,
        )
        keep, give, query_low, own_context, own_attended, grad_scores = own_large(
            rows, side, lax.axis_index("batch"), grad_attended, grad_context,
            hidden, keys, values, cls_query, probs,
        )

    parts, sum_done = scatter_sum(keep, give, batch_n)
    peers, size = parts.shape[:2]
    for_input = (
        pick, grad_scores, probs, own_context, cls_query, query_low, own_attended, query_weight, key_weight,
        value_weight,
    )
    if small_case and size % 16 == 0:
        saved = (active_low, second_low, first_low, pre_low, both, attended_low, rows.slots()[None, :])
        grad_outer_weight, grad_inner_weight, grad_out_weight, all_tokens, input_grad, weight_done = call(
            grads_kernel,
            [
                (outer_weight.shape, F32, False),
                (inner_weight.shape, F32, False),
                (out_weight.shape, F32, False),
                ((4 * rows.batch_n * rows.slot, width), BF, False),
                (hidden.shape, BF, False),
            ],
            saved + for_input,
            flops=2 * rows.count * width * (4 * width + width) + 6 * count_tok * width * width,
            far=tuple(i for i in range(17) if i != 12),
            late=range(2, 17),
            limit=40,
            after=(sum_done,),
            name="grads",
        )
        low = near_rows(query_low, weight_done)
        sent, add_done = call(
            functools.partial(add_parts_kernel, rows),
            [((peers, size + rows.slot, width), BF, True)],
            (parts,) + low,
            after=(weight_done,),
            name="add_parts",
        )
        whole = exchange(sent, batch_n)
        rows_out, dense_done = dense_rest(
            hidden, query_weight, vec(query_bias), keys, values, segments, first_context, matrices,
            (add_done,),
        )
        whole = behind(whole, dense_done)
        other = lax.ppermute(whole, "side", CORE_SWAP)
        grad_key_weight, grad_value_weight, grad_query_weight, grad_query_bias, _ = call(
            functools.partial(last_kernel, size),
            [((width, width), F32, False)] * 3 + [((1, width), F32, False)],
            (whole, other, all_tokens),
            far=(2,),
            limit=12,
            name="last_grads",
        )
    else:
        input_grad, _ = call(
            input_grad_kernel,
            [(hidden.shape, BF, False)],
            for_input,
            far=(1, 4, 2, 3, 0, 6, 8, 9, 7),
            limit=20,
            after=(sum_done,),
            name="input_grad",
        )
        rows_out, _ = dense_rest(
            hidden, query_weight, vec(query_bias), keys, values, segments, first_context, matrices,
            (sum_done,),
        )
        part = jnp.sum(parts.astype(F32), axis=0).astype(BF)
        whole = exchange(jnp.broadcast_to(part[None], parts.shape), batch_n).reshape(width, width)
        grad_outer_weight = t_dot(active_low, second_low)
        grad_inner_weight = t_dot(first_low, pre_low)
        grad_out_weight = t_dot(both[:, :width], attended_low)
        half, _ = call(
            functools.partial(half_kernel, rows),
            [((rows.half, width), BF, True)],
            near_rows(query_low),
            name="low_rows",
        )
        flat = (batch_n * rows.half, width)
        half = jnp.broadcast_to(half[None], (batch_n,) + half.shape)
        low_mine = lax.all_to_all(half, "batch", split_axis=0, concat_axis=0).reshape(flat)
        low_theirs = lax.ppermute(low_mine, "side", CORE_SWAP)
        all_low = join_halves(side % 2, low_mine, low_theirs)[np.argsort(rows.landed(np.arange(rows.batch_n)))]
        grad_query_weight = t_dot(both[:, width:], all_low)
        grad_query_bias = jnp.sum(all_low.astype(F32), axis=0)
        other = lax.ppermute(whole, "side", CORE_SWAP)
        first_core = side % 2 == 0
        grad_key_weight = jnp.where(first_core, whole, other).astype(F32)
        grad_value_weight = jnp.where(first_core, other, whole).astype(F32)

    return (
        loss.reshape(()),
        rows_out.reshape(hidden_in.shape),
        input_grad.reshape(hidden_in.shape),
        grad_query_weight,
        grad_query_bias.reshape(-1),
        grad_key_weight,
        grad_value_weight,
        small[6],
        grad_out_weight,
        small[5],
        small[3],
        small[4],
        grad_inner_weight,
        grad_inner_bias.reshape(-1),
        grad_outer_weight,
        small[2],
        small[0],
        small[1],
    )


def solution(mesh):
    rows = P("side", "batch", None, None)
    in_specs = (
        rows,
        P("side", "batch", None),
        P("batch", None),
        P("side", "batch", None),
        P("batch"),
        P(),
        P("batch", None),
    ) + (P(),) * 15
    out_specs = (P(), rows, rows) + (P(),) * 15
    return jax.shard_map(body, mesh=mesh, in_specs=in_specs, out_specs=out_specs, check_vma=False)
```

```python
import functools

import jax
import jax.numpy as jnp
import numpy as np
from jax import lax
from jax.experimental import pallas as pl
from jax.experimental.pallas import tpu as pltpu
from jax.sharding import PartitionSpec as P

HEADS = 8
HD = 64
EPSILON = 1e-05
NEG_FILL = -1e30
BF = jnp.bfloat16
F32 = jnp.float32
CORE_SWAP = [(0, 1), (1, 0), (2, 3), (3, 2)]
CHIP_SWAP = [(0, 2), (2, 0), (1, 3), (3, 1)]
MIB = 1 << 20
VM = pl.BlockSpec(memory_space=pltpu.VMEM)


def dot(left, right, precision=None):
    return jnp.dot(left, right, preferred_element_type=F32, precision=precision)


def dot_t(left, right):
    return lax.dot_general(left, right, (((1,), (1,)), ((), ())), preferred_element_type=F32)


def t_dot(left, right):
    return lax.dot_general(left, right, (((0,), (0,)), ((), ())), preferred_element_type=F32)


def iota(shape, axis):
    return lax.broadcasted_iota(jnp.int32, shape, axis)


def one_hot(rows, cols, row_of_col):
    return jnp.where(iota((rows, cols), 0) == row_of_col, 1.0, 0.0).astype(BF)


def norm_stats(summed):
    centre = jnp.mean(summed, axis=1, keepdims=True)
    deviation = summed - centre
    inverse = lax.rsqrt(jnp.mean(deviation * deviation, axis=1, keepdims=True) + EPSILON)
    return deviation * inverse, inverse


def norm_back(upstream, normed, inverse, gain):
    scaled = upstream * gain
    inner = jnp.mean(scaled, axis=1, keepdims=True)
    cross = jnp.mean(scaled * normed, axis=1, keepdims=True)
    return inverse * (scaled - inner - normed * cross)


def gelu(pre):
    return (0.5 * pre) * (1.0 + lax.erf(pre * (0.5**0.5)))


def gelu_parts(pre):
    phi = 0.5 + 0.5 * lax.erf(pre * (0.5**0.5))
    density = jnp.exp(-0.5 * (pre * pre)) * 0.3989422804014327
    return pre * phi, phi + pre * density


def spread_heads(rows):
    head = iota((1, rows.shape[1]), 1) // HD
    return jnp.concatenate(
        [jnp.where(head == h, rows, jnp.zeros_like(rows)) for h in range(HEADS)], axis=0
    )


def fold_heads(wide):
    count = wide.shape[0] // HEADS
    head = iota((1, wide.shape[1]), 1) // HD
    total = jnp.zeros((count, wide.shape[1]), wide.dtype)
    for h in range(HEADS):
        total = jnp.where(head == h, wide[h * count : (h + 1) * count], total)
    return total


class Fetched:
    def __init__(self, source, buffer, semaphores, axis=0, parts=1):
        self.buffer, self.shape = buffer, buffer.shape
        self.axis, self.size = axis, buffer.shape[axis] // parts
        self.waiting, self.copies = {}, []
        for i in range(parts):
            at = self.place(i) if parts > 1 else (Ellipsis,)
            self.copies.append(pltpu.make_async_copy(source.at[at], buffer.at[at], semaphores.at[i]))

    def start(self):
        if not self.waiting and self.copies:
            self.waiting = dict(enumerate(self.copies))
            self.copies = []
            for copy in self.waiting.values():
                copy.start()

    def place(self, i):
        return (slice(None),) * self.axis + (pl.ds(i * self.size, self.size),)

    def part(self, i):
        self.start()
        if i in self.waiting:
            self.waiting.pop(i).wait()
        return self.buffer[self.place(i)]

    def ref(self):
        self.start()
        for i in sorted(self.waiting):
            self.waiting.pop(i).wait()
        return self.buffer

    def __getitem__(self, index):
        return self.ref()[index]


def ref_of(x):
    return x.ref() if isinstance(x, Fetched) else x.buffer if isinstance(x, Result) else x


class Result:
    def __init__(self, buffer, target, semaphores):
        self.buffer, self.target, self.semaphores = buffer, target, semaphores
        self.shape, self.dtype, self.copies = buffer.shape, buffer.dtype, []

    def __setitem__(self, index, value):
        self.buffer[index] = value

    def __getitem__(self, index):
        return self.buffer[index]

    def flush(self, first=None, size=None):
        source, target = self.buffer, self.target
        if first is not None:
            source, target = source.at[pl.ds(first, size)], target.at[pl.ds(first, size)]
        copy = pltpu.make_async_copy(source, target, self.semaphores.at[len(self.copies)])
        copy.start()
        self.copies.append(copy)


PARTS = 4
SLABS_AT_ONCE = {384: 2, 512: 2, 768: 2}
TOKEN = ((8, 128), F32, False)


def call(kernel, outs, ins, flops=0, scratch=(), limit=8, far=(), smem=(), split=None, late=(), after=(), name=None):
    n_in, n_out, n_after = len(ins), len(outs), len(after)
    split = split or {}
    far_in = list(smem) + [i for i in far if i not in smem]
    far_out = [i for i in range(n_out) if not outs[i][2]]
    shapes = [(pltpu.VMEM if near else pltpu.HBM)(s, d) for s, d, near in list(outs) + [TOKEN]]
    moved = sum(x.size * x.dtype.itemsize for x in ins)
    moved += sum(int(np.prod(s)) * jnp.dtype(d).itemsize for s, d, _ in outs)
    ins = [pltpu.with_memory_space_constraint(x, pltpu.HBM) if i in far_in else x for i, x in enumerate(ins)]
    after = [pltpu.with_memory_space_constraint(x, pltpu.HBM) for x in after]

    def wrapped(*refs):
        refs = list(refs)
        in_refs, refs = refs[:n_in], refs[n_in + n_after :]
        out_refs, refs = refs[:n_out], refs[n_out + 1 :]
        in_bufs, refs = refs[: len(far_in)], refs[len(far_in) :]
        out_bufs, refs = refs[: len(far_out)], refs[len(far_out) :]
        if far_in:
            semaphores, refs = refs[0], refs[1:]
            for k, i in enumerate(far_in):
                in_refs[i] = Fetched(in_refs[i], in_bufs[k], semaphores.at[k], *split.get(i, ()))
                if i not in late:
                    in_refs[i].start()
        if far_out:
            semaphores, refs = refs[0], refs[1:]
            for k, i in enumerate(far_out):
                out_refs[i] = Result(out_bufs[k], out_refs[i], semaphores.at[k])
        kernel(*in_refs, *out_refs, *refs)
        for i in far_in:
            in_refs[i].ref()
        for i in far_out:
            if not out_refs[i].copies:
                out_refs[i].flush()
        for i in far_out:
            for copy in out_refs[i].copies:
                copy.wait()

    hbm = pl.BlockSpec(memory_space=pltpu.HBM)
    spaces = [hbm if i in far_in else VM for i in range(n_in)] + [hbm] * n_after
    out_spaces = [hbm if i in far_out else VM for i in range(n_out)] + [hbm]
    buffers = [(pltpu.SMEM if i in smem else pltpu.VMEM)(ins[i].shape, ins[i].dtype) for i in far_in]
    buffers += [pltpu.VMEM(outs[i][0], outs[i][1]) for i in far_out]
    if far_in:
        buffers.append(pltpu.SemaphoreType.DMA((len(far_in), PARTS)))
    if far_out:
        buffers.append(pltpu.SemaphoreType.DMA((len(far_out), PARTS)))
    return pl.pallas_call(
        wrapped,
        out_shape=shapes,
        in_specs=spaces,
        out_specs=out_spaces,
        scratch_shapes=buffers + list(scratch),
        compiler_params=pltpu.CompilerParams(vmem_limit_bytes=limit * MIB),
        cost_estimate=pl.CostEstimate(
            flops=int(flops), bytes_accessed=int(moved), transcendentals=0
        ),
        name=name,
    )(*ins, *after)


def behind(value, *tokens):
    tokens = [pltpu.with_memory_space_constraint(x, pltpu.HBM) for x in tokens]
    return pl.pallas_call(
        lambda *refs: None,
        out_shape=pltpu.VMEM(value.shape, value.dtype),
        in_specs=[VM] + [pl.BlockSpec(memory_space=pltpu.HBM)] * len(tokens),
        out_specs=VM,
        input_output_aliases={0: 0},
        compiler_params=pltpu.CompilerParams(vmem_limit_bytes=MIB),
        name="hand_on",
    )(value, *tokens)


def exchange_order(batch_n):
    order = []
    for x in range(2):
        run = [b for b in range(batch_n) if b % 2 == x][::-1]
        order += run[1:] + run[:1]
    return order


class Rows:
    def __init__(self, batch_n, n_query, n_pass, pass_count):
        block = n_query + 3 * n_pass
        block += -block % 16
        self.batch_n, self.n_query, self.n_pass, self.block = batch_n, n_query, n_pass, block
        self.half = block // 2
        self.columns = pass_count + 1 + -(pass_count + 1) % 128
        self.count = batch_n * block
        self.queries = batch_n * n_query
        self.quarter = block // 4
        self.slot = self.quarter + -self.quarter % 16
        batch, place = np.meshgrid(np.arange(batch_n), np.arange(block), indexing="ij")
        group, slot = (place - n_query) // n_pass, (place - n_query) % n_pass
        order = self.queries + (group * batch_n + batch) * n_pass + slot
        order = np.where(place < n_query, batch * n_query + place, order)
        order = np.where(group < 3, order, self.queries + pass_count + batch)
        self.order = order
        self.code = np.empty(self.count, np.int32)
        self.code[order.reshape(-1)] = np.arange(self.count)

    def landed(self, batches):
        halves = self.order.reshape(self.batch_n, 2, self.half).transpose(1, 0, 2)[:, batches]
        return halves.reshape(-1).astype(np.int32)

    def slots(self):
        quarters = self.order.reshape(self.batch_n, 2, 2, self.quarter).transpose(1, 2, 0, 3)
        quarters = quarters[:, :, exchange_order(self.batch_n)]
        none = np.full((2, 2, self.batch_n, self.slot - self.quarter), -1)
        return np.concatenate([quarters, none], axis=3).reshape(-1).astype(np.int32)


def core_chip():
    side = lax.axis_index("side")
    return side % 2, side // 2


def block_source(rows, at):
    core, chip = core_chip()
    n, p = rows.n_query, rows.n_pass
    begin = lambda c, y: jnp.where(y == chip, 0, 2 * n) + jnp.where(c == core, 0, n)
    source = jnp.where(at < n + 3 * p, begin(1, 1) + at - (n + 2 * p), -1)
    source = jnp.where(at < n + 2 * p, begin(0, 1) + at - (n + p), source)
    source = jnp.where(at < n + p, begin(1, 0) + at - n, source)
    return jnp.where(at < n, begin(0, 0) + at, source)


def take_rows(source, parts):
    total = sum(p.shape[0] for p in parts)
    pick = jnp.where(iota((source.shape[0], total), 1) == source, 1.0, 0.0).astype(BF)
    return dot(pick, jnp.concatenate([p[...] for p in parts], axis=0)).astype(BF)


def half_kernel(rows, own_ref, other_ref, far_ref, far_other_ref, *refs):
    core, chip = core_chip()
    n = rows.n_query
    at = iota((rows.half, 1), 0) + core * rows.half
    half = take_rows(block_source(rows, at), (own_ref, other_ref, far_ref, far_other_ref))
    out_ref = refs[-1]
    if len(refs) == 1:
        out_ref[...] = half
        return
    full = jnp.concatenate([half, refs[0][...]], axis=1)
    for b in range(rows.batch_n):
        out_ref[b] = full


def teacher_rows(rows, teacher_ref, pair_ref, out_ref):
    core, _ = core_chip()
    count, told = teacher_ref.shape
    line = iota((count, 1), 0)
    pair = jnp.zeros((count, 1), jnp.int32)
    for i in range(count):
        pair = jnp.where(line == i, pair_ref.ref()[i], pair)
    pair = jnp.broadcast_to(pair.astype(F32), (count, rows.columns - told))
    whole = jnp.concatenate([teacher_ref[...], pair], axis=1).astype(BF)
    place = iota((rows.half, 1), 0) + core * rows.half
    out_ref[...] = take_rows(jnp.where(place < count, place, -1), (whole,))


def near_rows(own, *tokens):
    other = lax.ppermute(own, "side", CORE_SWAP)
    far = lax.ppermute(own, "side", CHIP_SWAP)
    if tokens:
        far = behind(far, *tokens)
    return own, other, far, lax.ppermute(far, "side", CORE_SWAP)


def join_halves(core, mine, theirs):
    return jnp.concatenate(
        [jnp.where(core == 0, mine, theirs), jnp.where(core == 0, theirs, mine)], axis=0
    )


def softmax_of(scores, pick, seg_ref):
    seg = seg_ref[0].astype(F32)
    cls_seg = jnp.sum(jnp.where(pick, seg, 0.0), axis=1, keepdims=True)
    bias = jnp.where(cls_seg == seg, 0.0, NEG_FILL)
    scores = scores + jnp.concatenate([bias] * HEADS, axis=0)
    expo = jnp.exp(scores - jnp.max(scores, axis=1, keepdims=True))
    return expo / jnp.sum(expo, axis=1, keepdims=True)


def cls_forward_kernel(
    rows, with_teacher, x_ref, seg_ref, query_cls_ref, pass_cls_ref, wq_ref, bq_ref, wk_ref, wv_ref, bv_ref,
    teacher_ref, pair_ref, rows_ref, query_ref, pick_ref, told_ref, key_ref,
):
    n_pass = rows.n_pass
    side = lax.axis_index("side")
    n_query, width = query_ref.shape
    slot = iota((n_query, 1), 0)
    cls = jnp.full((n_query, 1), -1, jnp.int32)
    for i in range(n_query):
        first = query_cls_ref.ref()[0, i]
        place = jnp.where(side == 0, first, pass_cls_ref.ref()[0, 0, i] if i < n_pass else -1)
        cls = jnp.where(slot == i, place, cls)
    pick = iota((n_query, x_ref.shape[0]), 1) == cls
    pick_low = jnp.where(pick, 1.0, 0.0).astype(BF)
    pick_ref[...] = pick_low
    pick_ref.flush()
    if with_teacher:
        teacher_rows(rows, teacher_ref, pair_ref, told_ref)
    key_ref[...] = dot(x_ref[...], wk_ref[...]).astype(BF)
    key_ref.flush()
    tokens = dot(pick_low, x_ref[...]).astype(BF)
    query = (dot(tokens, wq_ref[...]) + bq_ref[...]).astype(BF)
    query_ref[...] = query
    query_ref.flush()
    rows_ref[:, width:] = tokens
    probs = softmax_of(dot_t(spread_heads(query) * BF(HD**-0.5), key_ref[...]), pick, seg_ref)
    mixed = dot(probs.astype(BF), x_ref[...])
    high = mixed.astype(BF)
    rest = (mixed - high.astype(F32)).astype(BF)
    context = fold_heads(dot(high, wv_ref[...]) + dot(rest, wv_ref[...])) + bv_ref[...]
    rows_ref[:, :width] = context.astype(BF)


def middle_kernel(
    rows, pass_count,
    mine_ref, theirs_ref, wo_ref, vector_ref, wi_ref, wu_ref, code_ref, landed_ref, value_ref, probs_ref, x_ref, key_ref, query_ref, cluster_ref,
    keep_ref, give_ref, low_ref, context_ref, gown_ref, scores_ref,
    loss_ref, small_ref, inner_bias_ref,
    both_ref, first_ref, active_ref, pre_ref, second_ref, attended_ref, slope_ref,
):
    width = wo_ref.shape[0]
    bo_ref, g1_ref, s1_ref, bu_ref, g2_ref, s2_ref, bi_ref = vectors_of(vector_ref, width)
    n_queries, n_columns = rows.queries, rows.columns
    chunk = wi_ref.shape[1] // PARTS
    side, batch = lax.axis_index("side"), lax.axis_index("batch")
    core = side % 2
    order = one_hot(rows.count, rows.count, landed_ref[...])
    placed = dot(order, join_halves(core, mine_ref[...], theirs_ref[...]))
    both_ref[...] = placed[:, : 2 * width].astype(BF)
    told = placed[: rows.queries, 2 * width :]
    attended = both_ref[:, width:].astype(F32) + (dot(both_ref[:, :width], wo_ref[...]) + bo_ref[...])
    first_hat, first_inv = norm_stats(attended)
    for ref in (value_ref, probs_ref, x_ref, key_ref, query_ref):
        ref.start()
    first = first_hat * g1_ref[...] + s1_ref[...]
    first_low = first.astype(BF)
    first_ref[...] = first_low
    second = first + bu_ref[...]
    for i in range(PARTS):
        c = i * chunk
        pre = dot(first_low, wi_ref[:, c : c + chunk]) + bi_ref[:, c : c + chunk]
        active, slope = gelu_parts(pre)
        active = active.astype(BF)
        active_ref[:, c : c + chunk] = active
        slope_ref[:, c : c + chunk] = slope
        second += dot(active, wu_ref[c : c + chunk, :])
    both_ref.flush()
    first_ref.flush()
    active_ref.flush()
    second_hat, second_inv = norm_stats(second)
    final = (second_hat * g2_ref[...] + s2_ref[...]).astype(BF)

    scale = width ** (-0.5)
    query_vec, pass_vec = final[:n_queries], final[n_queries:]
    score = dot_t(query_vec, pass_vec) * scale
    column = iota((n_queries, n_columns), 1)
    is_pair = column == told[:, n_columns - 1 :].astype(jnp.int32)
    none = jnp.full((1, n_columns - pass_count), -1.0, F32)
    cluster = jnp.concatenate([cluster_ref[...].astype(F32), none], axis=1)
    query_cluster = jnp.sum(jnp.where(is_pair, cluster, 0.0), axis=1, keepdims=True)
    counted = (cluster == query_cluster) & jnp.logical_not(is_pair) & (column < pass_count)
    pair_score = jnp.sum(jnp.where(is_pair, score, 0.0), axis=1, keepdims=True)
    resid = jnp.where(counted, pair_score - score - told, 0.0)
    squares = jnp.sum(jnp.sum(resid * resid, axis=1, keepdims=True), axis=0, keepdims=True)
    pairs = jnp.where(counted, 1.0, 0.0)
    pairs = jnp.sum(jnp.sum(pairs, axis=1, keepdims=True), axis=0, keepdims=True)
    loss_ref[...] = squares / jnp.maximum(pairs, 1.0)
    loss_ref.flush()
    grad_score = jnp.where(is_pair, jnp.sum(resid, axis=1, keepdims=True), 0.0) - resid
    grad_low = (grad_score * scale).astype(BF)
    grad_final = jnp.concatenate([dot(grad_low, pass_vec), t_dot(grad_low, query_vec)], axis=0)

    def note(at, value):
        small_ref[at : at + 1, :] = jnp.sum(value, axis=0, keepdims=True)

    grad_second = norm_back(grad_final, second_hat, second_inv, g2_ref[...])
    second_low = grad_second.astype(BF)
    second_ref[...] = second_low
    grad_first = grad_second
    for i in range(PARTS):
        c = i * chunk
        grad_pre = dot_t(second_low, wu_ref[c : c + chunk, :]) * slope_ref[:, c : c + chunk]
        inner_bias_ref[:, c : c + chunk] = jnp.sum(grad_pre, axis=0, keepdims=True)
        pre_low = grad_pre.astype(BF)
        pre_ref[:, c : c + chunk] = pre_low
        grad_first += dot_t(pre_low, wi_ref[:, c : c + chunk])
    inner_bias_ref.flush()
    pre_ref.flush()
    second_ref.flush()
    grad_attended = norm_back(grad_first, first_hat, first_inv, g1_ref[...])
    attended_low = grad_attended.astype(BF)
    attended_ref[...] = attended_low
    attended_ref.flush()
    grad_context = dot_t(attended_low, wo_ref[...]).astype(BF)
    note(0, grad_final * second_hat)
    note(1, grad_final)
    note(2, grad_second)
    note(3, grad_first * first_hat)
    note(4, grad_first)
    note(5, grad_attended)
    note(6, grad_context.astype(F32))
    small_ref[7:8, :] = jnp.zeros((1, width), F32)
    small_ref.flush()


    slot = iota((rows.n_query, 1), 0)
    base = batch * rows.block + jnp.where(side == 0, 0, rows.n_query + rows.n_pass * (side - 1))
    live = slot < jnp.where(side == 0, rows.n_query, rows.n_pass)
    own = (code_ref[...] == base + slot) & live
    high = grad_attended.astype(BF)
    rest = (grad_attended - high.astype(F32)).astype(BF)
    own = jnp.where(own, 1.0, 0.0).astype(BF)
    gown_ref[...] = dot(own, high) + dot(own, rest)
    gown_ref.flush()
    context = dot(own, grad_context).astype(BF)
    context_ref[...] = context
    context_ref.flush()
    wide = spread_heads(context)
    probs = probs_ref[...]
    grad_probs = dot_t(wide, value_ref[...])
    row_dot = jnp.sum(probs * grad_probs, axis=1, keepdims=True)
    grad_scores = (probs * (grad_probs - row_dot)).astype(BF)
    scores_ref[...] = grad_scores
    scores_ref.flush()
    query_wide = spread_heads(query_ref[...]) * BF(HD**-0.5)
    x = x_ref.ref()
    key_side = dot(grad_scores, x[...]).astype(BF)
    value_side = dot(probs.astype(BF), x[...]).astype(BF)
    key_part = t_dot(key_side, query_wide)
    value_part = t_dot(value_side, wide)
    keep_ref[...] = jnp.where(core == 0, key_part, value_part)
    give_ref[...] = jnp.where(core == 0, value_part, key_part).astype(BF)
    low_ref[...] = (fold_heads(dot(grad_scores, key_ref[...])) * HD**-0.5).astype(BF)


def grads_kernel(*refs):
    weights, inputs, outs = refs[:7], refs[7:17], refs[17:]
    weights[0].ref(), weights[1].ref()
    for ref in weights[2:] + inputs:
        if isinstance(ref, Fetched):
            ref.start()
    weight_grads_kernel(*weights, *outs[:4])
    input_grad_kernel(*inputs, outs[4])


def input_grad_kernel(
    pick_ref, scores_ref, probs_ref, context_ref, query_ref, low_ref, gown_ref,
    wq_ref, wk_ref, wv_ref, out_ref,
):
    query_wide = spread_heads(query_ref[...]) * BF(HD**-0.5)
    key_low = t_dot(scores_ref[...], query_wide).astype(BF)
    value_low = t_dot(probs_ref[...].astype(BF), spread_heads(context_ref[...])).astype(BF)
    sparse = gown_ref[...] + dot_t(low_ref[...], wq_ref[...])
    high = sparse.astype(BF)
    rest = (sparse - high.astype(F32)).astype(BF)
    pick = pick_ref[...]
    total = dot_t(key_low, wk_ref[...]) + dot_t(value_low, wv_ref[...])
    total += t_dot(jnp.concatenate([pick, pick], axis=0), jnp.concatenate([high, rest], axis=0))
    out_ref[...] = total.astype(BF)


def chip_sum_kernel(keep_ref, got_ref, out_ref):
    out_ref[...] = (keep_ref[...] + got_ref[...].astype(F32)).astype(BF)


def add_parts_kernel(rows, parts_ref, own_ref, other_ref, far_ref, far_other_ref, out_ref):
    core, chip = core_chip()
    peers, size = parts_ref.shape[:2]
    total = parts_ref[0].astype(F32)
    for i in range(1, peers):
        total += parts_ref[i].astype(F32)
    at = iota((rows.slot, 1), 0)
    source = block_source(rows, core * rows.half + chip * rows.quarter + at)
    source = jnp.where(at < rows.quarter, source, -1)
    low = take_rows(source, (own_ref, other_ref, far_ref, far_other_ref))
    total = jnp.concatenate([total.astype(BF), low], axis=0)
    for i in range(peers):
        out_ref[i] = total


def last_kernel(size, mine_ref, theirs_ref, x_ref, key_ref, value_ref, query_ref, bias_ref):
    core, _ = core_chip()
    peers = mine_ref.shape[0]
    step = peers // PARTS
    for i in range(PARTS):
        for j in range(i * step, i * step + step):
            mine, theirs = mine_ref[j, :size].astype(F32), theirs_ref[j, :size].astype(F32)
            key_ref[j * size : j * size + size, :] = jnp.where(core == 0, mine, theirs)
            value_ref[j * size : j * size + size, :] = jnp.where(core == 0, theirs, mine)
        key_ref.flush(i * step * size, step * size)
        value_ref.flush(i * step * size, step * size)
    mine = jnp.concatenate([mine_ref[j, size:] for j in range(peers)], axis=0)
    theirs = jnp.concatenate([theirs_ref[j, size:] for j in range(peers)], axis=0)
    low = join_halves(core, mine, theirs)
    bias_ref[...] = jnp.sum(low.astype(F32), axis=0, keepdims=True)
    part_rows(query_ref, x_ref, low)


def core_groups(batch_n):
    order = exchange_order(batch_n)
    return [[(y * 2 + c) * batch_n + b for y in range(2) for b in order] for c in range(2)]


def exchange(sent, batch_n):
    return lax.all_to_all(
        sent, ("side", "batch"), split_axis=0, concat_axis=0, axis_index_groups=core_groups(batch_n)
    )


def scatter_sum(keep, give, batch_n):
    got = lax.ppermute(give, "side", CORE_SWAP)
    total, token = call(chip_sum_kernel, [(keep.shape, BF, True)], (keep, got), name="chip_sum")
    return exchange(total.reshape(2 * batch_n, keep.shape[0] // (2 * batch_n), keep.shape[1]), batch_n), token


def part_rows(result, left, right):
    size = result.shape[0] // PARTS
    for i in range(PARTS):
        result[i * size : i * size + size, :] = t_dot(left[:, i * size : i * size + size], right)
        result.flush(i * size, size)


def weight_grads_kernel(
    active_ref, second_ref, first_ref, pre_ref, both_ref, attended_ref, slots_ref,
    outer_ref, inner_ref, out_ref, x_ref,
):
    part_rows(outer_ref, active_ref, second_ref[...])
    part_rows(inner_ref, first_ref, pre_ref[...])
    part_rows(out_ref, both_ref, attended_ref[...])
    width = out_ref.shape[0]
    count = both_ref.shape[0]
    pick = one_hot(count, slots_ref.shape[1], slots_ref[...])
    x_ref[...] = t_dot(pick, both_ref[:, width:]).astype(BF)


class Row:
    def __init__(self, source, at, width):
        self.source, self.at, self.width = source, at, width

    def __getitem__(self, index):
        first, last = 0, self.width
        if index is not Ellipsis:
            first, last = index[1].start, index[1].stop
        return self.source[self.at : self.at + 1, first:last]


def vectors_of(source, width):
    return [Row(source, i, width) for i in range(6)] + [Row(source, 6, source.shape[1])]


def column_of(row):
    return jnp.transpose(jnp.broadcast_to(row, (128, row.shape[1])))[:, :1]


def attention_kernel(
    tile, tiles, sizes, x_ref, wq_ref, bq_ref, key_ref, value_ref, seg_ref, out_ref, q_scr, bias_scr
):
    count = x_ref.shape[0]
    x, wq, bq, seg = ref_of(x_ref), ref_of(wq_ref), bq_ref[...], seg_ref[0]
    places = iota((1, count), 1)
    keys, values, seg_whole = ref_of(key_ref), ref_of(value_ref), ref_of(seg_ref)

    @pl.loop(*tiles)
    def _(i):
        row = pl.multiple_of(i * tile, tile)
        q = (dot(x[pl.ds(row, tile), :], wq[...]) + bq).astype(BF)
        q_scr[...] = q * BF(HD**-0.5)
        first = jnp.max(jnp.where(places == row, seg, -2))
        last = jnp.max(jnp.where(places == row + (tile - 1), seg, -2))
        low = jnp.min(jnp.where(seg == first, places, count)) // 128 * 128
        high = jnp.max(jnp.where(seg == last, places, -1)) + 1
        own = seg_whole[0, :, pl.ds(row, tile)].astype(F32)
        own = column_of(own)
        before = jnp.int32(0)
        for size in sizes:
            start = jnp.minimum(low, count - size)
            fits = (high - start <= size) if size < count else jnp.bool_(True)

            @pl.when(jnp.logical_and(before == 0, fits))
            def _(size=size, start=start):
                at = pl.multiple_of(start, 128)
                near = seg_whole[0, :, pl.ds(at, size)].astype(F32)
                bias_scr[:, :size] = jnp.where(own == near, 0.0, NEG_FILL)
                half = iota((1, 2 * HD), 1) // HD
                here = pl.ds(row - tiles[0] * tile, tile)

                def heads(first):
                    slabs = [pl.ds(first + k * 2 * HD, 2 * HD) for k in range(together)]
                    both = [(slab, h) for slab in slabs for h in range(2)]
                    scores = [
                        dot_t(jnp.where(half == h, q_scr[:, slab], BF(0)), keys[pl.ds(at, size), slab])
                        + bias_scr[:, :size]
                        for slab, h in both
                    ]
                    expos = [jnp.exp(s - jnp.max(s, axis=1, keepdims=True)).astype(BF) for s in scores]
                    outs = []
                    for (slab, h), expo in zip(both, expos):
                        mixed = dot(expo, jnp.where(half == h, values[pl.ds(at, size), slab], BF(1)))
                        outs.append(mixed / pltpu.roll(mixed, HD, 1))
                    for k, slab in enumerate(slabs):
                        out = jnp.where(half == 0, outs[2 * k], outs[2 * k + 1])
                        ref_of(out_ref)[here, slab] = out.astype(BF)

                together = SLABS_AT_ONCE.get(size, 1 if size > 512 else HEADS // 2)
                if together == HEADS // 2:
                    heads(0)
                else:

                    @pl.loop(0, HEADS // 2 // together)
                    def _(j):
                        heads(pl.multiple_of(j * (together * 2 * HD), together * 2 * HD))

            before = jnp.where(fits, 1, before)


def window_sizes(count):
    return [size for size in (384, 512, 768) if size < count] + [count]


def first_attention_kernel(
    tile, tiles, x_ref, key_ref, wv_ref, bv_ref, wq_ref, bq_ref, seg_ref, pick_ref, query_ref, *refs
):
    out_ref, value_ref, probs_ref, vector_ref, q_scr, bias_scr = refs[-6:]
    value_ref[...] = (dot(x_ref[...], wv_ref[...]) + bv_ref[...]).astype(BF)
    value_ref.flush()
    scores = dot_t(spread_heads(query_ref[...]) * BF(HD**-0.5), key_ref[...])
    probs_ref[...] = softmax_of(scores, pick_ref[...].astype(F32) > 0.5, seg_ref)
    probs_ref.flush()
    for i, ref in enumerate(refs[:-6]):
        vector_ref[i : i + 1, : ref.shape[1]] = ref[...]
    vector_ref.flush()
    sizes = window_sizes(x_ref.shape[0])
    attention_kernel(
        tile, tiles, sizes, x_ref, wq_ref, bq_ref, key_ref, value_ref, seg_ref, out_ref, q_scr, bias_scr
    )


def first_attention(x, keys, wv, bv, wq, bq, seg, pick, query, vectors, after, share, tile=256):
    t, d = x.shape
    return call(
        functools.partial(first_attention_kernel, tile, (0, share // tile)),
        [
            ((share, d), BF, False),
            ((t, d), BF, False),
            ((HEADS * query.shape[0], t), F32, False),
            ((8, vectors[-1].shape[1]), F32, False),
        ],
        (x, keys, wv, bv, wq, bq, seg, pick, query) + vectors,
        flops=6 * 10**9,
        far=range(9 + len(vectors)),
        scratch=[pltpu.VMEM((tile, d), BF), pltpu.VMEM((tile, t), F32)],
        limit=24,
        after=after,
        name="first_attention",
    )


def ffn_kernel(
    tile, x_ref, first_ref, rest_ref, wo_ref, vector_ref, wi_ref, wu_ref, out_ref,
):
    bo_ref, g1_ref, s1_ref, bu_ref, g2_ref, s2_ref, bi_ref = vectors_of(vector_ref, x_ref.shape[1])
    chunk = wi_ref.size
    for t in range(0, x_ref.shape[0], tile):
        part = slice(t, t + tile)
        share = first_ref.shape[0]
        near = first_ref[part, :] if t < share else rest_ref[t - share : t - share + tile, :]
        attended = x_ref[part, :].astype(F32) + (dot(near, wo_ref[...]) + bo_ref[...])
        first = norm_stats(attended)[0] * g1_ref[...] + s1_ref[...]
        first_low = first.astype(BF)
        second = first + bu_ref[...]
        for c in range(PARTS):
            pre = dot(first_low, wi_ref.part(c)) + bi_ref[:, c * chunk : c * chunk + chunk]
            second += dot(gelu(pre).astype(BF), wu_ref.part(c))
        out_ref[part, :] = (norm_stats(second)[0] * g2_ref[...] + s2_ref[...]).astype(BF)
        out_ref.flush(t, tile)


def dense_kernel(
    tile, tiles, x_ref, wq_ref, bq_ref, key_ref, value_ref, seg_ref, first_ref, wo_ref, vector_ref, wi_ref,
    wu_ref, out_ref, rest_ref, q_scr, bias_scr,
):
    for ref in (x_ref, wq_ref, bq_ref, key_ref, value_ref, seg_ref):
        ref.ref()
    for ref in (first_ref, wo_ref, vector_ref, wi_ref, wu_ref):
        ref.start()
    count = x_ref.shape[0]
    attention_kernel(
        tile, tiles, window_sizes(count), x_ref, wq_ref, bq_ref, key_ref, value_ref, seg_ref, rest_ref,
        q_scr, bias_scr,
    )
    ffn_kernel(512, x_ref, first_ref, rest_ref, wo_ref, vector_ref, wi_ref, wu_ref, out_ref)


def dense_rest(x, wq, bq, keys, values, seg, context, weights, after, tile=256):
    t, d = x.shape
    share = context.shape[0]
    return call(
        functools.partial(dense_kernel, tile, (share // tile, t // tile)),
        [(x.shape, BF, False)],
        (x, wq, bq, keys, values, seg, context) + weights,
        flops=8 * 10**9,
        far=(0, 1, 2, 5, 3, 4, 6, 7, 8, 9, 10),
        late=range(6, 11),
        split={9: (1, PARTS), 10: (0, PARTS)},
        scratch=[pltpu.VMEM((t - share, d), BF), pltpu.VMEM((tile, d), BF), pltpu.VMEM((tile, t), F32)],
        limit=40,
        after=after,
        name="dense_rest",
    )


def middle_large(
    rows, pass_count, core, mine, theirs, told, cluster, wo, bo, g1, s1, wi, bi, wu, bu, g2, s2
):
    width = wo.shape[0]
    both = join_halves(core, mine, theirs)[np.argsort(rows.landed(np.arange(rows.batch_n)))]
    attended = both[:, width:].astype(F32) + (dot(both[:, :width], wo) + bo)
    first_hat, first_inv = norm_stats(attended)
    first = first_hat * g1 + s1
    first_low = first.astype(BF)
    active, slope = gelu_parts(dot(first_low, wi) + bi)
    active_low = active.astype(BF)
    second = first + (dot(active_low, wu) + bu)
    second_hat, second_inv = norm_stats(second)
    final = (second_hat * g2 + s2).astype(BF)
    query_vec, pass_vec = final[: rows.queries], final[rows.queries : rows.queries + pass_count]
    scale = width ** (-0.5)
    score = dot_t(query_vec, pass_vec) * scale
    is_pair = iota(score.shape, 1) == told[:, pass_count:].astype(jnp.int32)
    query_cluster = jnp.sum(jnp.where(is_pair, cluster, 0.0), axis=1, keepdims=True)
    counted = (cluster == query_cluster) & jnp.logical_not(is_pair)
    pair_score = jnp.sum(jnp.where(is_pair, score, 0.0), axis=1, keepdims=True)
    resid = jnp.where(counted, pair_score - score - told[:, :pass_count], 0.0)
    loss = jnp.sum(resid * resid) / jnp.maximum(jnp.sum(counted.astype(F32)), 1.0)
    grad_score = jnp.where(is_pair, jnp.sum(resid, axis=1, keepdims=True), 0.0) - resid
    grad_low = (grad_score * scale).astype(BF)
    none = jnp.zeros((rows.count - rows.queries - pass_count, width), F32)
    grad_final = jnp.concatenate([dot(grad_low, pass_vec), t_dot(grad_low, query_vec), none], axis=0)
    grad_second = norm_back(grad_final, second_hat, second_inv, g2)
    second_low = grad_second.astype(BF)
    grad_pre = dot_t(second_low, wu) * slope
    pre_low = grad_pre.astype(BF)
    grad_first = dot_t(pre_low, wi) + grad_second
    grad_attended = norm_back(grad_first, first_hat, first_inv, g1)
    attended_low = grad_attended.astype(BF)
    grad_context = dot_t(attended_low, wo).astype(BF)
    small = jnp.stack(
        [
            jnp.sum(v, axis=0)
            for v in (
                grad_final * second_hat, grad_final, grad_second, grad_first * first_hat,
                grad_first, grad_attended, grad_context.astype(F32),
            )
        ]
    )
    inner_bias = jnp.sum(grad_pre, axis=0, keepdims=True)
    return (
        loss.reshape(1, 1), grad_attended, grad_context, small, inner_bias,
        both, first_low, active_low, pre_low, second_low, attended_low,
    )


def own_large(rows, side, batch, grad_attended, grad_context, tokens, keys, values, cls_query, probs):
    core = side % 2
    slot = jnp.arange(rows.n_query)[:, None]
    base = batch * rows.block + jnp.where(side == 0, 0, rows.n_query + rows.n_pass * (side - 1))
    live = slot < jnp.where(side == 0, rows.n_query, rows.n_pass)
    own = ((rows.code[None, :] == base + slot) & live).astype(F32)
    own_attended = dot(own, grad_attended, lax.Precision.HIGHEST)
    context = dot(own.astype(BF), grad_context).astype(BF)
    wide = spread_heads(context)
    grad_probs = dot_t(wide, values)
    row_dot = jnp.sum(probs * grad_probs, axis=1, keepdims=True)
    grad_scores = (probs * (grad_probs - row_dot)).astype(BF)
    query_wide = spread_heads(cls_query) * BF(HD**-0.5)
    key_part = t_dot(dot(grad_scores, tokens).astype(BF), query_wide)
    value_part = t_dot(dot(probs.astype(BF), tokens).astype(BF), wide)
    keep = jnp.where(core == 0, key_part, value_part)
    give = jnp.where(core == 0, value_part, key_part).astype(BF)
    low = (fold_heads(dot(grad_scores, keys)) * HD**-0.5).astype(BF)
    return keep, give, low, context, own_attended, grad_scores


def fetch(arrays, behind_this):
    hbm = pl.BlockSpec(memory_space=pltpu.HBM)
    count = len(arrays)

    def kernel(*refs):
        semaphores = refs[-1]
        copies = [
            pltpu.make_async_copy(refs[i], refs[count + 1 + i], semaphores.at[i]) for i in range(count)
        ]
        for copy in copies:
            copy.start()
        for copy in copies:
            copy.wait()

    return pl.pallas_call(
        kernel,
        out_shape=[pltpu.VMEM(x.shape, x.dtype) for x in arrays],
        in_specs=[hbm] * count + [VM],
        out_specs=[VM] * count,
        scratch_shapes=[pltpu.SemaphoreType.DMA((count,))],
        compiler_params=pltpu.CompilerParams(vmem_limit_bytes=4 * MIB),
        name="fetch",
    )(*[pltpu.with_memory_space_constraint(x, pltpu.HBM) for x in arrays], behind_this)


def middle(rows, pass_count, mine, theirs, kept, weights, cluster, hidden, after):
    width, ff = weights[2].shape
    count = rows.count
    keys, values, cls_query, probs = kept
    landed = rows.landed(exchange_order(rows.batch_n))
    ins = (mine, theirs) + weights
    ins += (rows.code[None, :], landed[None, :], values, probs, hidden, keys, cls_query, cluster[None, :])
    outs = [
        ((width, width), F32, True), ((width, width), BF, True), ((rows.n_query, width), BF, True),
        ((rows.n_query, width), BF, False), ((rows.n_query, width), F32, False), (probs.shape, BF, False),
        ((1, 1), F32, False), ((8, width), F32, False), ((1, ff), F32, False),
        ((count, 2 * width), BF, False), ((count, width), BF, False), ((count, ff), BF, False),
        ((count, ff), BF, False), ((count, width), BF, False), ((count, width), BF, False),
    ]
    return call(
        functools.partial(middle_kernel, rows, pass_count),
        outs,
        ins,
        flops=12 * count * width * ff,
        scratch=[pltpu.VMEM((count, ff), F32)],
        far=(7, 6) + tuple(range(8, len(ins))),
        late=range(8, len(ins) - 1),
        limit=32,
        after=after,
        name="cls_middle",
    )


def body(
    hidden_in,
    segments,
    query_cls,
    passage_cls,
    pair_passage,
    passage_cluster,
    teacher,
    query_weight,
    query_bias,
    key_weight,
    value_weight,
    value_bias,
    out_weight,
    out_bias,
    first_gain,
    first_shift,
    inner_weight,
    inner_bias,
    outer_weight,
    outer_bias,
    second_gain,
    second_shift,
):
    count_tok = hidden_in.shape[2]
    width = hidden_in.shape[3]
    n_query = query_cls.shape[1]
    n_pass = passage_cls.shape[2]
    batch_n = lax.axis_size("batch")
    side = lax.axis_index("side")
    pass_count = teacher.shape[1]
    rows = Rows(batch_n, n_query, n_pass, pass_count)

    hidden = hidden_in.reshape(count_tok, width)

    def vec(v):
        return v.reshape(1, -1)

    weights = (
        out_weight, vec(out_bias), vec(first_gain), vec(first_shift), inner_weight, vec(inner_bias),
        outer_weight, vec(outer_bias), vec(second_gain), vec(second_shift),
    )
    small_case = rows.count <= 512 and rows.columns == 128 and count_tok % 512 == 0

    own, cls_query, pick, told, keys, _ = call(
        functools.partial(cls_forward_kernel, rows, small_case),
        [
            ((n_query, 2 * width), BF, True),
            ((n_query, width), BF, False),
            ((n_query, count_tok), BF, False),
            ((rows.half, rows.columns), BF, True),
            ((count_tok, width), BF, False),
        ],
        (
            hidden, segments, query_cls, passage_cls, query_weight, vec(query_bias), key_weight,
            value_weight, vec(value_bias), teacher, pair_passage,
        ),
        flops=2 * count_tok * width * width,
        far=(6, 0, 4, 1, 5, 9, 7, 8),
        smem=(2, 3, 10),
        limit=24,
        name="cls_forward",
    )

    near = near_rows(own)
    if small_case:
        sent, half_done = call(
            functools.partial(half_kernel, rows),
            [((batch_n, rows.half, 2 * width + rows.columns), BF, True)],
            near + (told,),
            name="half_rows",
        )
    else:
        half, half_done = call(
            functools.partial(half_kernel, rows),
            [((rows.half, 2 * width), BF, True)],
            near,
            name="half_rows",
        )
        sent = jnp.broadcast_to(half[None], (batch_n,) + half.shape)
    batches = exchange_order(batch_n)
    mine = lax.all_to_all(
        sent, "batch", split_axis=0, concat_axis=0, axis_index_groups=[batches] if small_case else None
    )
    vectors = (weights[1], weights[2], weights[3], weights[7], weights[8], weights[9], weights[5])
    share = count_tok // 2
    first_context, values, probs, vectors, attention_done = first_attention(
        hidden, keys, value_weight, vec(value_bias), query_weight, vec(query_bias), segments, pick,
        cls_query, vectors, (half_done,), share,
    )
    matrices = (out_weight, vectors, inner_weight, outer_weight)
    if small_case:
        mine = behind(mine, attention_done)
    theirs = lax.ppermute(mine, "side", CORE_SWAP)

    if small_case:
        kept = (keys, values, cls_query, probs)
        flat = (batch_n * rows.half, mine.shape[2])
        (
            keep, give, query_low, own_context, own_attended, grad_scores, loss, small, grad_inner_bias,
            both, first_low, active_low, pre_low, second_low, attended_low, _,
        ) = middle(
            rows, pass_count, mine.reshape(flat), theirs.reshape(flat), kept, tuple(fetch(matrices, mine)),
            passage_cluster, hidden, (),
        )
    else:
        told = jnp.concatenate([teacher, pair_passage[:, None].astype(F32)], axis=1)
        told = lax.all_to_all(
            jnp.broadcast_to(told[None], (batch_n,) + told.shape), "batch", split_axis=0, concat_axis=0
        ).reshape(batch_n * n_query, pass_count + 1)
        flat = (batch_n * rows.half, 2 * width)
        (
            loss, grad_attended, grad_context, small, grad_inner_bias,
            both, first_low, active_low, pre_low, second_low, attended_low,
        ) = middle_large(
            rows, pass_count, side % 2, mine.reshape(flat), theirs.reshape(flat), told,
            passage_cluster.astype(F32)[None, :], *weights,
        )
        keep, give, query_low, own_context, own_attended, grad_scores = own_large(
            rows, side, lax.axis_index("batch"), grad_attended, grad_context,
            hidden, keys, values, cls_query, probs,
        )

    parts, sum_done = scatter_sum(keep, give, batch_n)
    peers, size = parts.shape[:2]
    for_input = (
        pick, grad_scores, probs, own_context, cls_query, query_low, own_attended, query_weight, key_weight,
        value_weight,
    )
    if small_case and size % 16 == 0:
        saved = (active_low, second_low, first_low, pre_low, both, attended_low, rows.slots()[None, :])
        grad_outer_weight, grad_inner_weight, grad_out_weight, all_tokens, input_grad, weight_done = call(
            grads_kernel,
            [
                (outer_weight.shape, F32, False),
                (inner_weight.shape, F32, False),
                (out_weight.shape, F32, False),
                ((4 * rows.batch_n * rows.slot, width), BF, False),
                (hidden.shape, BF, False),
            ],
            saved + for_input,
            flops=2 * rows.count * width * (4 * width + width) + 6 * count_tok * width * width,
            far=tuple(i for i in range(17) if i != 12),
            late=range(2, 17),
            limit=40,
            after=(sum_done,),
            name="grads",
        )
        low = near_rows(query_low, weight_done)
        sent, add_done = call(
            functools.partial(add_parts_kernel, rows),
            [((peers, size + rows.slot, width), BF, True)],
            (parts,) + low,
            after=(weight_done,),
            name="add_parts",
        )
        whole = exchange(sent, batch_n)
        rows_out, dense_done = dense_rest(
            hidden, query_weight, vec(query_bias), keys, values, segments, first_context, matrices,
            (add_done,),
        )
        whole = behind(whole, dense_done)
        other = lax.ppermute(whole, "side", CORE_SWAP)
        grad_key_weight, grad_value_weight, grad_query_weight, grad_query_bias, _ = call(
            functools.partial(last_kernel, size),
            [((width, width), F32, False)] * 3 + [((1, width), F32, False)],
            (whole, other, all_tokens),
            far=(2,),
            limit=12,
            name="last_grads",
        )
    else:
        input_grad, _ = call(
            input_grad_kernel,
            [(hidden.shape, BF, False)],
            for_input,
            far=(1, 4, 2, 3, 0, 6, 8, 9, 7),
            limit=20,
            after=(sum_done,),
            name="input_grad",
        )
        rows_out, _ = dense_rest(
            hidden, query_weight, vec(query_bias), keys, values, segments, first_context, matrices,
            (sum_done,),
        )
        part = jnp.sum(parts.astype(F32), axis=0).astype(BF)
        whole = exchange(jnp.broadcast_to(part[None], parts.shape), batch_n).reshape(width, width)
        grad_outer_weight = t_dot(active_low, second_low)
        grad_inner_weight = t_dot(first_low, pre_low)
        grad_out_weight = t_dot(both[:, :width], attended_low)
        half, _ = call(
            functools.partial(half_kernel, rows),
            [((rows.half, width), BF, True)],
            near_rows(query_low),
            name="low_rows",
        )
        flat = (batch_n * rows.half, width)
        half = jnp.broadcast_to(half[None], (batch_n,) + half.shape)
        low_mine = lax.all_to_all(half, "batch", split_axis=0, concat_axis=0).reshape(flat)
        low_theirs = lax.ppermute(low_mine, "side", CORE_SWAP)
        all_low = join_halves(side % 2, low_mine, low_theirs)[np.argsort(rows.landed(np.arange(rows.batch_n)))]
        grad_query_weight = t_dot(both[:, width:], all_low)
        grad_query_bias = jnp.sum(all_low.astype(F32), axis=0)
        other = lax.ppermute(whole, "side", CORE_SWAP)
        first_core = side % 2 == 0
        grad_key_weight = jnp.where(first_core, whole, other).astype(F32)
        grad_value_weight = jnp.where(first_core, other, whole).astype(F32)

    return (
        loss.reshape(()),
        rows_out.reshape(hidden_in.shape),
        input_grad.reshape(hidden_in.shape),
        grad_query_weight,
        grad_query_bias.reshape(-1),
        grad_key_weight,
        grad_value_weight,
        small[6],
        grad_out_weight,
        small[5],
        small[3],
        small[4],
        grad_inner_weight,
        grad_inner_bias.reshape(-1),
        grad_outer_weight,
        small[2],
        small[0],
        small[1],
    )


def solution(mesh):
    rows = P("side", "batch", None, None)
    in_specs = (
        rows,
        P("side", "batch", None),
        P("batch", None),
        P("side", "batch", None),
        P("batch"),
        P(),
        P("batch", None),
    ) + (P(),) * 15
    out_specs = (P(), rows, rows) + (P(),) * 15
    return jax.shard_map(body, mesh=mesh, in_specs=in_specs, out_specs=out_specs, check_vma=False)
```

```python
import functools

import jax
import jax.numpy as jnp
import numpy as np
from jax import lax
from jax.experimental import pallas as pl
from jax.experimental.pallas import tpu as pltpu
from jax.sharding import PartitionSpec as P

HEADS = 8
HD = 64
EPSILON = 1e-05
NEG_FILL = -1e30
BF = jnp.bfloat16
F32 = jnp.float32
CORE_SWAP = [(0, 1), (1, 0), (2, 3), (3, 2)]
CHIP_SWAP = [(0, 2), (2, 0), (1, 3), (3, 1)]
MIB = 1 << 20
VM = pl.BlockSpec(memory_space=pltpu.VMEM)


def dot(left, right, precision=None):
    return jnp.dot(left, right, preferred_element_type=F32, precision=precision)


def dot_t(left, right):
    return lax.dot_general(left, right, (((1,), (1,)), ((), ())), preferred_element_type=F32)


def t_dot(left, right):
    return lax.dot_general(left, right, (((0,), (0,)), ((), ())), preferred_element_type=F32)


def iota(shape, axis):
    return lax.broadcasted_iota(jnp.int32, shape, axis)


def one_hot(rows, cols, row_of_col):
    return jnp.where(iota((rows, cols), 0) == row_of_col, 1.0, 0.0).astype(BF)


def norm_stats(summed):
    centre = jnp.mean(summed, axis=1, keepdims=True)
    deviation = summed - centre
    inverse = lax.rsqrt(jnp.mean(deviation * deviation, axis=1, keepdims=True) + EPSILON)
    return deviation * inverse, inverse


def norm_back(upstream, normed, inverse, gain):
    scaled = upstream * gain
    inner = jnp.mean(scaled, axis=1, keepdims=True)
    cross = jnp.mean(scaled * normed, axis=1, keepdims=True)
    return inverse * (scaled - inner - normed * cross)


def gelu(pre):
    return (0.5 * pre) * (1.0 + lax.erf(pre * (0.5**0.5)))


def gelu_parts(pre):
    phi = 0.5 + 0.5 * lax.erf(pre * (0.5**0.5))
    density = jnp.exp(-0.5 * (pre * pre)) * 0.3989422804014327
    return pre * phi, phi + pre * density


def spread_heads(rows):
    head = iota((1, rows.shape[1]), 1) // HD
    return jnp.concatenate(
        [jnp.where(head == h, rows, jnp.zeros_like(rows)) for h in range(HEADS)], axis=0
    )


def fold_heads(wide):
    count = wide.shape[0] // HEADS
    head = iota((1, wide.shape[1]), 1) // HD
    total = jnp.zeros((count, wide.shape[1]), wide.dtype)
    for h in range(HEADS):
        total = jnp.where(head == h, wide[h * count : (h + 1) * count], total)
    return total


class Fetched:
    def __init__(self, source, buffer, semaphores, axis=0, parts=1):
        self.buffer, self.shape = buffer, buffer.shape
        self.axis, self.size = axis, buffer.shape[axis] // parts
        self.waiting, self.copies = {}, []
        for i in range(parts):
            at = self.place(i) if parts > 1 else (Ellipsis,)
            self.copies.append(pltpu.make_async_copy(source.at[at], buffer.at[at], semaphores.at[i]))

    def start(self):
        if not self.waiting and self.copies:
            self.waiting = dict(enumerate(self.copies))
            self.copies = []
            for copy in self.waiting.values():
                copy.start()

    def place(self, i):
        return (slice(None),) * self.axis + (pl.ds(i * self.size, self.size),)

    def part(self, i):
        self.start()
        if i in self.waiting:
            self.waiting.pop(i).wait()
        return self.buffer[self.place(i)]

    def ref(self):
        self.start()
        for i in sorted(self.waiting):
            self.waiting.pop(i).wait()
        return self.buffer

    def __getitem__(self, index):
        return self.ref()[index]


def ref_of(x):
    return x.ref() if isinstance(x, Fetched) else x.buffer if isinstance(x, Result) else x


class Result:
    def __init__(self, buffer, target, semaphores):
        self.buffer, self.target, self.semaphores = buffer, target, semaphores
        self.shape, self.dtype, self.copies = buffer.shape, buffer.dtype, []

    def __setitem__(self, index, value):
        self.buffer[index] = value

    def __getitem__(self, index):
        return self.buffer[index]

    def flush(self, first=None, size=None):
        source, target = self.buffer, self.target
        if first is not None:
            source, target = source.at[pl.ds(first, size)], target.at[pl.ds(first, size)]
        copy = pltpu.make_async_copy(source, target, self.semaphores.at[len(self.copies)])
        copy.start()
        self.copies.append(copy)


PARTS = 4
SLABS_AT_ONCE = {384: 2, 512: 2, 768: 2}
TOKEN = ((8, 128), F32, False)


def call(kernel, outs, ins, flops=0, scratch=(), limit=8, far=(), smem=(), split=None, late=(), after=(), name=None):
    n_in, n_out, n_after = len(ins), len(outs), len(after)
    split = split or {}
    far_in = list(smem) + [i for i in far if i not in smem]
    far_out = [i for i in range(n_out) if not outs[i][2]]
    shapes = [(pltpu.VMEM if near else pltpu.HBM)(s, d) for s, d, near in list(outs) + [TOKEN]]
    moved = sum(x.size * x.dtype.itemsize for x in ins)
    moved += sum(int(np.prod(s)) * jnp.dtype(d).itemsize for s, d, _ in outs)
    ins = [pltpu.with_memory_space_constraint(x, pltpu.HBM) if i in far_in else x for i, x in enumerate(ins)]
    after = [pltpu.with_memory_space_constraint(x, pltpu.HBM) for x in after]

    def wrapped(*refs):
        refs = list(refs)
        in_refs, refs = refs[:n_in], refs[n_in + n_after :]
        out_refs, refs = refs[:n_out], refs[n_out + 1 :]
        in_bufs, refs = refs[: len(far_in)], refs[len(far_in) :]
        out_bufs, refs = refs[: len(far_out)], refs[len(far_out) :]
        if far_in:
            semaphores, refs = refs[0], refs[1:]
            for k, i in enumerate(far_in):
                in_refs[i] = Fetched(in_refs[i], in_bufs[k], semaphores.at[k], *split.get(i, ()))
                if i not in late:
                    in_refs[i].start()
        if far_out:
            semaphores, refs = refs[0], refs[1:]
            for k, i in enumerate(far_out):
                out_refs[i] = Result(out_bufs[k], out_refs[i], semaphores.at[k])
        kernel(*in_refs, *out_refs, *refs)
        for i in far_in:
            in_refs[i].ref()
        for i in far_out:
            if not out_refs[i].copies:
                out_refs[i].flush()
        for i in far_out:
            for copy in out_refs[i].copies:
                copy.wait()

    hbm = pl.BlockSpec(memory_space=pltpu.HBM)
    spaces = [hbm if i in far_in else VM for i in range(n_in)] + [hbm] * n_after
    out_spaces = [hbm if i in far_out else VM for i in range(n_out)] + [hbm]
    buffers = [(pltpu.SMEM if i in smem else pltpu.VMEM)(ins[i].shape, ins[i].dtype) for i in far_in]
    buffers += [pltpu.VMEM(outs[i][0], outs[i][1]) for i in far_out]
    if far_in:
        buffers.append(pltpu.SemaphoreType.DMA((len(far_in), PARTS)))
    if far_out:
        buffers.append(pltpu.SemaphoreType.DMA((len(far_out), PARTS)))
    return pl.pallas_call(
        wrapped,
        out_shape=shapes,
        in_specs=spaces,
        out_specs=out_spaces,
        scratch_shapes=buffers + list(scratch),
        compiler_params=pltpu.CompilerParams(vmem_limit_bytes=limit * MIB),
        cost_estimate=pl.CostEstimate(
            flops=int(flops), bytes_accessed=int(moved), transcendentals=0
        ),
        name=name,
    )(*ins, *after)


def behind(value, *tokens):
    tokens = [pltpu.with_memory_space_constraint(x, pltpu.HBM) for x in tokens]
    return pl.pallas_call(
        lambda *refs: None,
        out_shape=pltpu.VMEM(value.shape, value.dtype),
        in_specs=[VM] + [pl.BlockSpec(memory_space=pltpu.HBM)] * len(tokens),
        out_specs=VM,
        input_output_aliases={0: 0},
        compiler_params=pltpu.CompilerParams(vmem_limit_bytes=MIB),
        name="hand_on",
    )(value, *tokens)


def exchange_order(batch_n):
    order = []
    for x in range(2):
        run = [b for b in range(batch_n) if b % 2 == x][::-1]
        order += run[1:] + run[:1]
    return order


class Rows:
    def __init__(self, batch_n, n_query, n_pass, pass_count):
        block = n_query + 3 * n_pass
        block += -block % 16
        self.batch_n, self.n_query, self.n_pass, self.block = batch_n, n_query, n_pass, block
        self.half = block // 2
        self.columns = pass_count + 1 + -(pass_count + 1) % 128
        self.count = batch_n * block
        self.queries = batch_n * n_query
        self.quarter = block // 4
        self.slot = self.quarter + -self.quarter % 16
        batch, place = np.meshgrid(np.arange(batch_n), np.arange(block), indexing="ij")
        group, slot = (place - n_query) // n_pass, (place - n_query) % n_pass
        order = self.queries + (group * batch_n + batch) * n_pass + slot
        order = np.where(place < n_query, batch * n_query + place, order)
        order = np.where(group < 3, order, self.queries + pass_count + batch)
        self.order = order
        self.code = np.empty(self.count, np.int32)
        self.code[order.reshape(-1)] = np.arange(self.count)

    def landed(self, batches):
        halves = self.order.reshape(self.batch_n, 2, self.half).transpose(1, 0, 2)[:, batches]
        return halves.reshape(-1).astype(np.int32)

    def slots(self):
        quarters = self.order.reshape(self.batch_n, 2, 2, self.quarter).transpose(1, 2, 0, 3)
        quarters = quarters[:, :, exchange_order(self.batch_n)]
        none = np.full((2, 2, self.batch_n, self.slot - self.quarter), -1)
        return np.concatenate([quarters, none], axis=3).reshape(-1).astype(np.int32)


def core_chip():
    side = lax.axis_index("side")
    return side % 2, side // 2


def block_source(rows, at):
    core, chip = core_chip()
    n, p = rows.n_query, rows.n_pass
    begin = lambda c, y: jnp.where(y == chip, 0, 2 * n) + jnp.where(c == core, 0, n)
    source = jnp.where(at < n + 3 * p, begin(1, 1) + at - (n + 2 * p), -1)
    source = jnp.where(at < n + 2 * p, begin(0, 1) + at - (n + p), source)
    source = jnp.where(at < n + p, begin(1, 0) + at - n, source)
    return jnp.where(at < n, begin(0, 0) + at, source)


def take_rows(source, parts):
    total = sum(p.shape[0] for p in parts)
    pick = jnp.where(iota((source.shape[0], total), 1) == source, 1.0, 0.0).astype(BF)
    return dot(pick, jnp.concatenate([p[...] for p in parts], axis=0)).astype(BF)


def half_kernel(rows, own_ref, other_ref, far_ref, far_other_ref, *refs):
    core, chip = core_chip()
    n = rows.n_query
    at = iota((rows.half, 1), 0) + core * rows.half
    half = take_rows(block_source(rows, at), (own_ref, other_ref, far_ref, far_other_ref))
    out_ref = refs[-1]
    if len(refs) == 1:
        out_ref[...] = half
        return
    full = jnp.concatenate([half, refs[0][...]], axis=1)
    for b in range(rows.batch_n):
        out_ref[b] = full


def teacher_rows(rows, teacher_ref, pair_ref, out_ref):
    core, _ = core_chip()
    count, told = teacher_ref.shape
    line = iota((count, 1), 0)
    pair = jnp.zeros((count, 1), jnp.int32)
    for i in range(count):
        pair = jnp.where(line == i, pair_ref.ref()[i], pair)
    pair = jnp.broadcast_to(pair.astype(F32), (count, rows.columns - told))
    whole = jnp.concatenate([teacher_ref[...], pair], axis=1).astype(BF)
    place = iota((rows.half, 1), 0) + core * rows.half
    out_ref[...] = take_rows(jnp.where(place < count, place, -1), (whole,))


def near_rows(own, *tokens):
    other = lax.ppermute(own, "side", CORE_SWAP)
    far = lax.ppermute(own, "side", CHIP_SWAP)
    if tokens:
        far = behind(far, *tokens)
    return own, other, far, lax.ppermute(far, "side", CORE_SWAP)


def join_halves(core, mine, theirs):
    return jnp.concatenate(
        [jnp.where(core == 0, mine, theirs), jnp.where(core == 0, theirs, mine)], axis=0
    )


def softmax_of(scores, pick, seg_ref):
    seg = seg_ref[0].astype(F32)
    cls_seg = jnp.sum(jnp.where(pick, seg, 0.0), axis=1, keepdims=True)
    bias = jnp.where(cls_seg == seg, 0.0, NEG_FILL)
    scores = scores + jnp.concatenate([bias] * HEADS, axis=0)
    expo = jnp.exp(scores - jnp.max(scores, axis=1, keepdims=True))
    return expo / jnp.sum(expo, axis=1, keepdims=True)


def cls_forward_kernel(
    rows, with_teacher, x_ref, seg_ref, query_cls_ref, pass_cls_ref, wq_ref, bq_ref, wk_ref, wv_ref, bv_ref,
    teacher_ref, pair_ref, rows_ref, query_ref, pick_ref, told_ref, key_ref,
):
    n_pass = rows.n_pass
    side = lax.axis_index("side")
    n_query, width = query_ref.shape
    slot = iota((n_query, 1), 0)
    cls = jnp.full((n_query, 1), -1, jnp.int32)
    for i in range(n_query):
        first = query_cls_ref.ref()[0, i]
        place = jnp.where(side == 0, first, pass_cls_ref.ref()[0, 0, i] if i < n_pass else -1)
        cls = jnp.where(slot == i, place, cls)
    pick = iota((n_query, x_ref.shape[0]), 1) == cls
    pick_low = jnp.where(pick, 1.0, 0.0).astype(BF)
    pick_ref[...] = pick_low
    pick_ref.flush()
    if with_teacher:
        teacher_rows(rows, teacher_ref, pair_ref, told_ref)
    key_ref[...] = dot(x_ref[...], wk_ref[...]).astype(BF)
    key_ref.flush()
    tokens = dot(pick_low, x_ref[...]).astype(BF)
    query = (dot(tokens, wq_ref[...]) + bq_ref[...]).astype(BF)
    query_ref[...] = query
    query_ref.flush()
    rows_ref[:, width:] = tokens
    probs = softmax_of(dot_t(spread_heads(query) * BF(HD**-0.5), key_ref[...]), pick, seg_ref)
    mixed = dot(probs.astype(BF), x_ref[...])
    high = mixed.astype(BF)
    rest = (mixed - high.astype(F32)).astype(BF)
    context = fold_heads(dot(high, wv_ref[...]) + dot(rest, wv_ref[...])) + bv_ref[...]
    rows_ref[:, :width] = context.astype(BF)


def middle_kernel(
    rows, pass_count,
    mine_ref, theirs_ref, wo_ref, vector_ref, wi_ref, wu_ref, code_ref, landed_ref, value_ref, probs_ref, x_ref, key_ref, query_ref, cluster_ref,
    keep_ref, give_ref, low_ref, context_ref, gown_ref, scores_ref,
    loss_ref, small_ref, inner_bias_ref,
    both_ref, first_ref, active_ref, pre_ref, second_ref, attended_ref, slope_ref,
):
    width = wo_ref.shape[0]
    bo_ref, g1_ref, s1_ref, bu_ref, g2_ref, s2_ref, bi_ref = vectors_of(vector_ref, width)
    n_queries, n_columns = rows.queries, rows.columns
    chunk = wi_ref.shape[1] // PARTS
    side, batch = lax.axis_index("side"), lax.axis_index("batch")
    core = side % 2
    order = one_hot(rows.count, rows.count, landed_ref[...])
    placed = dot(order, join_halves(core, mine_ref[...], theirs_ref[...]))
    both_ref[...] = placed[:, : 2 * width].astype(BF)
    told = placed[: rows.queries, 2 * width :]
    attended = both_ref[:, width:].astype(F32) + (dot(both_ref[:, :width], wo_ref[...]) + bo_ref[...])
    first_hat, first_inv = norm_stats(attended)
    for ref in (value_ref, probs_ref, x_ref, key_ref, query_ref):
        ref.start()
    first = first_hat * g1_ref[...] + s1_ref[...]
    first_low = first.astype(BF)
    first_ref[...] = first_low
    second = first + bu_ref[...]
    for i in range(PARTS):
        c = i * chunk
        pre = dot(first_low, wi_ref[:, c : c + chunk]) + bi_ref[:, c : c + chunk]
        active, slope = gelu_parts(pre)
        active = active.astype(BF)
        active_ref[:, c : c + chunk] = active
        slope_ref[:, c : c + chunk] = slope
        second += dot(active, wu_ref[c : c + chunk, :])
    both_ref.flush()
    first_ref.flush()
    active_ref.flush()
    second_hat, second_inv = norm_stats(second)
    final = (second_hat * g2_ref[...] + s2_ref[...]).astype(BF)

    scale = width ** (-0.5)
    query_vec, pass_vec = final[:n_queries], final[n_queries:]
    score = dot_t(query_vec, pass_vec) * scale
    column = iota((n_queries, n_columns), 1)
    is_pair = column == told[:, n_columns - 1 :].astype(jnp.int32)
    none = jnp.full((1, n_columns - pass_count), -1.0, F32)
    cluster = jnp.concatenate([cluster_ref[...].astype(F32), none], axis=1)
    query_cluster = jnp.sum(jnp.where(is_pair, cluster, 0.0), axis=1, keepdims=True)
    counted = (cluster == query_cluster) & jnp.logical_not(is_pair) & (column < pass_count)
    pair_score = jnp.sum(jnp.where(is_pair, score, 0.0), axis=1, keepdims=True)
    resid = jnp.where(counted, pair_score - score - told, 0.0)
    squares = jnp.sum(jnp.sum(resid * resid, axis=1, keepdims=True), axis=0, keepdims=True)
    pairs = jnp.where(counted, 1.0, 0.0)
    pairs = jnp.sum(jnp.sum(pairs, axis=1, keepdims=True), axis=0, keepdims=True)
    loss_ref[...] = squares / jnp.maximum(pairs, 1.0)
    loss_ref.flush()
    grad_score = jnp.where(is_pair, jnp.sum(resid, axis=1, keepdims=True), 0.0) - resid
    grad_low = (grad_score * scale).astype(BF)
    grad_final = jnp.concatenate([dot(grad_low, pass_vec), t_dot(grad_low, query_vec)], axis=0)

    def note(at, value):
        small_ref[at : at + 1, :] = jnp.sum(value, axis=0, keepdims=True)

    grad_second = norm_back(grad_final, second_hat, second_inv, g2_ref[...])
    second_low = grad_second.astype(BF)
    second_ref[...] = second_low
    grad_first = grad_second
    for i in range(PARTS):
        c = i * chunk
        grad_pre = dot_t(second_low, wu_ref[c : c + chunk, :]) * slope_ref[:, c : c + chunk]
        inner_bias_ref[:, c : c + chunk] = jnp.sum(grad_pre, axis=0, keepdims=True)
        pre_low = grad_pre.astype(BF)
        pre_ref[:, c : c + chunk] = pre_low
        grad_first += dot_t(pre_low, wi_ref[:, c : c + chunk])
    inner_bias_ref.flush()
    pre_ref.flush()
    second_ref.flush()
    grad_attended = norm_back(grad_first, first_hat, first_inv, g1_ref[...])
    attended_low = grad_attended.astype(BF)
    attended_ref[...] = attended_low
    attended_ref.flush()
    grad_context = dot_t(attended_low, wo_ref[...]).astype(BF)
    note(0, grad_final * second_hat)
    note(1, grad_final)
    note(2, grad_second)
    note(3, grad_first * first_hat)
    note(4, grad_first)
    note(5, grad_attended)
    note(6, grad_context.astype(F32))
    small_ref[7:8, :] = jnp.zeros((1, width), F32)
    small_ref.flush()


    slot = iota((rows.n_query, 1), 0)
    base = batch * rows.block + jnp.where(side == 0, 0, rows.n_query + rows.n_pass * (side - 1))
    live = slot < jnp.where(side == 0, rows.n_query, rows.n_pass)
    own = (code_ref[...] == base + slot) & live
    high = grad_attended.astype(BF)
    rest = (grad_attended - high.astype(F32)).astype(BF)
    own = jnp.where(own, 1.0, 0.0).astype(BF)
    gown_ref[...] = dot(own, high) + dot(own, rest)
    gown_ref.flush()
    context = dot(own, grad_context).astype(BF)
    context_ref[...] = context
    context_ref.flush()
    wide = spread_heads(context)
    probs = probs_ref[...]
    grad_probs = dot_t(wide, value_ref[...])
    row_dot = jnp.sum(probs * grad_probs, axis=1, keepdims=True)
    grad_scores = (probs * (grad_probs - row_dot)).astype(BF)
    scores_ref[...] = grad_scores
    scores_ref.flush()
    query_wide = spread_heads(query_ref[...]) * BF(HD**-0.5)
    x = x_ref.ref()
    key_side = dot(grad_scores, x[...]).astype(BF)
    value_side = dot(probs.astype(BF), x[...]).astype(BF)
    key_part = t_dot(key_side, query_wide)
    value_part = t_dot(value_side, wide)
    keep_ref[...] = jnp.where(core == 0, key_part, value_part)
    give_ref[...] = jnp.where(core == 0, value_part, key_part).astype(BF)
    low_ref[...] = (fold_heads(dot(grad_scores, key_ref[...])) * HD**-0.5).astype(BF)


def grads_kernel(*refs):
    weights, inputs, outs = refs[:7], refs[7:17], refs[17:]
    for ref in inputs + weights:
        if isinstance(ref, Fetched):
            ref.start()
    part_rows(outs[0], weights[0], weights[1][...])
    input_grad_kernel(*inputs, outs[4])
    outs[4].flush()
    weight_grads_kernel(*weights[2:], *outs[1:4])


def input_grad_kernel(
    pick_ref, scores_ref, probs_ref, context_ref, query_ref, low_ref, gown_ref,
    wq_ref, wk_ref, wv_ref, out_ref,
):
    query_wide = spread_heads(query_ref[...]) * BF(HD**-0.5)
    key_low = t_dot(scores_ref[...], query_wide).astype(BF)
    value_low = t_dot(probs_ref[...].astype(BF), spread_heads(context_ref[...])).astype(BF)
    sparse = gown_ref[...] + dot_t(low_ref[...], wq_ref[...])
    high = sparse.astype(BF)
    rest = (sparse - high.astype(F32)).astype(BF)
    pick = pick_ref[...]
    total = dot_t(key_low, wk_ref[...]) + dot_t(value_low, wv_ref[...])
    total += t_dot(jnp.concatenate([pick, pick], axis=0), jnp.concatenate([high, rest], axis=0))
    out_ref[...] = total.astype(BF)


def chip_sum_kernel(keep_ref, got_ref, out_ref):
    out_ref[...] = (keep_ref[...] + got_ref[...].astype(F32)).astype(BF)


def add_parts_kernel(rows, parts_ref, own_ref, other_ref, far_ref, far_other_ref, out_ref):
    core, chip = core_chip()
    peers, size = parts_ref.shape[:2]
    total = parts_ref[0].astype(F32)
    for i in range(1, peers):
        total += parts_ref[i].astype(F32)
    at = iota((rows.slot, 1), 0)
    source = block_source(rows, core * rows.half + chip * rows.quarter + at)
    source = jnp.where(at < rows.quarter, source, -1)
    low = take_rows(source, (own_ref, other_ref, far_ref, far_other_ref))
    total = jnp.concatenate([total.astype(BF), low], axis=0)
    for i in range(peers):
        out_ref[i] = total


def last_kernel(size, mine_ref, theirs_ref, x_ref, key_ref, value_ref, query_ref, bias_ref):
    core, _ = core_chip()
    peers = mine_ref.shape[0]
    step = peers // PARTS
    for i in range(PARTS):
        for j in range(i * step, i * step + step):
            mine, theirs = mine_ref[j, :size].astype(F32), theirs_ref[j, :size].astype(F32)
            key_ref[j * size : j * size + size, :] = jnp.where(core == 0, mine, theirs)
            value_ref[j * size : j * size + size, :] = jnp.where(core == 0, theirs, mine)
        key_ref.flush(i * step * size, step * size)
        value_ref.flush(i * step * size, step * size)
    mine = jnp.concatenate([mine_ref[j, size:] for j in range(peers)], axis=0)
    theirs = jnp.concatenate([theirs_ref[j, size:] for j in range(peers)], axis=0)
    low = join_halves(core, mine, theirs)
    bias_ref[...] = jnp.sum(low.astype(F32), axis=0, keepdims=True)
    part_rows(query_ref, x_ref, low)


def core_groups(batch_n):
    order = exchange_order(batch_n)
    return [[(y * 2 + c) * batch_n + b for y in range(2) for b in order] for c in range(2)]


def exchange(sent, batch_n):
    return lax.all_to_all(
        sent, ("side", "batch"), split_axis=0, concat_axis=0, axis_index_groups=core_groups(batch_n)
    )


def scatter_sum(keep, give, batch_n):
    got = lax.ppermute(give, "side", CORE_SWAP)
    total, token = call(chip_sum_kernel, [(keep.shape, BF, True)], (keep, got), name="chip_sum")
    return exchange(total.reshape(2 * batch_n, keep.shape[0] // (2 * batch_n), keep.shape[1]), batch_n), token


def part_rows(result, left, right):
    size = result.shape[0] // PARTS
    for i in range(PARTS):
        result[i * size : i * size + size, :] = t_dot(left[:, i * size : i * size + size], right)
        result.flush(i * size, size)


def weight_grads_kernel(
    first_ref, pre_ref, both_ref, attended_ref, slots_ref, inner_ref, out_ref, x_ref
):
    part_rows(inner_ref, first_ref, pre_ref[...])
    part_rows(out_ref, both_ref, attended_ref[...])
    width = out_ref.shape[0]
    count = both_ref.shape[0]
    pick = one_hot(count, slots_ref.shape[1], slots_ref[...])
    x_ref[...] = t_dot(pick, both_ref[:, width:]).astype(BF)


class Row:
    def __init__(self, source, at, width):
        self.source, self.at, self.width = source, at, width

    def __getitem__(self, index):
        first, last = 0, self.width
        if index is not Ellipsis:
            first, last = index[1].start, index[1].stop
        return self.source[self.at : self.at + 1, first:last]


def vectors_of(source, width):
    return [Row(source, i, width) for i in range(6)] + [Row(source, 6, source.shape[1])]


def column_of(row):
    return jnp.transpose(jnp.broadcast_to(row, (128, row.shape[1])))[:, :1]


def attention_kernel(
    tile, tiles, sizes, x_ref, wq_ref, bq_ref, key_ref, value_ref, seg_ref, out_ref, q_scr, bias_scr
):
    count = x_ref.shape[0]
    x, wq, bq, seg = ref_of(x_ref), ref_of(wq_ref), bq_ref[...], seg_ref[0]
    places = iota((1, count), 1)
    keys, values, seg_whole = ref_of(key_ref), ref_of(value_ref), ref_of(seg_ref)

    @pl.loop(*tiles)
    def _(i):
        row = pl.multiple_of(i * tile, tile)
        q = (dot(x[pl.ds(row, tile), :], wq[...]) + bq).astype(BF)
        q_scr[...] = q * BF(HD**-0.5)
        first = jnp.max(jnp.where(places == row, seg, -2))
        last = jnp.max(jnp.where(places == row + (tile - 1), seg, -2))
        low = jnp.min(jnp.where(seg == first, places, count)) // 128 * 128
        high = jnp.max(jnp.where(seg == last, places, -1)) + 1
        own = seg_whole[0, :, pl.ds(row, tile)].astype(F32)
        own = column_of(own)
        before = jnp.int32(0)
        for size in sizes:
            start = jnp.minimum(low, count - size)
            fits = (high - start <= size) if size < count else jnp.bool_(True)

            @pl.when(jnp.logical_and(before == 0, fits))
            def _(size=size, start=start):
                at = pl.multiple_of(start, 128)
                near = seg_whole[0, :, pl.ds(at, size)].astype(F32)
                bias_scr[:, :size] = jnp.where(own == near, 0.0, NEG_FILL)
                half = iota((1, 2 * HD), 1) // HD
                here = pl.ds(row - tiles[0] * tile, tile)

                def heads(first):
                    slabs = [pl.ds(first + k * 2 * HD, 2 * HD) for k in range(together)]
                    both = [(slab, h) for slab in slabs for h in range(2)]
                    scores = [
                        dot_t(jnp.where(half == h, q_scr[:, slab], BF(0)), keys[pl.ds(at, size), slab])
                        + bias_scr[:, :size]
                        for slab, h in both
                    ]
                    expos = [jnp.exp(s - jnp.max(s, axis=1, keepdims=True)).astype(BF) for s in scores]
                    outs = []
                    for (slab, h), expo in zip(both, expos):
                        mixed = dot(expo, jnp.where(half == h, values[pl.ds(at, size), slab], BF(1)))
                        outs.append(mixed / pltpu.roll(mixed, HD, 1))
                    for k, slab in enumerate(slabs):
                        out = jnp.where(half == 0, outs[2 * k], outs[2 * k + 1])
                        ref_of(out_ref)[here, slab] = out.astype(BF)

                together = SLABS_AT_ONCE.get(size, 1 if size > 512 else HEADS // 2)
                if together == HEADS // 2:
                    heads(0)
                else:

                    @pl.loop(0, HEADS // 2 // together)
                    def _(j):
                        heads(pl.multiple_of(j * (together * 2 * HD), together * 2 * HD))

            before = jnp.where(fits, 1, before)


def window_sizes(count):
    return [size for size in (384, 512, 768) if size < count] + [count]


def first_attention_kernel(
    tile, tiles, x_ref, key_ref, wv_ref, bv_ref, wq_ref, bq_ref, seg_ref, pick_ref, query_ref, *refs
):
    out_ref, value_ref, probs_ref, vector_ref, q_scr, bias_scr = refs[-6:]
    value_ref[...] = (dot(x_ref[...], wv_ref[...]) + bv_ref[...]).astype(BF)
    value_ref.flush()
    scores = dot_t(spread_heads(query_ref[...]) * BF(HD**-0.5), key_ref[...])
    probs_ref[...] = softmax_of(scores, pick_ref[...].astype(F32) > 0.5, seg_ref)
    probs_ref.flush()
    for i, ref in enumerate(refs[:-6]):
        vector_ref[i : i + 1, : ref.shape[1]] = ref[...]
    vector_ref.flush()
    sizes = window_sizes(x_ref.shape[0])
    attention_kernel(
        tile, tiles, sizes, x_ref, wq_ref, bq_ref, key_ref, value_ref, seg_ref, out_ref, q_scr, bias_scr
    )


def first_attention(x, keys, wv, bv, wq, bq, seg, pick, query, vectors, after, share, tile=256):
    t, d = x.shape
    return call(
        functools.partial(first_attention_kernel, tile, (0, share // tile)),
        [
            ((share, d), BF, False),
            ((t, d), BF, False),
            ((HEADS * query.shape[0], t), F32, False),
            ((8, vectors[-1].shape[1]), F32, False),
        ],
        (x, keys, wv, bv, wq, bq, seg, pick, query) + vectors,
        flops=6 * 10**9,
        far=range(9 + len(vectors)),
        scratch=[pltpu.VMEM((tile, d), BF), pltpu.VMEM((tile, t), F32)],
        limit=24,
        after=after,
        name="first_attention",
    )


def ffn_kernel(
    tile, x_ref, first_ref, rest_ref, wo_ref, vector_ref, wi_ref, wu_ref, out_ref,
):
    bo_ref, g1_ref, s1_ref, bu_ref, g2_ref, s2_ref, bi_ref = vectors_of(vector_ref, x_ref.shape[1])
    chunk = wi_ref.size
    for t in range(0, x_ref.shape[0], tile):
        part = slice(t, t + tile)
        share = first_ref.shape[0]
        near = first_ref[part, :] if t < share else rest_ref[t - share : t - share + tile, :]
        attended = x_ref[part, :].astype(F32) + (dot(near, wo_ref[...]) + bo_ref[...])
        first = norm_stats(attended)[0] * g1_ref[...] + s1_ref[...]
        first_low = first.astype(BF)
        second = first + bu_ref[...]
        for c in range(PARTS):
            pre = dot(first_low, wi_ref.part(c)) + bi_ref[:, c * chunk : c * chunk + chunk]
            second += dot(gelu(pre).astype(BF), wu_ref.part(c))
        out_ref[part, :] = (norm_stats(second)[0] * g2_ref[...] + s2_ref[...]).astype(BF)
        out_ref.flush(t, tile)


def dense_kernel(
    tile, tiles, x_ref, wq_ref, bq_ref, key_ref, value_ref, seg_ref, first_ref, wo_ref, vector_ref, wi_ref,
    wu_ref, out_ref, rest_ref, q_scr, bias_scr,
):
    for ref in (x_ref, wq_ref, bq_ref, key_ref, value_ref, seg_ref):
        ref.ref()
    for ref in (first_ref, wo_ref, vector_ref, wi_ref, wu_ref):
        ref.start()
    count = x_ref.shape[0]
    attention_kernel(
        tile, tiles, window_sizes(count), x_ref, wq_ref, bq_ref, key_ref, value_ref, seg_ref, rest_ref,
        q_scr, bias_scr,
    )
    ffn_kernel(512, x_ref, first_ref, rest_ref, wo_ref, vector_ref, wi_ref, wu_ref, out_ref)


def dense_rest(x, wq, bq, keys, values, seg, context, weights, after, tile=256):
    t, d = x.shape
    share = context.shape[0]
    return call(
        functools.partial(dense_kernel, tile, (share // tile, t // tile)),
        [(x.shape, BF, False)],
        (x, wq, bq, keys, values, seg, context) + weights,
        flops=8 * 10**9,
        far=(0, 1, 2, 5, 3, 4, 6, 7, 8, 9, 10),
        late=range(6, 11),
        split={9: (1, PARTS), 10: (0, PARTS)},
        scratch=[pltpu.VMEM((t - share, d), BF), pltpu.VMEM((tile, d), BF), pltpu.VMEM((tile, t), F32)],
        limit=40,
        after=after,
        name="dense_rest",
    )


def middle_large(
    rows, pass_count, core, mine, theirs, told, cluster, wo, bo, g1, s1, wi, bi, wu, bu, g2, s2
):
    width = wo.shape[0]
    both = join_halves(core, mine, theirs)[np.argsort(rows.landed(np.arange(rows.batch_n)))]
    attended = both[:, width:].astype(F32) + (dot(both[:, :width], wo) + bo)
    first_hat, first_inv = norm_stats(attended)
    first = first_hat * g1 + s1
    first_low = first.astype(BF)
    active, slope = gelu_parts(dot(first_low, wi) + bi)
    active_low = active.astype(BF)
    second = first + (dot(active_low, wu) + bu)
    second_hat, second_inv = norm_stats(second)
    final = (second_hat * g2 + s2).astype(BF)
    query_vec, pass_vec = final[: rows.queries], final[rows.queries : rows.queries + pass_count]
    scale = width ** (-0.5)
    score = dot_t(query_vec, pass_vec) * scale
    is_pair = iota(score.shape, 1) == told[:, pass_count:].astype(jnp.int32)
    query_cluster = jnp.sum(jnp.where(is_pair, cluster, 0.0), axis=1, keepdims=True)
    counted = (cluster == query_cluster) & jnp.logical_not(is_pair)
    pair_score = jnp.sum(jnp.where(is_pair, score, 0.0), axis=1, keepdims=True)
    resid = jnp.where(counted, pair_score - score - told[:, :pass_count], 0.0)
    loss = jnp.sum(resid * resid) / jnp.maximum(jnp.sum(counted.astype(F32)), 1.0)
    grad_score = jnp.where(is_pair, jnp.sum(resid, axis=1, keepdims=True), 0.0) - resid
    grad_low = (grad_score * scale).astype(BF)
    none = jnp.zeros((rows.count - rows.queries - pass_count, width), F32)
    grad_final = jnp.concatenate([dot(grad_low, pass_vec), t_dot(grad_low, query_vec), none], axis=0)
    grad_second = norm_back(grad_final, second_hat, second_inv, g2)
    second_low = grad_second.astype(BF)
    grad_pre = dot_t(second_low, wu) * slope
    pre_low = grad_pre.astype(BF)
    grad_first = dot_t(pre_low, wi) + grad_second
    grad_attended = norm_back(grad_first, first_hat, first_inv, g1)
    attended_low = grad_attended.astype(BF)
    grad_context = dot_t(attended_low, wo).astype(BF)
    small = jnp.stack(
        [
            jnp.sum(v, axis=0)
            for v in (
                grad_final * second_hat, grad_final, grad_second, grad_first * first_hat,
                grad_first, grad_attended, grad_context.astype(F32),
            )
        ]
    )
    inner_bias = jnp.sum(grad_pre, axis=0, keepdims=True)
    return (
        loss.reshape(1, 1), grad_attended, grad_context, small, inner_bias,
        both, first_low, active_low, pre_low, second_low, attended_low,
    )


def own_large(rows, side, batch, grad_attended, grad_context, tokens, keys, values, cls_query, probs):
    core = side % 2
    slot = jnp.arange(rows.n_query)[:, None]
    base = batch * rows.block + jnp.where(side == 0, 0, rows.n_query + rows.n_pass * (side - 1))
    live = slot < jnp.where(side == 0, rows.n_query, rows.n_pass)
    own = ((rows.code[None, :] == base + slot) & live).astype(F32)
    own_attended = dot(own, grad_attended, lax.Precision.HIGHEST)
    context = dot(own.astype(BF), grad_context).astype(BF)
    wide = spread_heads(context)
    grad_probs = dot_t(wide, values)
    row_dot = jnp.sum(probs * grad_probs, axis=1, keepdims=True)
    grad_scores = (probs * (grad_probs - row_dot)).astype(BF)
    query_wide = spread_heads(cls_query) * BF(HD**-0.5)
    key_part = t_dot(dot(grad_scores, tokens).astype(BF), query_wide)
    value_part = t_dot(dot(probs.astype(BF), tokens).astype(BF), wide)
    keep = jnp.where(core == 0, key_part, value_part)
    give = jnp.where(core == 0, value_part, key_part).astype(BF)
    low = (fold_heads(dot(grad_scores, keys)) * HD**-0.5).astype(BF)
    return keep, give, low, context, own_attended, grad_scores


def fetch(arrays, behind_this):
    hbm = pl.BlockSpec(memory_space=pltpu.HBM)
    count = len(arrays)

    def kernel(*refs):
        semaphores = refs[-1]
        copies = [
            pltpu.make_async_copy(refs[i], refs[count + 1 + i], semaphores.at[i]) for i in range(count)
        ]
        for copy in copies:
            copy.start()
        for copy in copies:
            copy.wait()

    return pl.pallas_call(
        kernel,
        out_shape=[pltpu.VMEM(x.shape, x.dtype) for x in arrays],
        in_specs=[hbm] * count + [VM],
        out_specs=[VM] * count,
        scratch_shapes=[pltpu.SemaphoreType.DMA((count,))],
        compiler_params=pltpu.CompilerParams(vmem_limit_bytes=4 * MIB),
        name="fetch",
    )(*[pltpu.with_memory_space_constraint(x, pltpu.HBM) for x in arrays], behind_this)


def middle(rows, pass_count, mine, theirs, kept, weights, cluster, hidden, after):
    width, ff = weights[2].shape
    count = rows.count
    keys, values, cls_query, probs = kept
    landed = rows.landed(exchange_order(rows.batch_n))
    ins = (mine, theirs) + weights
    ins += (rows.code[None, :], landed[None, :], values, probs, hidden, keys, cls_query, cluster[None, :])
    outs = [
        ((width, width), F32, True), ((width, width), BF, True), ((rows.n_query, width), BF, True),
        ((rows.n_query, width), BF, False), ((rows.n_query, width), F32, False), (probs.shape, BF, False),
        ((1, 1), F32, False), ((8, width), F32, False), ((1, ff), F32, False),
        ((count, 2 * width), BF, False), ((count, width), BF, False), ((count, ff), BF, False),
        ((count, ff), BF, False), ((count, width), BF, False), ((count, width), BF, False),
    ]
    return call(
        functools.partial(middle_kernel, rows, pass_count),
        outs,
        ins,
        flops=12 * count * width * ff,
        scratch=[pltpu.VMEM((count, ff), F32)],
        far=(7, 6) + tuple(range(8, len(ins))),
        late=range(8, len(ins) - 1),
        limit=32,
        after=after,
        name="cls_middle",
    )


def body(
    hidden_in,
    segments,
    query_cls,
    passage_cls,
    pair_passage,
    passage_cluster,
    teacher,
    query_weight,
    query_bias,
    key_weight,
    value_weight,
    value_bias,
    out_weight,
    out_bias,
    first_gain,
    first_shift,
    inner_weight,
    inner_bias,
    outer_weight,
    outer_bias,
    second_gain,
    second_shift,
):
    count_tok = hidden_in.shape[2]
    width = hidden_in.shape[3]
    n_query = query_cls.shape[1]
    n_pass = passage_cls.shape[2]
    batch_n = lax.axis_size("batch")
    side = lax.axis_index("side")
    pass_count = teacher.shape[1]
    rows = Rows(batch_n, n_query, n_pass, pass_count)

    hidden = hidden_in.reshape(count_tok, width)

    def vec(v):
        return v.reshape(1, -1)

    weights = (
        out_weight, vec(out_bias), vec(first_gain), vec(first_shift), inner_weight, vec(inner_bias),
        outer_weight, vec(outer_bias), vec(second_gain), vec(second_shift),
    )
    small_case = rows.count <= 512 and rows.columns == 128 and count_tok % 512 == 0

    own, cls_query, pick, told, keys, _ = call(
        functools.partial(cls_forward_kernel, rows, small_case),
        [
            ((n_query, 2 * width), BF, True),
            ((n_query, width), BF, False),
            ((n_query, count_tok), BF, False),
            ((rows.half, rows.columns), BF, True),
            ((count_tok, width), BF, False),
        ],
        (
            hidden, segments, query_cls, passage_cls, query_weight, vec(query_bias), key_weight,
            value_weight, vec(value_bias), teacher, pair_passage,
        ),
        flops=2 * count_tok * width * width,
        far=(6, 0, 4, 1, 5, 9, 7, 8),
        smem=(2, 3, 10),
        limit=24,
        name="cls_forward",
    )

    near = near_rows(own)
    if small_case:
        sent, half_done = call(
            functools.partial(half_kernel, rows),
            [((batch_n, rows.half, 2 * width + rows.columns), BF, True)],
            near + (told,),
            name="half_rows",
        )
    else:
        half, half_done = call(
            functools.partial(half_kernel, rows),
            [((rows.half, 2 * width), BF, True)],
            near,
            name="half_rows",
        )
        sent = jnp.broadcast_to(half[None], (batch_n,) + half.shape)
    batches = exchange_order(batch_n)
    mine = lax.all_to_all(
        sent, "batch", split_axis=0, concat_axis=0, axis_index_groups=[batches] if small_case else None
    )
    vectors = (weights[1], weights[2], weights[3], weights[7], weights[8], weights[9], weights[5])
    share = count_tok // 2
    first_context, values, probs, vectors, attention_done = first_attention(
        hidden, keys, value_weight, vec(value_bias), query_weight, vec(query_bias), segments, pick,
        cls_query, vectors, (half_done,), share,
    )
    matrices = (out_weight, vectors, inner_weight, outer_weight)
    if small_case:
        mine = behind(mine, attention_done)
    theirs = lax.ppermute(mine, "side", CORE_SWAP)

    if small_case:
        kept = (keys, values, cls_query, probs)
        flat = (batch_n * rows.half, mine.shape[2])
        (
            keep, give, query_low, own_context, own_attended, grad_scores, loss, small, grad_inner_bias,
            both, first_low, active_low, pre_low, second_low, attended_low, _,
        ) = middle(
            rows, pass_count, mine.reshape(flat), theirs.reshape(flat), kept, tuple(fetch(matrices, mine)),
            passage_cluster, hidden, (),
        )
    else:
        told = jnp.concatenate([teacher, pair_passage[:, None].astype(F32)], axis=1)
        told = lax.all_to_all(
            jnp.broadcast_to(told[None], (batch_n,) + told.shape), "batch", split_axis=0, concat_axis=0
        ).reshape(batch_n * n_query, pass_count + 1)
        flat = (batch_n * rows.half, 2 * width)
        (
            loss, grad_attended, grad_context, small, grad_inner_bias,
            both, first_low, active_low, pre_low, second_low, attended_low,
        ) = middle_large(
            rows, pass_count, side % 2, mine.reshape(flat), theirs.reshape(flat), told,
            passage_cluster.astype(F32)[None, :], *weights,
        )
        keep, give, query_low, own_context, own_attended, grad_scores = own_large(
            rows, side, lax.axis_index("batch"), grad_attended, grad_context,
            hidden, keys, values, cls_query, probs,
        )

    parts, sum_done = scatter_sum(keep, give, batch_n)
    peers, size = parts.shape[:2]
    for_input = (
        pick, grad_scores, probs, own_context, cls_query, query_low, own_attended, query_weight, key_weight,
        value_weight,
    )
    if small_case and size % 16 == 0:
        saved = (active_low, second_low, first_low, pre_low, both, attended_low, rows.slots()[None, :])
        grad_outer_weight, grad_inner_weight, grad_out_weight, all_tokens, input_grad, weight_done = call(
            grads_kernel,
            [
                (outer_weight.shape, F32, False),
                (inner_weight.shape, F32, False),
                (out_weight.shape, F32, False),
                ((4 * rows.batch_n * rows.slot, width), BF, False),
                (hidden.shape, BF, False),
            ],
            saved + for_input,
            flops=2 * rows.count * width * (4 * width + width) + 6 * count_tok * width * width,
            far=tuple(i for i in range(17) if i != 12),
            late=range(2, 17),
            limit=40,
            after=(sum_done,),
            name="grads",
        )
        low = near_rows(query_low, weight_done)
        sent, add_done = call(
            functools.partial(add_parts_kernel, rows),
            [((peers, size + rows.slot, width), BF, True)],
            (parts,) + low,
            after=(weight_done,),
            name="add_parts",
        )
        whole = exchange(sent, batch_n)
        rows_out, dense_done = dense_rest(
            hidden, query_weight, vec(query_bias), keys, values, segments, first_context, matrices,
            (add_done,),
        )
        whole = behind(whole, dense_done)
        other = lax.ppermute(whole, "side", CORE_SWAP)
        grad_key_weight, grad_value_weight, grad_query_weight, grad_query_bias, _ = call(
            functools.partial(last_kernel, size),
            [((width, width), F32, False)] * 3 + [((1, width), F32, False)],
            (whole, other, all_tokens),
            far=(2,),
            limit=12,
            name="last_grads",
        )
    else:
        input_grad, _ = call(
            input_grad_kernel,
            [(hidden.shape, BF, False)],
            for_input,
            far=(1, 4, 2, 3, 0, 6, 8, 9, 7),
            limit=20,
            after=(sum_done,),
            name="input_grad",
        )
        rows_out, _ = dense_rest(
            hidden, query_weight, vec(query_bias), keys, values, segments, first_context, matrices,
            (sum_done,),
        )
        part = jnp.sum(parts.astype(F32), axis=0).astype(BF)
        whole = exchange(jnp.broadcast_to(part[None], parts.shape), batch_n).reshape(width, width)
        grad_outer_weight = t_dot(active_low, second_low)
        grad_inner_weight = t_dot(first_low, pre_low)
        grad_out_weight = t_dot(both[:, :width], attended_low)
        half, _ = call(
            functools.partial(half_kernel, rows),
            [((rows.half, width), BF, True)],
            near_rows(query_low),
            name="low_rows",
        )
        flat = (batch_n * rows.half, width)
        half = jnp.broadcast_to(half[None], (batch_n,) + half.shape)
        low_mine = lax.all_to_all(half, "batch", split_axis=0, concat_axis=0).reshape(flat)
        low_theirs = lax.ppermute(low_mine, "side", CORE_SWAP)
        all_low = join_halves(side % 2, low_mine, low_theirs)[np.argsort(rows.landed(np.arange(rows.batch_n)))]
        grad_query_weight = t_dot(both[:, width:], all_low)
        grad_query_bias = jnp.sum(all_low.astype(F32), axis=0)
        other = lax.ppermute(whole, "side", CORE_SWAP)
        first_core = side % 2 == 0
        grad_key_weight = jnp.where(first_core, whole, other).astype(F32)
        grad_value_weight = jnp.where(first_core, other, whole).astype(F32)

    return (
        loss.reshape(()),
        rows_out.reshape(hidden_in.shape),
        input_grad.reshape(hidden_in.shape),
        grad_query_weight,
        grad_query_bias.reshape(-1),
        grad_key_weight,
        grad_value_weight,
        small[6],
        grad_out_weight,
        small[5],
        small[3],
        small[4],
        grad_inner_weight,
        grad_inner_bias.reshape(-1),
        grad_outer_weight,
        small[2],
        small[0],
        small[1],
    )


def solution(mesh):
    rows = P("side", "batch", None, None)
    in_specs = (
        rows,
        P("side", "batch", None),
        P("batch", None),
        P("side", "batch", None),
        P("batch"),
        P(),
        P("batch", None),
    ) + (P(),) * 15
    out_specs = (P(), rows, rows) + (P(),) * 15
    return jax.shard_map(body, mesh=mesh, in_specs=in_specs, out_specs=out_specs, check_vma=False)
```
